32 devices in a mesh: round: 4 (over z), stab: 8 (over y, x, core).
Axes of the slice: x: 2, y: 2, z: 4, core: 2. Of those that a mesh axis runs over, the one named last changes fastest.
Arguments:
- inputs: bfloat16 [32, 896, 512], P('round', 'stab'), may hold values from -6 to 6
- labels: int32 [32, 896], P('round', 'stab'), may hold values 0 or 1
- neighbours: int32 [224, 16], replicated, may hold values from 0 to 209, as said below
- space_in_weights: bfloat16 [512, 1536], replicated
- space_out_weights: bfloat16 [512, 512], replicated, may hold values from -0.25 to 0.25
- space_gain: float32 [512], replicated, may hold values from 0.5 to 1.5
- time_in_weights: bfloat16 [512, 1536], replicated
- time_out_weights: bfloat16 [512, 512], replicated, may hold values from -0.25 to 0.25
- time_gain: float32 [512], replicated, may hold values from 0.5 to 1.5
- readout: float32 [512], replicated, may hold values from -1 to 1
Outputs:
- grad_inputs: float32 [32, 896, 512], P('round', 'stab')
The draws below stay inside these ranges and needn't reach their ends.
Inputs may be any that keep to these rules, and one draw needn't show every extreme that they name: `neighbours`: row b lists 16 distinct blocks below 210; each such block b lists itself.
All inputs are finite; a program needn't handle non-finite values. No bound on the sum of `labels` on one device may be relied on, other than what follows from the above.
Results may differ from the reference program's by a relative error of at most 0.0085.
Values may be sent and summed in bfloat16 or wider, within the bound.
A program may use at most 320 MiB of HBM per device.

```python
import jax
import jax.numpy as jnp
from jax import lax

D = 512
HEADS = 8
HEAD_DIM = 64
STABS = 896
STABS_REAL = 840
BLOCK = 4
LINKS = 16
ROUNDS = 32


def draw_neighbours(key, part):
    real_blocks = STABS_REAL // BLOCK
    all_blocks = STABS // BLOCK
    scores = jax.random.randint(key, (all_blocks, real_blocks), 0, 1 << 20) * 256 + jnp.arange(real_blocks)[None, :]
    itself = jnp.arange(all_blocks)[:, None] == jnp.arange(real_blocks)[None, :]
    scores = scores + jnp.where(itself, 1 << 28, 0)
    return lax.top_k(scores, LINKS)[1].astype(jnp.int32)


def input_weights(key):
    base = jax.random.normal(key, (D, 3, D), jnp.float32) * D ** (-0.5)
    return base.reshape(D, 3 * D)


def draw_space_in_weights(key, part):
    return input_weights(jax.random.fold_in(key, 11)).astype(jnp.bfloat16)


def draw_time_in_weights(key, part):
    return input_weights(jax.random.fold_in(key, 12)).astype(jnp.bfloat16)


def place_ends(entries, key, least, largest):
    dims = entries.shape
    place = [jax.random.randint(jax.random.fold_in(key, axis), (), 0, dims[axis]) for axis in range(len(dims))]
    entries = entries.at[tuple(place)].set(least)
    longest = dims.index(max(dims))
    place[longest] = (place[longest] + 1) % dims[longest]
    return entries.at[tuple(place)].set(largest)


def steps_of(stream_key, shape, cuts, low, largest):
    def one(axis_at, blocks):
        draws = jax.random.uniform(jax.random.fold_in(jax.random.fold_in(stream_key, 6), axis_at), (blocks,), jnp.float32, low / len(cuts), largest / len(cuts))
        return jnp.repeat(jnp.exp(draws), shape[axis_at] // blocks).reshape((-1,) + (1,) * (len(shape) - axis_at - 1))

    level = one(*cuts[0])
    for cut in cuts[1:]:
        level = level * one(*cut)
    return level


def bell_draw(key, extent, scale, most, cuts=(), kind=jnp.bfloat16):
    result = jax.random.normal(key, extent, jnp.float32) * scale
    if len(cuts) > 0:
        result = steps_of(key, extent, cuts, -0.22, 0.18) * result
    return jnp.clip(result, min=-most, max=most).astype(kind)


def setup_inputs(seed: int = 0) -> dict:
    key_list = jax.random.split(jax.random.key(seed), 11)
    inputs = bell_draw(key_list[0], (ROUNDS, STABS, D), 1.0, 6.0, ((0, 4), (1, 8)))
    labels = place_ends((jax.random.randint(key_list[1], (ROUNDS, STABS), 0, 2) < 1).astype(jnp.int32), jax.random.fold_in(key_list[1], 1), 0, 1)
    neighbours = draw_neighbours(jax.random.fold_in(key_list[10], 71), 0)
    space_in_weights = draw_space_in_weights(jax.random.fold_in(key_list[10], 71), 0)
    space_out_weights = bell_draw(key_list[4], (D, D), D ** -0.5, 0.25)
    space_gain = jnp.clip(1.0 + 0.1 * jax.random.normal(key_list[5], (D,), jnp.float32), 0.5, 1.5)
    time_in_weights = draw_time_in_weights(jax.random.fold_in(key_list[10], 71), 0)
    time_out_weights = bell_draw(key_list[7], (D, D), D ** -0.5, 0.25)
    time_gain = jnp.clip(1.0 + 0.1 * jax.random.normal(key_list[8], (D,), jnp.float32), 0.5, 1.5)
    readout = bell_draw(key_list[9], (D,), 0.18, 1.0, (), jnp.float32)
    return dict(inputs=inputs, labels=labels, neighbours=neighbours, space_in_weights=space_in_weights, space_out_weights=space_out_weights, space_gain=space_gain, time_in_weights=time_in_weights, time_out_weights=time_out_weights, time_gain=time_gain, readout=readout)


EPSILON = 1e-06
MASKED_SCORE = -1e+30

def contract(form, first_operand, second_operand):
    return jnp.einsum(form, first_operand.astype(jnp.float32), second_operand.astype(jnp.float32))

def norm_rows(hidden, gain):
    inverse = lax.rsqrt(lax.optimization_barrier(jnp.mean(hidden * hidden, axis=-1, keepdims=True)) + EPSILON)
    return ((hidden * inverse * gain).astype(jnp.bfloat16), inverse)

def norm_back(hidden, inverse, gain, upstream):
    scaled = upstream * gain
    inner = lax.optimization_barrier(jnp.mean(hidden * scaled, axis=-1, keepdims=True))
    return inverse * scaled - hidden * inverse * inverse * inverse * inner

def block_keys(field, neighbours):
    head_depth = field.shape[0]
    blocked = field.reshape(head_depth, -1, BLOCK)
    return blocked[:, neighbours].reshape(head_depth, neighbours.shape[0], -1)

def spread_back(near_grad, neighbours):
    head_depth = near_grad.shape[0]
    block_count = neighbours.shape[0]
    pieces = near_grad.reshape(head_depth, block_count, neighbours.shape[1], BLOCK)
    summed = jnp.zeros((head_depth, block_count, BLOCK), near_grad.dtype).at[:, neighbours].add(pieces)
    return summed.reshape(head_depth, -1)

def space_scores(queries, key_rows, neighbours):
    head_depth = queries.shape[0]
    factor = head_depth ** (-0.5)
    query_blocks = queries.reshape(head_depth, -1, BLOCK)
    near_keys = block_keys(key_rows, neighbours)
    return (contract('dni,dnj->nij', query_blocks, near_keys) * factor, query_blocks, near_keys, factor)

def space_forward(queries, key_rows, values, neighbours):
    scores, query_blocks, near_keys, factor = space_scores(queries, key_rows, neighbours)
    highest = lax.optimization_barrier(jnp.max(scores, axis=-1, keepdims=True))
    logsum = highest + jnp.log(lax.optimization_barrier(jnp.sum(jnp.exp(scores - highest), axis=-1, keepdims=True)))
    weights = jnp.exp(scores - logsum).astype(jnp.bfloat16)
    attended = contract('nij,dnj->dni', weights, block_keys(values, neighbours)).astype(jnp.bfloat16)
    return (attended.reshape(queries.shape), logsum)

def space_backward(queries, key_rows, values, neighbours, attended, grad_rows, logsum):
    scores, query_blocks, near_keys, factor = space_scores(queries, key_rows, neighbours)
    near_values = block_keys(values, neighbours)
    probability = jnp.exp(scores - logsum)
    weights = probability.astype(jnp.bfloat16)
    grad_blocks = grad_rows.reshape(query_blocks.shape)
    spread = lax.optimization_barrier(jnp.sum(grad_rows.astype(jnp.float32) * attended.astype(jnp.float32), axis=0)).reshape(-1, BLOCK)[:, :, None]
    grad_near_values = contract('nij,dni->dnj', weights, grad_blocks)
    grad_weights = contract('dni,dnj->nij', grad_blocks, near_values)
    grad_scores = (probability * (grad_weights - spread) * factor).astype(jnp.bfloat16)
    grad_queries = contract('nij,dnj->dni', grad_scores, near_keys).reshape(queries.shape)
    grad_near_keys = contract('nij,dni->dnj', grad_scores, query_blocks)
    return (grad_queries, spread_back(grad_near_keys, neighbours), spread_back(grad_near_values, neighbours))

def causal_scores(queries, key_rows, query_offset, key_offset):
    query_len, pair_count, span = queries.shape
    key_len = key_rows.shape[0]
    query_heads = queries.reshape(query_len, pair_count, 2, span // 2)
    key_heads = key_rows.reshape(key_len, pair_count, 2, span // 2)
    factor = (span // 2) ** (-0.5)
    scores = contract('qphd,kphd->phqk', query_heads, key_heads) * factor
    allowed = (query_offset + jnp.arange(query_len))[:, None] >= (key_offset + jnp.arange(key_len))[None, :]
    return (jnp.where(allowed, scores, MASKED_SCORE), query_heads, key_heads, factor)

def time_forward(queries, key_rows, values, query_offset, key_offset):
    scores, query_heads, key_heads, factor = causal_scores(queries, key_rows, query_offset, key_offset)
    value_heads = values.reshape(key_heads.shape)
    highest = lax.optimization_barrier(jnp.max(scores, axis=-1, keepdims=True))
    logsum = highest + jnp.log(lax.optimization_barrier(jnp.sum(jnp.exp(scores - highest), axis=-1, keepdims=True)))
    weights = jnp.exp(scores - logsum).astype(jnp.bfloat16)
    attended = contract('phqk,kphd->qphd', weights, value_heads).astype(jnp.bfloat16)
    return (attended.reshape(queries.shape), jnp.transpose(logsum[..., 0], (2, 0, 1)))

def delta_rows(attended, grad_rows):
    product = attended.astype(jnp.float32) * grad_rows.astype(jnp.float32)
    return lax.optimization_barrier(jnp.sum(product.reshape(attended.shape[0], attended.shape[1], 2, -1), axis=-1))

def time_backward(queries, key_rows, values, grad_rows, logsum, spread, query_offset, key_offset):
    scores, query_heads, key_heads, factor = causal_scores(queries, key_rows, query_offset, key_offset)
    value_heads = values.reshape(key_heads.shape)
    grad_heads = grad_rows.reshape(query_heads.shape)
    probability = jnp.exp(scores - jnp.transpose(logsum, (1, 2, 0))[..., None])
    weights = probability.astype(jnp.bfloat16)
    grad_values = contract('phqk,qphd->kphd', weights, grad_heads)
    grad_weights = contract('qphd,kphd->phqk', grad_heads, value_heads)
    grad_scores = (probability * (grad_weights - jnp.transpose(spread, (1, 2, 0))[..., None]) * factor).astype(jnp.bfloat16)
    grad_queries = contract('phqk,kphd->qphd', grad_scores, key_heads)
    grad_keys = contract('phqk,qphd->kphd', grad_scores, query_heads)
    return (grad_queries.reshape(queries.shape), grad_keys.reshape(key_rows.shape), grad_values.reshape(key_rows.shape))

def readout_grad(after_time, readout, targets, real_mask):
    logits = lax.optimization_barrier(jnp.sum(after_time * readout, axis=-1))
    grad_logits = (jax.nn.sigmoid(logits) - targets.astype(jnp.float32)) * real_mask
    return grad_logits[..., None] * readout

def reference(inputs, labels, neighbours, space_in_weights, space_out_weights, space_gain, time_in_weights, time_out_weights, time_gain, readout):
    rounds, stab_count, features = inputs.shape
    space_four = space_in_weights.reshape(features, 3, HEADS, HEAD_DIM)
    space_three = space_out_weights.reshape(HEADS, HEAD_DIM, features)
    time_three = time_in_weights.reshape(features, 3, features)
    attend = jax.vmap(space_forward, in_axes=(0, 0, 0, None))
    revert = jax.vmap(space_backward, in_axes=(0, 0, 0, None, 0, 0, 0))

    def space_prepare(round_rows):
        widened = round_rows.astype(jnp.float32)
        normed, inverse = norm_rows(widened, space_gain)
        triple = contract('sd,dchk->chks', normed, space_four).astype(jnp.bfloat16)
        attended, logsum = attend(triple[0], triple[1], triple[2], neighbours)
        return (widened, inverse, triple, attended, logsum)

    def space_ahead(round_rows):
        widened, inverse, triple, attended, logsum = space_prepare(round_rows)
        return widened + contract('hks,hkd->sd', attended, space_three)
    after_space = lax.map(space_ahead, inputs)
    blocks = stab_count // BLOCK
    block_rows = jnp.transpose(after_space.reshape(rounds, blocks, BLOCK, features), (1, 0, 2, 3))
    block_labels = jnp.transpose(labels.reshape(rounds, blocks, BLOCK), (1, 0, 2))
    block_real = (jnp.arange(stab_count) < STABS_REAL).astype(jnp.float32).reshape(blocks, BLOCK)

    def time_block(packed):
        row_block, targets, real_mask = packed
        normed, inverse = norm_rows(row_block, time_gain)
        triple = contract('rsd,dce->crse', normed, time_three).astype(jnp.bfloat16)
        triple = triple.reshape(3, rounds, BLOCK * HEADS // 2, 2 * HEAD_DIM)
        attended, logsum = time_forward(triple[0], triple[1], triple[2], 0, 0)
        after_time = row_block + jnp.dot(attended.reshape(-1, features), time_out_weights, preferred_element_type=jnp.float32).reshape(row_block.shape)
        grad_after = readout_grad(after_time, readout, targets, real_mask)
        grad_attended = contract('td,ed->te', grad_after.astype(jnp.bfloat16).reshape(-1, features), time_out_weights).astype(jnp.bfloat16).reshape(attended.shape)
        spread = delta_rows(attended, grad_attended)
        grad_three = time_backward(triple[0], triple[1], triple[2], grad_attended, logsum, spread, 0, 0)
        stacked = jnp.stack(grad_three).astype(jnp.bfloat16).reshape(3, rounds, BLOCK, features)
        grad_normed = contract('crse,dce->rsd', stacked, time_three)
        return grad_after + norm_back(row_block, inverse, time_gain, grad_normed)
    grad_blocks = lax.map(time_block, (block_rows, block_labels, block_real))
    grad_space_rows = jnp.transpose(grad_blocks, (1, 0, 2, 3)).reshape(rounds, stab_count, features)

    def space_behind(packed):
        round_rows, upstream = packed
        widened, inverse, triple, attended, logsum = space_prepare(round_rows)
        grad_attended = contract('sd,hkd->hks', upstream.astype(jnp.bfloat16), space_three).astype(jnp.bfloat16)
        grad_three = revert(triple[0], triple[1], triple[2], neighbours, attended, grad_attended, logsum)
        stacked = jnp.stack(grad_three).astype(jnp.bfloat16)
        grad_normed = contract('chks,dchk->sd', stacked, space_four)
        return upstream + norm_back(widened, inverse, space_gain, grad_normed)
    return lax.map(space_behind, (inputs, grad_space_rows))
```

```python
import functools

import jax
import jax.numpy as jnp
from jax import lax
from jax.experimental import pallas as pl
from jax.experimental.pallas import tpu as pltpu
from jax.sharding import PartitionSpec as P

HEADS = 8
HEAD_DIM = 64
STABS_REAL = 840
BLOCK = 4
PAIR = 2 * HEAD_DIM
CHUNK = 448
BACK_CHUNK = 448
GROUP = 128

EPSILON = 1e-06
MASKED_SCORE = -1e30
FACTOR = HEAD_DIM ** (-0.5)
VMEM_LIMIT = 50 * 1024 * 1024


def dot(first, second):
    return jnp.dot(first, second, preferred_element_type=jnp.float32)


def dot_nt(first, second):
    return lax.dot_general(
        first, second, (((1,), (1,)), ((), ())), preferred_element_type=jnp.float32
    )


def dot_tn(first, second):
    return lax.dot_general(
        first, second, (((0,), (0,)), ((), ())), preferred_element_type=jnp.float32
    )


def inverse_rms(hidden):
    return lax.rsqrt(jnp.mean(hidden * hidden, axis=-1, keepdims=True) + EPSILON)


def norm_back(hidden, inverse, gain, upstream):
    scaled = upstream * gain
    inner = jnp.mean(hidden * scaled, axis=-1, keepdims=True)
    return inverse * scaled - hidden * (inverse * inverse * inverse * inner)


def softmax_rows(scores):
    highest = jnp.max(scores, axis=-1, keepdims=True)
    weights = jnp.exp(scores - highest)
    total = jnp.sum(weights, axis=-1, keepdims=True)
    return (weights * (1.0 / total)).astype(jnp.bfloat16)


def space_forward_kernel(
    x_ref, near_ref, gain_ref, wq_ref, wk_ref, wv_ref, wo_ref,
    h_ref, q_ref, k_ref, v_ref, o_ref, p_ref,
    n_scr, bias_scr, acc_scr,
):
    step = pl.program_id(0)
    stabs = x_ref.shape[0]
    blocks, links = near_ref.shape

    @pl.when(step == 0)
    def _():
        x = x_ref[...].astype(jnp.float32)
        n_scr[...] = (x * inverse_rms(x) * gain_ref[...]).astype(jnp.bfloat16)
        acc_scr[...] = x
        lanes = lax.broadcasted_iota(jnp.int32, (blocks, blocks), 1)
        near = near_ref[...]
        listed = jnp.zeros((blocks, blocks), jnp.float32)
        for link in range(links):
            listed = jnp.where(lanes == near[:, link : link + 1], 1.0, listed)
        owner = lax.broadcasted_iota(jnp.int32, (stabs, blocks), 0) // BLOCK
        column = lax.broadcasted_iota(jnp.int32, (stabs, blocks), 1)
        widen = jnp.where(owner == column, 1.0, 0.0).astype(jnp.bfloat16)
        rows = dot(widen, listed.astype(jnp.bfloat16)).astype(jnp.bfloat16)
        bias_scr[...] = jnp.where(dot_nt(rows, widen) > 0.5, 0.0, MASKED_SCORE)

    n = n_scr[...]
    q_ref[...] = dot(n, wq_ref[...]).astype(jnp.bfloat16)
    k_ref[...] = dot(n, wk_ref[...]).astype(jnp.bfloat16)
    v_ref[...] = dot(n, wv_ref[...]).astype(jnp.bfloat16)
    for head in range(2):
        cols = slice(head * HEAD_DIM, (head + 1) * HEAD_DIM)
        keys = k_ref[:, cols]
        values = v_ref[:, cols]
        for start in range(0, stabs, CHUNK):
            rows = slice(start, start + CHUNK)
            scores = dot_nt(q_ref[rows, cols] * FACTOR, keys) + bias_scr[rows, :]
            weights = softmax_rows(scores)
            p_ref[head, rows, :] = weights
            o_ref[rows, cols] = dot(weights, values).astype(jnp.bfloat16)
    acc_scr[...] += dot(o_ref[...], wo_ref[...])

    @pl.when(step == pl.num_programs(0) - 1)
    def _():
        h_ref[...] = acc_scr[...].astype(jnp.bfloat16)


def space_backward_kernel(
    x_ref, gain_ref, g_ref, q_ref, k_ref, v_ref, o_ref, p_ref,
    wq_ref, wk_ref, wv_ref, wo_ref,
    out_ref,
    gn_scr, go_scr, gs_scr, dq_scr, dk_scr, dv_scr,
):
    step = pl.program_id(0)
    stabs = x_ref.shape[0]
    go = dot_nt(g_ref[...], wo_ref[...]).astype(jnp.bfloat16)
    go_scr[...] = go
    product = go.astype(jnp.float32) * o_ref[...].astype(jnp.float32)
    q_turned = q_ref[...].T
    go_turned = go.T
    for head in range(2):
        cols = slice(head * HEAD_DIM, (head + 1) * HEAD_DIM)
        keys = k_ref[:, cols]
        values = v_ref[:, cols]
        delta = jnp.sum(product[:, cols], axis=-1, keepdims=True)
        for start in range(0, stabs, BACK_CHUNK):
            rows = slice(start, start + BACK_CHUNK)
            grad_weights = dot_nt(go_scr[rows, cols], values)
            weights = p_ref[head, rows, :].astype(jnp.float32)
            grad_scores = (
                weights * ((grad_weights - delta[start : start + BACK_CHUNK]) * FACTOR)
            ).astype(jnp.bfloat16)
            gs_scr[rows, :] = grad_scores
            dq_scr[rows, cols] = dot(grad_scores, keys).astype(jnp.bfloat16)
        dk_scr[cols, :] = dot(q_turned[cols, :], gs_scr[...]).astype(jnp.bfloat16)
        dv_scr[cols, :] = dot(go_turned[cols, :], p_ref[head]).astype(jnp.bfloat16)
    part = (
        dot_nt(dq_scr[...], wq_ref[...])
        + dot_nt(dk_scr[...].T, wk_ref[...])
        + dot_nt(dv_scr[...].T, wv_ref[...])
    )

    @pl.when(step == 0)
    def _():
        gn_scr[...] = part

    @pl.when(step > 0)
    def _():
        gn_scr[...] += part

    @pl.when(step == pl.num_programs(0) - 1)
    def _():
        x = x_ref[...].astype(jnp.float32)
        back = norm_back(x, inverse_rms(x), gain_ref[...], gn_scr[...])
        out_ref[...] = (g_ref[...].astype(jnp.float32) + back).astype(jnp.bfloat16)


def time_kernel(
    width, h_ref, side_ref, gain_ref, readout_ref, win_ref, wout_ref,
    g_ref,
    qkv_scr, p_scr, o_scr, go_scr, d_scr,
):
    total, features = h_ref.shape
    tokens = p_scr.shape[-1]
    groups = total // tokens
    hidden = h_ref[...].astype(jnp.float32)
    inverse = inverse_rms(hidden)
    gain = gain_ref[...]
    normed = (hidden * inverse * gain).astype(jnp.bfloat16)
    qkv_scr[...] = dot(normed, win_ref[...]).astype(jnp.bfloat16)
    left = lax.broadcasted_iota(jnp.int32, (tokens, tokens), 0)
    right = lax.broadcasted_iota(jnp.int32, (tokens, tokens), 1)
    kept = ((left % width) == (right % width)) & (right <= left)
    bias = jnp.where(kept, 0.0, MASKED_SCORE)
    bias = jnp.concatenate([bias, bias], axis=0)

    pairs = features // PAIR
    lanes = lax.broadcasted_iota(jnp.int32, (tokens, PAIR), 1)
    near = lanes < HEAD_DIM

    def part(index, pair):
        start = index * features + pair * PAIR
        return slice(start, start + PAIR)

    def rows_of(group):
        return pl.ds(pl.multiple_of(group * tokens, tokens), tokens)

    def stacked(block):
        empty = jnp.zeros_like(block)
        return jnp.concatenate(
            [jnp.where(near, block, empty), jnp.where(near, empty, block)], axis=0
        )

    def merged(block):
        return jnp.where(near, block[:tokens], block[tokens:]).astype(jnp.bfloat16)

    def ahead(group, carry):
        rows = rows_of(group)
        scores = [
            dot_nt(stacked(qkv_scr[rows, part(0, pair)] * FACTOR), qkv_scr[rows, part(1, pair)])
            for pair in range(pairs)
        ]
        weights = [softmax_rows(score + bias) for score in scores]
        for pair in range(pairs):
            p_scr[group * pairs + pair] = weights[pair]
        outs = [dot(weights[pair], qkv_scr[rows, part(2, pair)]) for pair in range(pairs)]
        for pair in range(pairs):
            o_scr[rows, part(0, pair)] = merged(outs[pair])
        return carry

    lax.fori_loop(0, groups, ahead, 0)
    readout = readout_ref[...]
    after = hidden + dot(o_scr[...], wout_ref[...])
    logits = jnp.sum(after * readout, axis=-1, keepdims=True)
    side = side_ref[...]
    grad_logits = (jax.nn.sigmoid(logits) - side[:, 0:1]) * side[:, 1:2]
    grad_after = grad_logits * readout
    go_scr[...] = dot_nt(grad_after.astype(jnp.bfloat16), wout_ref[...]).astype(jnp.bfloat16)

    def behind(group, carry):
        rows = rows_of(group)
        span = range(pairs)
        upstream = [stacked(go_scr[rows, part(0, pair)]) for pair in span]
        products = [dot_nt(upstream[pair], qkv_scr[rows, part(2, pair)]) for pair in span]
        weights = [p_scr[group * pairs + pair] for pair in span]
        grad_scores = []
        for pair in span:
            attended = o_scr[rows, part(0, pair)].astype(jnp.float32)
            attended = jnp.concatenate([attended, attended], axis=0)
            delta = jnp.sum(
                upstream[pair].astype(jnp.float32) * attended, axis=-1, keepdims=True
            )
            grad_scores.append(
                (weights[pair].astype(jnp.float32) * ((products[pair] - delta) * FACTOR)).astype(
                    jnp.bfloat16
                )
            )
        queries = [dot(grad_scores[pair], qkv_scr[rows, part(1, pair)]) for pair in span]
        keys = [dot_tn(grad_scores[pair], stacked(qkv_scr[rows, part(0, pair)])) for pair in span]
        values = [dot_tn(weights[pair], upstream[pair]) for pair in span]
        for pair in span:
            d_scr[rows, part(0, pair)] = merged(queries[pair])
            d_scr[rows, part(1, pair)] = keys[pair].astype(jnp.bfloat16)
            d_scr[rows, part(2, pair)] = values[pair].astype(jnp.bfloat16)
        return carry

    lax.fori_loop(0, groups, behind, 0)
    grad_normed = dot_nt(d_scr[...], win_ref[...])
    hidden = h_ref[...].astype(jnp.float32)
    back = norm_back(hidden, inverse, gain, grad_normed)
    g_ref[...] = (grad_logits * readout + back).astype(jnp.bfloat16)


def everyone_kernel(axes, sizes, src_ref, dst_ref, send_sem, recv_sem, own_sem):
    total = src_ref.shape[0]
    inner = sizes[1]
    here = lax.axis_index("round") * inner + lax.axis_index("stab")
    base = here - lax.rem(here, total)
    place = here - base

    def device(slot):
        index = base + slot
        return (index // inner, lax.rem(index, inner))

    barrier = pltpu.get_barrier_semaphore()

    def greet(step, carry):
        pl.semaphore_signal(
            barrier, inc=1, device_id=device(lax.rem(place + step, total)),
            device_id_type=pl.DeviceIdType.MESH,
        )
        return carry

    lax.fori_loop(1, total, greet, 0)
    pl.semaphore_wait(barrier, total - 1)
    own = pltpu.make_async_copy(src_ref.at[place], dst_ref.at[place], own_sem)
    own.start()

    def copy(step, target, landing):
        return pltpu.make_async_remote_copy(
            src_ref=src_ref.at[target], dst_ref=dst_ref.at[landing],
            send_sem=send_sem.at[target], recv_sem=recv_sem.at[landing],
            device_id=device(target), device_id_type=pl.DeviceIdType.MESH,
        )

    def start(step, carry):
        copy(step, lax.rem(place + step, total), place).start()
        return carry

    def finish(step, carry):
        peer = lax.rem(place + step, total)
        copy(step, peer, peer).wait()
        return carry

    lax.fori_loop(1, total, start, 0)
    lax.fori_loop(1, total, finish, 0)
    own.wait()


def exchange(array, sizes, collective_id):
    total = array.shape[0]
    return pl.pallas_call(
        functools.partial(everyone_kernel, None, sizes),
        out_shape=jax.ShapeDtypeStruct(array.shape, array.dtype),
        in_specs=[pl.BlockSpec(memory_space=pltpu.VMEM)],
        out_specs=pl.BlockSpec(memory_space=pltpu.VMEM),
        scratch_shapes=[
            pltpu.SemaphoreType.DMA((total,)),
            pltpu.SemaphoreType.DMA((total,)),
            pltpu.SemaphoreType.DMA,
        ],
        compiler_params=pltpu.CompilerParams(
            collective_id=collective_id, has_side_effects=True, vmem_limit_bytes=VMEM_LIMIT
        ),
        name="exchange",
    )(array)


def whole(*shape):
    return pl.BlockSpec(shape, lambda step: (0,) * len(shape))


def weight_specs(features):
    pairs = features // PAIR
    return [
        pl.BlockSpec((features, PAIR), lambda step: (0, step)),
        pl.BlockSpec((features, PAIR), lambda step: (0, pairs + step)),
        pl.BlockSpec((features, PAIR), lambda step: (0, 2 * pairs + step)),
        pl.BlockSpec((PAIR, features), lambda step: (step, 0)),
    ]


def space_forward(x, neighbours, gain, w_in, w_out):
    stabs, features = x.shape
    pairs = features // PAIR
    column = pl.BlockSpec((stabs, PAIR), lambda step: (0, step))
    rows = jax.ShapeDtypeStruct((stabs, features), jnp.bfloat16)
    square = pl.BlockSpec((2, stabs, stabs), lambda step: (step, 0, 0))
    return pl.pallas_call(
        space_forward_kernel,
        grid=(pairs,),
        in_specs=[whole(stabs, features), whole(*neighbours.shape), whole(1, features)]
        + weight_specs(features),
        out_specs=[whole(stabs, features), column, column, column, column, square],
        out_shape=[
            rows, rows, rows, rows, rows,
            jax.ShapeDtypeStruct((2 * pairs, stabs, stabs), jnp.bfloat16),
        ],
        scratch_shapes=[
            pltpu.VMEM((stabs, features), jnp.bfloat16),
            pltpu.VMEM((stabs, stabs), jnp.float32),
            pltpu.VMEM((stabs, features), jnp.float32),
        ],
        compiler_params=pltpu.CompilerParams(vmem_limit_bytes=VMEM_LIMIT),
        name="space_forward",
    )(x, neighbours, gain, w_in, w_in, w_in, w_out)


def space_backward(x, gain, grad, saved, w_in, w_out):
    stabs, features = x.shape
    pairs = features // PAIR
    column = pl.BlockSpec((stabs, PAIR), lambda step: (0, step))
    square = pl.BlockSpec((2, stabs, stabs), lambda step: (step, 0, 0))
    return pl.pallas_call(
        space_backward_kernel,
        grid=(pairs,),
        in_specs=[whole(stabs, features), whole(1, features), whole(stabs, features)]
        + [column] * 4
        + [square]
        + weight_specs(features),
        out_specs=whole(stabs, features),
        out_shape=jax.ShapeDtypeStruct((stabs, features), jnp.bfloat16),
        scratch_shapes=[
            pltpu.VMEM((stabs, features), jnp.float32),
            pltpu.VMEM((stabs, PAIR), jnp.bfloat16),
            pltpu.VMEM((stabs, stabs), jnp.bfloat16),
            pltpu.VMEM((stabs, PAIR), jnp.bfloat16),
            pltpu.VMEM((PAIR, stabs), jnp.bfloat16),
            pltpu.VMEM((PAIR, stabs), jnp.bfloat16),
        ],
        compiler_params=pltpu.CompilerParams(vmem_limit_bytes=VMEM_LIMIT),
        name="space_backward",
    )(x, gain, grad, *saved, w_in, w_in, w_in, w_out)


def time_both(hidden, side, gain, readout, w_in, w_out, width, tokens):
    total, features = hidden.shape
    return pl.pallas_call(
        functools.partial(time_kernel, width),
        out_shape=jax.ShapeDtypeStruct((total, features), jnp.bfloat16),
        scratch_shapes=[
            pltpu.VMEM((total, 3 * features), jnp.bfloat16),
            pltpu.VMEM((total // tokens * (features // PAIR), 2 * tokens, tokens), jnp.bfloat16),
            pltpu.VMEM((total, features), jnp.bfloat16),
            pltpu.VMEM((total, features), jnp.bfloat16),
            pltpu.VMEM((total, 3 * features), jnp.bfloat16),
        ],
        compiler_params=pltpu.CompilerParams(vmem_limit_bytes=VMEM_LIMIT),
        name="time_both",
    )(hidden, side, gain, readout, w_in, w_out)


def body(
    round_size,
    stab_size,
    inputs,
    labels,
    neighbours,
    space_in_weights,
    space_out_weights,
    space_gain,
    time_in_weights,
    time_out_weights,
    time_gain,
    readout,
):
    rounds_here, stabs_here, features = inputs.shape
    rounds = rounds_here * round_size
    stabs = stabs_here * stab_size
    copies = stab_size // rounds_here
    assert copies * rounds_here == stab_size
    padded = -(-stabs_here // round_size) * round_size
    part = padded // round_size
    direct = copies == 1 and padded == stabs_here
    sizes = (round_size, stab_size)
    both = ("round", "stab")
    space_gain, time_gain, readout = space_gain[None], time_gain[None], readout[None]

    def to_rounds(tokens):
        if copies > 1:
            tokens = jnp.repeat(tokens, copies, axis=0)
        if direct:
            return exchange(tokens, sizes, 1).reshape(stabs, features)
        return lax.all_to_all(tokens, "stab", split_axis=0, concat_axis=1, tiled=True)[0]

    def to_tokens(rows):
        split = rows.reshape(stab_size, stabs_here, features)
        if direct:
            return exchange(split, sizes, 1)
        moved = lax.all_to_all(split, "stab", split_axis=0, concat_axis=0, tiled=True)
        return moved[::copies] if copies > 1 else moved

    def pad_stabs(tokens):
        return jnp.pad(tokens, ((0, 0), (0, padded - stabs_here), (0, 0)))

    def to_times(rows):
        if direct:
            sent = rows.reshape(rounds, part * features // 128, 128)
            return exchange(sent, sizes, 2).reshape(rounds, part, features)
        tokens = pad_stabs(to_tokens(rows))
        return lax.all_to_all(tokens, "round", split_axis=1, concat_axis=0, tiled=True)

    def from_times(times):
        if direct:
            sent = times.reshape(rounds, part * features // 128, 128)
            return exchange(sent, sizes, 2).reshape(stabs, features)
        tokens = lax.all_to_all(times, "round", split_axis=0, concat_axis=1, tiled=True)
        return to_rounds(tokens[:, :stabs_here])

    here_round, here_stab = lax.axis_index("round"), lax.axis_index("stab")
    if direct:
        first = (here_round * stab_size + here_stab) * part
        chunks = jnp.transpose(labels.reshape(rounds_here, round_size, part), (1, 0, 2))
        sent = jnp.tile(chunks.reshape(round_size, rounds_here * part), (stab_size, 1))
        came = lax.all_to_all(sent, both, split_axis=0, concat_axis=0, tiled=True)
        came = came.reshape(round_size, stab_size, rounds_here, part)
        owner = (here_round * stab_size + here_stab) // round_size
        targets = lax.dynamic_index_in_dim(came, owner, 1, keepdims=False)
        targets = targets.reshape(rounds, part).astype(jnp.float32)
    else:
        first = here_stab * stabs_here + here_round * part
        labels_all = lax.all_gather(labels, both, axis=0, tiled=False)
        labels_all = labels_all.reshape(round_size, stab_size, rounds_here, stabs_here)
        labels_all = jnp.transpose(labels_all, (0, 2, 1, 3)).reshape(rounds, stabs)
        labels_all = jnp.pad(labels_all, ((0, 0), (0, padded)))
        targets = lax.dynamic_slice(labels_all, (0, first), (rounds, part)).astype(jnp.float32)
    slot = jnp.arange(part) + (here_round * part if not direct else 0)
    real = first + jnp.arange(part) < STABS_REAL
    if not direct:
        real = real & (slot < stabs_here)
    side = jnp.stack([targets, jnp.broadcast_to(real.astype(jnp.float32), targets.shape)], axis=-1)

    width = max(1, GROUP // rounds)
    while part % width:
        width -= 1
    groups = part // width
    tokens = width * rounds

    def to_groups(times):
        depth = times.shape[-1]
        split = times.reshape(rounds, groups, width, depth)
        return jnp.transpose(split, (1, 0, 2, 3)).reshape(groups * tokens, depth)

    def from_groups(rows):
        split = rows.reshape(groups, rounds, width, features)
        return jnp.transpose(split, (1, 0, 2, 3)).reshape(rounds, part, features)

    x = to_rounds(inputs)
    after_space, *saved = space_forward(
        x, neighbours, space_gain, space_in_weights, space_out_weights
    )
    times = to_groups(to_times(after_space))
    grad_times = time_both(
        times, to_groups(side), time_gain, readout, time_in_weights, time_out_weights, width, tokens
    )
    grad_space = from_times(from_groups(grad_times))
    grad = space_backward(x, space_gain, grad_space, saved, space_in_weights, space_out_weights)
    return to_tokens(grad).astype(jnp.float32)


def solution(mesh):
    in_specs = (
        P("round", "stab", None),
        P("round", "stab"),
        P(),
        P(),
        P(),
        P(),
        P(),
        P(),
        P(),
        P(),
    )
    out_specs = P("round", "stab", None)
    sized = functools.partial(body, mesh.shape["round"], mesh.shape["stab"])
    return jax.shard_map(sized, mesh=mesh, in_specs=in_specs, out_specs=out_specs, check_vma=False)
```

```python
import functools

import jax
import jax.numpy as jnp
from jax import lax
from jax.experimental import pallas as pl
from jax.experimental.pallas import tpu as pltpu
from jax.sharding import PartitionSpec as P

HEADS = 8
HEAD_DIM = 64
STABS_REAL = 840
BLOCK = 4
PAIR = 2 * HEAD_DIM
CHUNK = 448
BACK_CHUNK = 448
GROUP = 128

EPSILON = 1e-06
MASKED_SCORE = -1e30
FACTOR = HEAD_DIM ** (-0.5)
VMEM_LIMIT = 50 * 1024 * 1024


def dot(first, second):
    return jnp.dot(first, second, preferred_element_type=jnp.float32)


def dot_nt(first, second):
    return lax.dot_general(
        first, second, (((1,), (1,)), ((), ())), preferred_element_type=jnp.float32
    )


def dot_tn(first, second):
    return lax.dot_general(
        first, second, (((0,), (0,)), ((), ())), preferred_element_type=jnp.float32
    )


def inverse_rms(hidden):
    return lax.rsqrt(jnp.mean(hidden * hidden, axis=-1, keepdims=True) + EPSILON)


def norm_back(hidden, inverse, gain, upstream):
    scaled = upstream * gain
    inner = jnp.mean(hidden * scaled, axis=-1, keepdims=True)
    return inverse * scaled - hidden * (inverse * inverse * inverse * inner)


def softmax_rows(scores):
    highest = jnp.max(scores, axis=-1, keepdims=True)
    weights = jnp.exp(scores - highest)
    total = jnp.sum(weights, axis=-1, keepdims=True)
    return (weights * (1.0 / total)).astype(jnp.bfloat16)


def space_forward_kernel(
    x_ref, near_ref, gain_ref, wq_ref, wk_ref, wv_ref, wo_ref,
    h_ref, q_ref, k_ref, v_ref, o_ref, p_ref,
    n_scr, bias_scr, acc_scr,
):
    step = pl.program_id(0)
    stabs = x_ref.shape[0]
    blocks, links = near_ref.shape

    @pl.when(step == 0)
    def _():
        x = x_ref[...].astype(jnp.float32)
        n_scr[...] = (x * inverse_rms(x) * gain_ref[...]).astype(jnp.bfloat16)
        acc_scr[...] = x
        lanes = lax.broadcasted_iota(jnp.int32, (blocks, blocks), 1)
        near = near_ref[...]
        listed = jnp.zeros((blocks, blocks), jnp.float32)
        for link in range(links):
            listed = jnp.where(lanes == near[:, link : link + 1], 1.0, listed)
        owner = lax.broadcasted_iota(jnp.int32, (stabs, blocks), 0) // BLOCK
        column = lax.broadcasted_iota(jnp.int32, (stabs, blocks), 1)
        widen = jnp.where(owner == column, 1.0, 0.0).astype(jnp.bfloat16)
        rows = dot(widen, listed.astype(jnp.bfloat16)).astype(jnp.bfloat16)
        bias_scr[...] = jnp.where(dot_nt(rows, widen) > 0.5, 0.0, MASKED_SCORE)

    n = n_scr[...]
    q_ref[...] = dot(n, wq_ref[...]).astype(jnp.bfloat16)
    k_ref[...] = dot(n, wk_ref[...]).astype(jnp.bfloat16)
    v_ref[...] = dot(n, wv_ref[...]).astype(jnp.bfloat16)
    for head in range(2):
        cols = slice(head * HEAD_DIM, (head + 1) * HEAD_DIM)
        keys = k_ref[:, cols]
        values = v_ref[:, cols]
        for start in range(0, stabs, CHUNK):
            rows = slice(start, start + CHUNK)
            scores = dot_nt(q_ref[rows, cols] * FACTOR, keys) + bias_scr[rows, :]
            weights = softmax_rows(scores)
            p_ref[head, rows, :] = weights
            o_ref[rows, cols] = dot(weights, values).astype(jnp.bfloat16)
    acc_scr[...] += dot(o_ref[...], wo_ref[...])

    @pl.when(step == pl.num_programs(0) - 1)
    def _():
        h_ref[...] = acc_scr[...].astype(jnp.bfloat16)


def space_backward_kernel(
    x_ref, gain_ref, g_ref, q_ref, k_ref, v_ref, o_ref, p_ref,
    wq_ref, wk_ref, wv_ref, wo_ref,
    out_ref,
    gn_scr, go_scr, gs_scr, dq_scr, dk_scr, dv_scr,
):
    step = pl.program_id(0)
    stabs = x_ref.shape[0]
    go = dot_nt(g_ref[...], wo_ref[...]).astype(jnp.bfloat16)
    go_scr[...] = go
    product = go.astype(jnp.float32) * o_ref[...].astype(jnp.float32)
    q_turned = q_ref[...].T
    go_turned = go.T
    for head in range(2):
        cols = slice(head * HEAD_DIM, (head + 1) * HEAD_DIM)
        keys = k_ref[:, cols]
        values = v_ref[:, cols]
        delta = jnp.sum(product[:, cols], axis=-1, keepdims=True)
        for start in range(0, stabs, BACK_CHUNK):
            rows = slice(start, start + BACK_CHUNK)
            grad_weights = dot_nt(go_scr[rows, cols], values)
            weights = p_ref[head, rows, :].astype(jnp.float32)
            grad_scores = (
                weights * ((grad_weights - delta[start : start + BACK_CHUNK]) * FACTOR)
            ).astype(jnp.bfloat16)
            gs_scr[rows, :] = grad_scores
            dq_scr[rows, cols] = dot(grad_scores, keys).astype(jnp.bfloat16)
        dk_scr[cols, :] = dot(q_turned[cols, :], gs_scr[...]).astype(jnp.bfloat16)
        dv_scr[cols, :] = dot(go_turned[cols, :], p_ref[head]).astype(jnp.bfloat16)
    part = (
        dot_nt(dq_scr[...], wq_ref[...])
        + dot_nt(dk_scr[...].T, wk_ref[...])
        + dot_nt(dv_scr[...].T, wv_ref[...])
    )

    @pl.when(step == 0)
    def _():
        gn_scr[...] = part

    @pl.when(step > 0)
    def _():
        gn_scr[...] += part

    @pl.when(step == pl.num_programs(0) - 1)
    def _():
        x = x_ref[...].astype(jnp.float32)
        back = norm_back(x, inverse_rms(x), gain_ref[...], gn_scr[...])
        out_ref[...] = (g_ref[...].astype(jnp.float32) + back).astype(jnp.bfloat16)


def time_kernel(
    width, h_ref, side_ref, gain_ref, readout_ref, win_ref, wout_ref,
    g_ref,
    qkv_scr, p_scr, o_scr, go_scr, d_scr,
):
    total, features = h_ref.shape
    tokens = p_scr.shape[-1]
    groups = total // tokens
    hidden = h_ref[...].astype(jnp.float32)
    inverse = inverse_rms(hidden)
    gain = gain_ref[...]
    normed = (hidden * inverse * gain).astype(jnp.bfloat16)
    qkv_scr[...] = dot(normed, win_ref[...]).astype(jnp.bfloat16)
    left = lax.broadcasted_iota(jnp.int32, (tokens, tokens), 0)
    right = lax.broadcasted_iota(jnp.int32, (tokens, tokens), 1)
    kept = ((left % width) == (right % width)) & (right <= left)
    bias = jnp.where(kept, 0.0, MASKED_SCORE)
    bias = jnp.concatenate([bias, bias], axis=0)

    pairs = features // PAIR
    lanes = lax.broadcasted_iota(jnp.int32, (tokens, PAIR), 1)
    near = lanes < HEAD_DIM

    def part(index, pair):
        start = index * features + pair * PAIR
        return slice(start, start + PAIR)

    def rows_of(group):
        return pl.ds(pl.multiple_of(group * tokens, tokens), tokens)

    def stacked(block):
        empty = jnp.zeros_like(block)
        return jnp.concatenate(
            [jnp.where(near, block, empty), jnp.where(near, empty, block)], axis=0
        )

    def merged(block):
        return jnp.where(near, block[:tokens], block[tokens:]).astype(jnp.bfloat16)

    def ahead(group, carry):
        rows = rows_of(group)
        scores = [
            dot_nt(stacked(qkv_scr[rows, part(0, pair)] * FACTOR), qkv_scr[rows, part(1, pair)])
            for pair in range(pairs)
        ]
        weights = [softmax_rows(score + bias) for score in scores]
        for pair in range(pairs):
            p_scr[group * pairs + pair] = weights[pair]
        outs = [dot(weights[pair], qkv_scr[rows, part(2, pair)]) for pair in range(pairs)]
        for pair in range(pairs):
            o_scr[rows, part(0, pair)] = merged(outs[pair])
        return carry

    lax.fori_loop(0, groups, ahead, 0)
    readout = readout_ref[...]
    after = hidden + dot(o_scr[...], wout_ref[...])
    logits = jnp.sum(after * readout, axis=-1, keepdims=True)
    side = side_ref[...]
    grad_logits = (jax.nn.sigmoid(logits) - side[:, 0:1]) * side[:, 1:2]
    grad_after = grad_logits * readout
    go_scr[...] = dot_nt(grad_after.astype(jnp.bfloat16), wout_ref[...]).astype(jnp.bfloat16)

    def behind(group, carry):
        rows = rows_of(group)
        span = range(pairs)
        upstream = [stacked(go_scr[rows, part(0, pair)]) for pair in span]
        products = [dot_nt(upstream[pair], qkv_scr[rows, part(2, pair)]) for pair in span]
        weights = [p_scr[group * pairs + pair] for pair in span]
        grad_scores = []
        for pair in span:
            attended = o_scr[rows, part(0, pair)].astype(jnp.float32)
            attended = jnp.concatenate([attended, attended], axis=0)
            delta = jnp.sum(
                upstream[pair].astype(jnp.float32) * attended, axis=-1, keepdims=True
            )
            grad_scores.append(
                (weights[pair].astype(jnp.float32) * ((products[pair] - delta) * FACTOR)).astype(
                    jnp.bfloat16
                )
            )
        queries = [dot(grad_scores[pair], qkv_scr[rows, part(1, pair)]) for pair in span]
        keys = [dot_tn(grad_scores[pair], stacked(qkv_scr[rows, part(0, pair)])) for pair in span]
        values = [dot_tn(weights[pair], upstream[pair]) for pair in span]
        for pair in span:
            d_scr[rows, part(0, pair)] = merged(queries[pair])
            d_scr[rows, part(1, pair)] = keys[pair].astype(jnp.bfloat16)
            d_scr[rows, part(2, pair)] = values[pair].astype(jnp.bfloat16)
        return carry

    lax.fori_loop(0, groups, behind, 0)
    grad_normed = dot_nt(d_scr[...], win_ref[...])
    hidden = h_ref[...].astype(jnp.float32)
    back = norm_back(hidden, inverse, gain, grad_normed)
    g_ref[...] = (grad_logits * readout + back).astype(jnp.bfloat16)


def whole(*shape):
    return pl.BlockSpec(shape, lambda step: (0,) * len(shape))


def weight_specs(features):
    pairs = features // PAIR
    return [
        pl.BlockSpec((features, PAIR), lambda step: (0, step)),
        pl.BlockSpec((features, PAIR), lambda step: (0, pairs + step)),
        pl.BlockSpec((features, PAIR), lambda step: (0, 2 * pairs + step)),
        pl.BlockSpec((PAIR, features), lambda step: (step, 0)),
    ]


def space_forward(x, neighbours, gain, w_in, w_out):
    stabs, features = x.shape
    pairs = features // PAIR
    column = pl.BlockSpec((stabs, PAIR), lambda step: (0, step))
    rows = jax.ShapeDtypeStruct((stabs, features), jnp.bfloat16)
    square = pl.BlockSpec((2, stabs, stabs), lambda step: (step, 0, 0))
    return pl.pallas_call(
        space_forward_kernel,
        grid=(pairs,),
        in_specs=[whole(stabs, features), whole(*neighbours.shape), whole(1, features)]
        + weight_specs(features),
        out_specs=[whole(stabs, features), column, column, column, column, square],
        out_shape=[
            rows, rows, rows, rows, rows,
            jax.ShapeDtypeStruct((2 * pairs, stabs, stabs), jnp.bfloat16),
        ],
        scratch_shapes=[
            pltpu.VMEM((stabs, features), jnp.bfloat16),
            pltpu.VMEM((stabs, stabs), jnp.float32),
            pltpu.VMEM((stabs, features), jnp.float32),
        ],
        compiler_params=pltpu.CompilerParams(vmem_limit_bytes=VMEM_LIMIT),
        name="space_forward",
    )(x, neighbours, gain, w_in, w_in, w_in, w_out)


def space_backward(x, gain, grad, saved, w_in, w_out):
    stabs, features = x.shape
    pairs = features // PAIR
    column = pl.BlockSpec((stabs, PAIR), lambda step: (0, step))
    square = pl.BlockSpec((2, stabs, stabs), lambda step: (step, 0, 0))
    return pl.pallas_call(
        space_backward_kernel,
        grid=(pairs,),
        in_specs=[whole(stabs, features), whole(1, features), whole(stabs, features)]
        + [column] * 4
        + [square]
        + weight_specs(features),
        out_specs=whole(stabs, features),
        out_shape=jax.ShapeDtypeStruct((stabs, features), jnp.bfloat16),
        scratch_shapes=[
            pltpu.VMEM((stabs, features), jnp.float32),
            pltpu.VMEM((stabs, PAIR), jnp.bfloat16),
            pltpu.VMEM((stabs, stabs), jnp.bfloat16),
            pltpu.VMEM((stabs, PAIR), jnp.bfloat16),
            pltpu.VMEM((PAIR, stabs), jnp.bfloat16),
            pltpu.VMEM((PAIR, stabs), jnp.bfloat16),
        ],
        compiler_params=pltpu.CompilerParams(vmem_limit_bytes=VMEM_LIMIT),
        name="space_backward",
    )(x, gain, grad, *saved, w_in, w_in, w_in, w_out)


def time_both(hidden, side, gain, readout, w_in, w_out, width, tokens):
    total, features = hidden.shape
    return pl.pallas_call(
        functools.partial(time_kernel, width),
        out_shape=jax.ShapeDtypeStruct((total, features), jnp.bfloat16),
        scratch_shapes=[
            pltpu.VMEM((total, 3 * features), jnp.bfloat16),
            pltpu.VMEM((total // tokens * (features // PAIR), 2 * tokens, tokens), jnp.bfloat16),
            pltpu.VMEM((total, features), jnp.bfloat16),
            pltpu.VMEM((total, features), jnp.bfloat16),
            pltpu.VMEM((total, 3 * features), jnp.bfloat16),
        ],
        compiler_params=pltpu.CompilerParams(vmem_limit_bytes=VMEM_LIMIT),
        name="time_both",
    )(hidden, side, gain, readout, w_in, w_out)


PIECE = 16
SPLIT = (1, 2, 2, 2)
MEGA_VMEM = 60 * 1024 * 1024


def spans():
    first = 0
    found = []
    for count in SPLIT:
        found.append((first, count))
        first += count
    return found


def half_turn(tiles):
    return pltpu.roll(tiles, 4, 1)


def pack_messages(rows):
    tiles = rows.shape[0] // 8
    cut = rows.reshape(tiles, 8, rows.shape[1])
    upper = lax.broadcasted_iota(jnp.int32, (tiles, 8, 128), 1) < 4
    parts = [cut[:, :, at : at + 128] for at in range(0, rows.shape[1], 128)]
    turned = [half_turn(part) for part in parts]
    low = [jnp.where(upper, parts[at], turned[at + 1]) for at in (0, 2)]
    high = [jnp.where(upper, turned[at], parts[at + 1]) for at in (0, 2)]
    low = jnp.concatenate(low, axis=1)[:, None]
    high = jnp.concatenate(high, axis=1)[:, None]
    return jnp.concatenate([low, high], axis=1).reshape(2 * tiles, 16, 128)


def unpack_messages(messages):
    tiles = messages.shape[0] // 2
    cut = messages.astype(jnp.float32).reshape(tiles, 2, 2, 8, 128)
    upper = lax.broadcasted_iota(jnp.int32, (tiles, 8, 128), 1) < 4
    found = []
    for part in range(2):
        low, high = cut[:, 0, part], cut[:, 1, part]
        found.append(jnp.where(upper, low, half_turn(high)))
        found.append(jnp.where(upper, half_turn(low), high))
    return jnp.concatenate(found, axis=2).reshape(8 * tiles, 512)


def layer_kernel(
    sizes,
    x_in, labels_in, near_ref, space_gain_ref, time_gain_ref, readout_ref,
    space_in_hbm, space_out_hbm, time_in_hbm, time_out_hbm,
    out_ref,
    x_scr, lab_scr, wsi, wso, wti, wto,
    bias_scr, qkv_scr, p_scr, o_scr, inv_scr,
    send_h, recv_h, send_g, recv_g, g_scr, go_scr, acc_scr, d_scr, out_scr,
    tqkv, tp, to, tgo, td,
    bar_dummy, weight_sem, x_send, x_recv, lab_send, lab_recv,
    h_send, h_recv, g_send, g_recv, out_send, out_recv,
):
    del bar_dummy
    depth, inner = sizes
    total = depth * inner
    here_z, here_s = lax.axis_index("round"), lax.axis_index("stab")
    here = here_z * inner + here_s
    here_chip = here_s // 2
    here_core = lax.rem(here_s, 2)
    mesh_ids = pl.DeviceIdType.MESH
    rounds_here, stabs_here, features = x_scr.shape
    stabs = rounds_here * stabs_here
    rounds = depth * rounds_here
    pairs = features // PAIR

    def device(index):
        return (index // inner, lax.rem(index, inner))

    barrier = pltpu.get_barrier_semaphore()

    def greet(step, carry):
        pl.semaphore_signal(
            barrier, inc=1, device_id=device(lax.rem(here + step, total)), device_id_type=mesh_ids
        )
        return carry

    lax.fori_loop(1, total, greet, 0)
    weights = [
        pltpu.make_async_copy(source, target, weight_sem.at[index])
        for index, (source, target) in enumerate(
            [(space_in_hbm, wsi), (space_out_hbm, wso), (time_in_hbm, wti), (time_out_hbm, wto)]
        )
    ]
    for copy in weights:
        copy.start()
    pl.semaphore_wait(barrier, total - 1)

    def send_x(step, carry):
        peer = lax.rem(here_s + step, inner)
        pltpu.make_async_remote_copy(
            src_ref=x_in.at[peer], dst_ref=x_scr.at[here_s],
            send_sem=x_send, recv_sem=x_recv,
            device_id=(here_z, peer), device_id_type=mesh_ids,
        ).start()
        return carry

    lax.fori_loop(1, inner, send_x, 0)
    pltpu.make_async_copy(x_in.at[here_s], x_scr.at[here_s], x_recv).start()

    def send_labels(step, carry):
        peer = lax.rem(here_z + step, depth)
        pltpu.make_async_remote_copy(
            src_ref=labels_in, dst_ref=lab_scr.at[here_z],
            send_sem=lab_send, recv_sem=lab_recv,
            device_id=(peer, here_s), device_id_type=mesh_ids,
        ).start()
        return carry

    lax.fori_loop(1, depth, send_labels, 0)
    pltpu.make_async_copy(labels_in, lab_scr.at[here_z], lab_recv).start()

    blocks = stabs // BLOCK
    owner = lax.broadcasted_iota(jnp.int32, (stabs, blocks), 0) // BLOCK
    column = lax.broadcasted_iota(jnp.int32, (stabs, blocks), 1)
    widen = jnp.where(owner == column, 1.0, 0.0).astype(jnp.bfloat16)
    key_block = lax.broadcasted_iota(jnp.int32, (blocks, 128), 0)
    for index in range(len(SPLIT)):
        near = near_ref[index]
        listed = jnp.zeros((blocks, 128), jnp.float32)
        for link in range(near.shape[0]):
            listed = jnp.where(key_block == near[link : link + 1, :], 1.0, listed)
        spread = dot(widen, listed.astype(jnp.bfloat16))
        bias_scr[index] = jnp.where(spread > 0.5, 0.0, MASKED_SCORE).astype(jnp.bfloat16)

    near_lanes = lax.broadcasted_iota(jnp.int32, (1, PAIR), 1) < HEAD_DIM
    head_masks = [
        near_lanes.astype(jnp.float32).astype(jnp.bfloat16),
        1 - near_lanes.astype(jnp.float32).astype(jnp.bfloat16),
    ]

    pltpu.make_async_copy(x_scr, x_scr, x_recv).wait()
    weights[0].wait()
    x = x_scr[...].reshape(stabs, features).astype(jnp.float32)
    normed = (x * inverse_rms(x) * space_gain_ref[...]).astype(jnp.bfloat16)
    for third in range(3):
        cols = slice(third * features, (third + 1) * features)
        made = dot(normed, wsi[:, cols]).astype(jnp.bfloat16)
        qkv_scr[:, :, cols] = made.reshape(rounds_here, stabs_here, features)
    weights[1].wait()

    def pair_cols(pair, third):
        return pl.ds(pl.multiple_of(third * features + pair * PAIR, PAIR), PAIR)

    def all_rows(pair, third):
        return qkv_scr[:, :, pair_cols(pair, third)].reshape(stabs, PAIR)

    def send_span(first, count, source, target, send_sem, recv_sem):
        rows = pl.ds(first * PIECE, count * PIECE)

        def send(step, carry):
            peer = lax.rem(here + step, total)
            pltpu.make_async_remote_copy(
                src_ref=source.at[peer, rows], dst_ref=target.at[here, rows],
                send_sem=send_sem, recv_sem=recv_sem,
                device_id=device(peer), device_id_type=mesh_ids,
            ).start()
            return carry

        lax.fori_loop(1, total, send, 0)
        pltpu.make_async_copy(source.at[here, rows], target.at[here, rows], recv_sem).start()

    def wait_span(first, count, target, recv_sem):
        whole_span = target.at[:, pl.ds(first * PIECE, count * PIECE)]
        pltpu.make_async_copy(whole_span, whole_span, recv_sem).wait()

    def place_messages(first, count, rows, target, outer):
        per = rows.shape[0] // count
        for piece in range(count):
            cut = rows[piece * per : (piece + 1) * per]
            target[:, (first + piece) * PIECE : (first + piece + 1) * PIECE, :] = cut

    for index, (first, count) in enumerate(spans()):
        height = count * 128
        rows = slice(first * PIECE, (first + count) * PIECE)
        flat = slice(first * 128, (first + count) * 128)
        row_block = lax.broadcasted_iota(jnp.int32, (height, 128), 0) // BLOCK
        lane = lax.broadcasted_iota(jnp.int32, (height, 128), 1)
        onehot = jnp.where(row_block == lane, 1.0, 0.0).astype(jnp.bfloat16)

        def ahead(pair, carry, rows=rows, flat=flat, height=height, onehot=onehot, index=index):
            queries = qkv_scr[:, rows, pair_cols(pair, 0)].reshape(height, PAIR) * FACTOR
            keys = jnp.concatenate([all_rows(pair, 1), bias_scr[index]], axis=1)
            values = all_rows(pair, 2)
            out = None
            for half in range(2):
                mask = head_masks[half]
                scores = dot_nt(jnp.concatenate([queries * mask, onehot], axis=1), keys)
                highest = jnp.max(scores, axis=-1, keepdims=True)
                expd = jnp.exp(scores - highest).astype(jnp.bfloat16)
                p_scr[pair * 2 + half, flat, :] = expd
                ones = jnp.broadcast_to(mask, (stabs, PAIR))
                part = dot(expd, jnp.concatenate([values * mask, ones], axis=1))
                out = part if out is None else out + part
            inverse = 1.0 / out[:, PAIR:]
            inv_scr[flat, pair_cols(pair, 0)] = inverse
            o_scr[flat, pair_cols(pair, 0)] = (out[:, :PAIR] * inverse).astype(jnp.bfloat16)
            return carry

        lax.fori_loop(0, pairs, ahead, 0)
        hidden = x_scr[:, rows, :].reshape(height, features).astype(jnp.float32)
        hidden = hidden + dot(o_scr[flat, :], wso[...])
        hidden = hidden.reshape(inner, count, PIECE, features)
        for piece in range(count):
            packed = pack_messages(hidden[:, piece].reshape(128, features)).astype(jnp.bfloat16)
            packed = packed.reshape(inner, depth, 16, 128)
            at = slice((first + piece) * PIECE, (first + piece + 1) * PIECE)
            for z in range(depth):
                send_h[z * inner : (z + 1) * inner, at, :] = packed[:, z]
        send_span(first, count, send_h, recv_h, h_send, h_recv.at[index])

    tokens = BLOCK * rounds
    left = lax.broadcasted_iota(jnp.int32, (tokens, tokens), 0)
    right = lax.broadcasted_iota(jnp.int32, (tokens, tokens), 1)
    kept = ((left % BLOCK) == (right % BLOCK)) & (right <= left)
    causal = jnp.where(kept, 0.0, MASKED_SCORE)
    causal = jnp.concatenate([causal, causal], axis=0)
    lanes = lax.broadcasted_iota(jnp.int32, (tokens, PAIR), 1)
    is_near = lanes < HEAD_DIM

    def stacked(block):
        empty = jnp.zeros_like(block)
        return jnp.concatenate(
            [jnp.where(is_near, block, empty), jnp.where(is_near, empty, block)], axis=0
        )

    def merged(block):
        return jnp.where(is_near, block[:tokens], block[tokens:]).astype(jnp.bfloat16)

    pltpu.make_async_copy(lab_scr, lab_scr, lab_recv).wait()
    token_round = lax.broadcasted_iota(jnp.int32, (tokens, rounds), 0) // BLOCK
    which_round = lax.broadcasted_iota(jnp.int32, (tokens, rounds), 1)
    pick = jnp.where(token_round == which_round, 1.0, 0.0).astype(jnp.bfloat16)
    labels = lab_scr[...].reshape(rounds, stabs_here).astype(jnp.float32).astype(jnp.bfloat16)
    token_labels = dot(pick, labels)
    stab_lane = lax.broadcasted_iota(jnp.int32, (tokens, stabs_here), 1)
    token_slot = lax.broadcasted_iota(jnp.int32, (tokens, stabs_here), 0) % BLOCK
    slot_column = lax.broadcasted_iota(jnp.int32, (tokens, 1), 0) % BLOCK
    weights[2].wait()
    weights[3].wait()

    for index, (first, count) in enumerate(spans()):
        wait_span(first, count, recv_h, h_recv.at[index])
        height = count * tokens
        pieces = range(count)
        found = [
            unpack_messages(recv_h[:, (first + piece) * PIECE : (first + piece + 1) * PIECE, :])
            for piece in pieces
        ]
        hidden = jnp.concatenate(found, axis=0) if count > 1 else found[0]
        inverse = inverse_rms(hidden)
        gain = time_gain_ref[...]
        normed = (hidden * inverse * gain).astype(jnp.bfloat16)
        tqkv[:height, :] = dot(normed, wti[...]).astype(jnp.bfloat16)
        jobs = [(piece, pair) for piece in pieces for pair in range(pairs)]

        def part(third, pair):
            return slice(third * features + pair * PAIR, third * features + (pair + 1) * PAIR)

        def span_of(piece):
            return slice(piece * tokens, (piece + 1) * tokens)

        scores = [
            dot_nt(stacked(tqkv[span_of(i), part(0, p)] * FACTOR), tqkv[span_of(i), part(1, p)])
            for i, p in jobs
        ]
        probs = [softmax_rows(score + causal) for score in scores]
        for job, (i, p) in enumerate(jobs):
            tp[job] = probs[job]
        outs = [dot(probs[job], tqkv[span_of(i), part(2, p)]) for job, (i, p) in enumerate(jobs)]
        for job, (i, p) in enumerate(jobs):
            to[span_of(i), part(0, p)] = merged(outs[job])
        readout = readout_ref[...]
        after = hidden + dot(to[:height, :], wto[...])
        logits = jnp.sum(after * readout, axis=-1, keepdims=True)
        targets, real = [], []
        for piece in pieces:
            at = (first + piece) * PIECE + here_z * BLOCK
            chosen = jnp.where(stab_lane == at + token_slot, token_labels, 0.0)
            targets.append(jnp.sum(chosen, axis=-1, keepdims=True))
            where = here_s * stabs_here + at + slot_column
            real.append(jnp.where(where < STABS_REAL, 1.0, 0.0))
        targets = jnp.concatenate(targets, axis=0) if count > 1 else targets[0]
        real = jnp.concatenate(real, axis=0) if count > 1 else real[0]
        grad_logits = (jax.nn.sigmoid(logits) - targets) * real
        grad_after = grad_logits * readout
        tgo[:height, :] = dot_nt(grad_after.astype(jnp.bfloat16), wto[...]).astype(jnp.bfloat16)

        upstream = [stacked(tgo[span_of(i), part(0, p)]) for i, p in jobs]
        products = [
            dot_nt(upstream[job], tqkv[span_of(i), part(2, p)]) for job, (i, p) in enumerate(jobs)
        ]
        grads = []
        for job, (i, p) in enumerate(jobs):
            attended = to[span_of(i), part(0, p)].astype(jnp.float32)
            attended = jnp.concatenate([attended, attended], axis=0)
            delta = jnp.sum(
                upstream[job].astype(jnp.float32) * attended, axis=-1, keepdims=True
            )
            grads.append(
                (tp[job].astype(jnp.float32) * ((products[job] - delta) * FACTOR)).astype(
                    jnp.bfloat16
                )
            )
        for job, (i, p) in enumerate(jobs):
            td[span_of(i), part(0, p)] = merged(dot(grads[job], tqkv[span_of(i), part(1, p)]))
            keys = dot_tn(grads[job], stacked(tqkv[span_of(i), part(0, p)]))
            td[span_of(i), part(1, p)] = keys.astype(jnp.bfloat16)
            td[span_of(i), part(2, p)] = dot_tn(tp[job], upstream[job]).astype(jnp.bfloat16)
        grad_normed = dot_nt(td[:height, :], wti[...])
        grad_hidden = grad_after + norm_back(hidden, inverse, gain, grad_normed)
        for piece in pieces:
            packed = pack_messages(grad_hidden[span_of(piece)]).astype(jnp.bfloat16)
            send_g[:, (first + piece) * PIECE : (first + piece + 1) * PIECE, :] = packed
        send_span(first, count, send_g, recv_g, g_send, g_recv.at[index])

    for index, (first, count) in enumerate(spans()):
        wait_span(first, count, recv_g, g_recv.at[index])
        height = count * 128
        rows = slice(first * PIECE, (first + count) * PIECE)
        flat = slice(first * 128, (first + count) * 128)
        for piece in range(count):
            at = slice((first + piece) * PIECE, (first + piece + 1) * PIECE)
            cut = jnp.concatenate(
                [recv_g[z * inner : (z + 1) * inner, at, :][:, None] for z in range(depth)], axis=1
            )
            grad = unpack_messages(cut.reshape(total, 16, 128)).astype(jnp.bfloat16)
            g_scr[:, at, :] = grad.reshape(inner, PIECE, features)
        grad = g_scr[:, rows, :].reshape(height, features)
        go_scr[:height, :] = dot_nt(grad, wso[...]).astype(jnp.bfloat16)
        lane = lax.broadcasted_iota(jnp.int32, (height, PAIR), 1)

        def behind(pair, carry, rows=rows, flat=flat, height=height, lane=lane, index=index):
            cols = pair_cols(pair, 0)
            queries = qkv_scr[:, rows, cols].reshape(height, PAIR) * FACTOR
            keys, values = all_rows(pair, 1), all_rows(pair, 2)
            scaled = (go_scr[:height, cols].astype(jnp.float32) * inv_scr[flat, cols]).astype(
                jnp.bfloat16
            )
            product = scaled.astype(jnp.float32) * o_scr[flat, cols].astype(jnp.float32)
            queries_turned, scaled_turned = queries.T, scaled.T
            ones = jnp.ones((stabs, PAIR), jnp.bfloat16)
            values = jnp.concatenate([values, ones], axis=1)
            grad_queries = None
            for half in range(2):
                mask = head_masks[half]
                mine = (lane < HEAD_DIM) if half == 0 else (lane >= HEAD_DIM)
                delta = jnp.sum(jnp.where(mine, product, 0.0), axis=-1, keepdims=True)
                coarse = delta.astype(jnp.bfloat16).astype(jnp.float32)
                extra = jnp.where(lane == 0, -coarse, jnp.where(lane == 1, coarse - delta, 0.0))
                joined = jnp.concatenate([scaled * mask, extra.astype(jnp.bfloat16)], axis=1)
                grad_weights = dot_nt(joined, values)
                expd = p_scr[pair * 2 + half, flat, :]
                grad_scores = (expd.astype(jnp.float32) * grad_weights).astype(jnp.bfloat16)
                part = dot(grad_scores, keys * mask)
                grad_queries = part if grad_queries is None else grad_queries + part
                turned = slice(half * HEAD_DIM, (half + 1) * HEAD_DIM)
                for kind, turned_rows, square in (
                    (0, queries_turned, grad_scores), (1, scaled_turned, expd),
                ):
                    start = kind * features + pair * PAIR + half * HEAD_DIM
                    into = pl.ds(pl.multiple_of(start, HEAD_DIM), HEAD_DIM)
                    made = dot(turned_rows[turned, :], square)
                    if index == 0:
                        acc_scr[into, :] = made
                    else:
                        acc_scr[into, :] += made
            made = (grad_queries * FACTOR).astype(jnp.bfloat16)
            d_scr[:, rows, cols] = made.reshape(rounds_here, -1, PAIR)
            return carry

        lax.fori_loop(0, pairs, behind, 0)

    def turn(step, carry):
        block = acc_scr[pl.ds(pl.multiple_of(step * PAIR, PAIR), PAIR), :].astype(jnp.bfloat16)
        into = pl.ds(pl.multiple_of(features + step * PAIR, PAIR), PAIR)
        d_scr[:, :, into] = block.T.reshape(rounds_here, stabs_here, PAIR)
        return carry

    lax.fori_loop(0, 2 * pairs, turn, 0)

    chips = inner // 2
    for step in range(1, chips + 1):
        chip = lax.rem(here_chip + step, chips)
        both = pl.ds(2 * chip, 2)
        upstream = d_scr[both].reshape(2 * stabs_here, 3 * features)
        grad_normed = dot_nt(upstream, wsi[...])
        x = x_scr[both].reshape(2 * stabs_here, features).astype(jnp.float32)
        back = norm_back(x, inverse_rms(x), space_gain_ref[...], grad_normed)
        grad = g_scr[both].reshape(2 * stabs_here, features).astype(jnp.float32) + back
        out_scr[both] = grad.astype(jnp.bfloat16).reshape(2, stabs_here, features)

        def send_out(core):
            peer = 2 * chip + core
            pltpu.make_async_remote_copy(
                src_ref=out_scr.at[peer], dst_ref=out_ref.at[here_s],
                send_sem=out_send, recv_sem=out_recv,
                device_id=(here_z, peer), device_id_type=mesh_ids,
            ).start()

        if step < chips:
            send_out(0)
            send_out(1)
        else:
            send_out(1 - here_core)
            pltpu.make_async_copy(out_scr.at[here_s], out_ref.at[here_s], out_recv).start()

    pltpu.make_async_copy(out_ref, out_ref, out_recv).wait()

    def drain(buffer, sem):
        some = buffer.at[pl.ds(0, buffer.shape[0] - 1)]
        pltpu.make_async_copy(some, some, sem).wait()

    drain(x_scr, x_send)
    drain(lab_scr, lab_send)
    drain(send_h, h_send)
    drain(send_g, g_send)
    drain(out_scr, out_send)


def whole_layer(
    sizes, x, labels, near, space_gain, time_gain, readout, space_in, space_out, time_in, time_out
):
    depth, inner = sizes
    total = depth * inner
    rounds_here, stabs_here, features = x.shape
    stabs = rounds_here * stabs_here
    bf16, f32 = jnp.bfloat16, jnp.float32
    most = max(SPLIT)
    tokens = BLOCK * depth * rounds_here
    pieces = stabs_here // PIECE
    vmem = pl.BlockSpec(memory_space=pltpu.VMEM)
    anywhere = pl.BlockSpec(memory_space=pl.ANY)
    messages = pltpu.VMEM((total, pieces * PIECE, 128), bf16)
    dma = pltpu.SemaphoreType.DMA
    return pl.pallas_call(
        functools.partial(layer_kernel, sizes),
        out_shape=jax.ShapeDtypeStruct(x.shape, bf16),
        in_specs=[anywhere, anywhere, vmem, vmem, vmem, vmem] + [anywhere] * 4,
        out_specs=anywhere,
        scratch_shapes=[
            pltpu.VMEM(x.shape, bf16),
            pltpu.VMEM((depth,) + labels.shape, jnp.int32),
            pltpu.VMEM(space_in.shape, bf16),
            pltpu.VMEM(space_out.shape, bf16),
            pltpu.VMEM(time_in.shape, bf16),
            pltpu.VMEM(time_out.shape, bf16),
            pltpu.VMEM((len(SPLIT), stabs, 128), bf16),
            pltpu.VMEM((rounds_here, stabs_here, 3 * features), bf16),
            pltpu.VMEM((HEADS, stabs, stabs), bf16),
            pltpu.VMEM((stabs, features), bf16),
            pltpu.VMEM((stabs, features), f32),
            messages, messages, messages, messages,
            pltpu.VMEM(x.shape, bf16),
            pltpu.VMEM((most * 128, features), bf16),
            pltpu.VMEM((2 * features, stabs), f32),
            pltpu.VMEM((rounds_here, stabs_here, 3 * features), bf16),
            pltpu.VMEM(x.shape, bf16),
            pltpu.VMEM((most * tokens, 3 * features), bf16),
            pltpu.VMEM((most * (features // PAIR), 2 * tokens, tokens), bf16),
            pltpu.VMEM((most * tokens, features), bf16),
            pltpu.VMEM((most * tokens, features), bf16),
            pltpu.VMEM((most * tokens, 3 * features), bf16),
            pltpu.SemaphoreType.REGULAR,
            dma((4,)), dma, dma, dma, dma,
            dma, dma((len(SPLIT),)), dma, dma((len(SPLIT),)), dma, dma,
        ],
        compiler_params=pltpu.CompilerParams(
            collective_id=1, has_side_effects=True, vmem_limit_bytes=MEGA_VMEM
        ),
        name="whole_layer",
    )(x, labels, near, space_gain, time_gain, readout, space_in, space_out, time_in, time_out)


def near_lists(neighbours, sizes, stabs_here):
    pieces = stabs_here // PIECE
    cut = neighbours.reshape(sizes[1], pieces, PIECE // BLOCK, neighbours.shape[1])
    found = []
    for first, count in spans():
        rows = cut[:, first : first + count].reshape(-1, neighbours.shape[1])
        turned = jnp.pad(rows.T, ((0, 0), (0, 128 - rows.shape[0])), constant_values=-1)
        found.append(turned)
    return jnp.stack(found)


def body(
    round_size,
    stab_size,
    inputs,
    labels,
    neighbours,
    space_in_weights,
    space_out_weights,
    space_gain,
    time_in_weights,
    time_out_weights,
    time_gain,
    readout,
):
    rounds_here, stabs_here, features = inputs.shape
    rounds = rounds_here * round_size
    stabs = stabs_here * stab_size
    copies = stab_size // rounds_here
    assert copies * rounds_here == stab_size
    padded = -(-stabs_here // round_size) * round_size
    part = padded // round_size
    direct = copies == 1 and padded == stabs_here
    both = ("round", "stab")
    space_gain, time_gain, readout = space_gain[None], time_gain[None], readout[None]
    sizes = (round_size, stab_size)
    if (
        copies == 1
        and round_size * BLOCK == PIECE
        and stabs_here == sum(SPLIT) * PIECE
        and rounds * BLOCK == GROUP
        and stab_size * PIECE == GROUP
    ):
        near = near_lists(neighbours, sizes, stabs_here)
        grad = whole_layer(
            sizes, inputs, labels, near, space_gain, time_gain, readout,
            space_in_weights, space_out_weights, time_in_weights, time_out_weights,
        )
        return grad.astype(jnp.float32)

    def to_rounds(tokens):
        if copies > 1:
            tokens = jnp.repeat(tokens, copies, axis=0)
        return lax.all_to_all(tokens, "stab", split_axis=0, concat_axis=1, tiled=True)[0]

    def to_tokens(rows):
        split = rows.reshape(stab_size, stabs_here, features)
        moved = lax.all_to_all(split, "stab", split_axis=0, concat_axis=0, tiled=True)
        return moved[::copies] if copies > 1 else moved

    def pad_stabs(tokens):
        return jnp.pad(tokens, ((0, 0), (0, padded - stabs_here), (0, 0)))

    def to_times(rows):
        if direct:
            return lax.all_to_all(
                rows.reshape(rounds, part, features), both, split_axis=0, concat_axis=0, tiled=True
            )
        tokens = pad_stabs(to_tokens(rows))
        return lax.all_to_all(tokens, "round", split_axis=1, concat_axis=0, tiled=True)

    def from_times(times):
        if direct:
            moved = lax.all_to_all(times, both, split_axis=0, concat_axis=0, tiled=True)
            return moved.reshape(stabs, features)
        tokens = lax.all_to_all(times, "round", split_axis=0, concat_axis=1, tiled=True)
        return to_rounds(tokens[:, :stabs_here])

    here_round, here_stab = lax.axis_index("round"), lax.axis_index("stab")
    if direct:
        first = (here_round * stab_size + here_stab) * part
        chunks = jnp.transpose(labels.reshape(rounds_here, round_size, part), (1, 0, 2))
        sent = jnp.tile(chunks.reshape(round_size, rounds_here * part), (stab_size, 1))
        came = lax.all_to_all(sent, both, split_axis=0, concat_axis=0, tiled=True)
        came = came.reshape(round_size, stab_size, rounds_here, part)
        owner = (here_round * stab_size + here_stab) // round_size
        targets = lax.dynamic_index_in_dim(came, owner, 1, keepdims=False)
        targets = targets.reshape(rounds, part).astype(jnp.float32)
    else:
        first = here_stab * stabs_here + here_round * part
        labels_all = lax.all_gather(labels, both, axis=0, tiled=False)
        labels_all = labels_all.reshape(round_size, stab_size, rounds_here, stabs_here)
        labels_all = jnp.transpose(labels_all, (0, 2, 1, 3)).reshape(rounds, stabs)
        labels_all = jnp.pad(labels_all, ((0, 0), (0, padded)))
        targets = lax.dynamic_slice(labels_all, (0, first), (rounds, part)).astype(jnp.float32)
    slot = jnp.arange(part) + (here_round * part if not direct else 0)
    real = first + jnp.arange(part) < STABS_REAL
    if not direct:
        real = real & (slot < stabs_here)
    side = jnp.stack([targets, jnp.broadcast_to(real.astype(jnp.float32), targets.shape)], axis=-1)

    width = max(1, GROUP // rounds)
    while part % width:
        width -= 1
    groups = part // width
    tokens = width * rounds

    def to_groups(times):
        depth = times.shape[-1]
        split = times.reshape(rounds, groups, width, depth)
        return jnp.transpose(split, (1, 0, 2, 3)).reshape(groups * tokens, depth)

    def from_groups(rows):
        split = rows.reshape(groups, rounds, width, features)
        return jnp.transpose(split, (1, 0, 2, 3)).reshape(rounds, part, features)

    x = to_rounds(inputs)
    after_space, *saved = space_forward(
        x, neighbours, space_gain, space_in_weights, space_out_weights
    )
    times = to_groups(to_times(after_space))
    grad_times = time_both(
        times, to_groups(side), time_gain, readout, time_in_weights, time_out_weights, width, tokens
    )
    grad_space = from_times(from_groups(grad_times))
    grad = space_backward(x, space_gain, grad_space, saved, space_in_weights, space_out_weights)
    return to_tokens(grad).astype(jnp.float32)


def solution(mesh):
    in_specs = (
        P("round", "stab", None),
        P("round", "stab"),
        P(),
        P(),
        P(),
        P(),
        P(),
        P(),
        P(),
        P(),
    )
    out_specs = P("round", "stab", None)
    sized = functools.partial(body, mesh.shape["round"], mesh.shape["stab"])
    return jax.shard_map(sized, mesh=mesh, in_specs=in_specs, out_specs=out_specs, check_vma=False)
```

```python
import functools

import jax
import jax.numpy as jnp
from jax import lax
from jax.experimental import pallas as pl
from jax.experimental.pallas import tpu as pltpu
from jax.sharding import PartitionSpec as P

HEADS = 8
HEAD_DIM = 64
STABS_REAL = 840
BLOCK = 4
PAIR = 2 * HEAD_DIM
CHUNK = 448
BACK_CHUNK = 448
GROUP = 128

EPSILON = 1e-06
MASKED_SCORE = -1e30
FACTOR = HEAD_DIM ** (-0.5)
VMEM_LIMIT = 50 * 1024 * 1024


def dot(first, second):
    return jnp.dot(first, second, preferred_element_type=jnp.float32)


def dot_nt(first, second):
    return lax.dot_general(
        first, second, (((1,), (1,)), ((), ())), preferred_element_type=jnp.float32
    )


def dot_tn(first, second):
    return lax.dot_general(
        first, second, (((0,), (0,)), ((), ())), preferred_element_type=jnp.float32
    )


def inverse_rms(hidden):
    return lax.rsqrt(jnp.mean(hidden * hidden, axis=-1, keepdims=True) + EPSILON)


def norm_back(hidden, inverse, gain, upstream):
    scaled = upstream * gain
    inner = jnp.mean(hidden * scaled, axis=-1, keepdims=True)
    return inverse * scaled - hidden * (inverse * inverse * inverse * inner)


def softmax_rows(scores):
    highest = jnp.max(scores, axis=-1, keepdims=True)
    weights = jnp.exp(scores - highest)
    total = jnp.sum(weights, axis=-1, keepdims=True)
    return (weights * (1.0 / total)).astype(jnp.bfloat16)


def space_forward_kernel(
    x_ref, near_ref, gain_ref, wq_ref, wk_ref, wv_ref, wo_ref,
    h_ref, q_ref, k_ref, v_ref, o_ref, p_ref,
    n_scr, bias_scr, acc_scr,
):
    step = pl.program_id(0)
    stabs = x_ref.shape[0]
    blocks, links = near_ref.shape

    @pl.when(step == 0)
    def _():
        x = x_ref[...].astype(jnp.float32)
        n_scr[...] = (x * inverse_rms(x) * gain_ref[...]).astype(jnp.bfloat16)
        acc_scr[...] = x
        lanes = lax.broadcasted_iota(jnp.int32, (blocks, blocks), 1)
        near = near_ref[...]
        listed = jnp.zeros((blocks, blocks), jnp.float32)
        for link in range(links):
            listed = jnp.where(lanes == near[:, link : link + 1], 1.0, listed)
        owner = lax.broadcasted_iota(jnp.int32, (stabs, blocks), 0) // BLOCK
        column = lax.broadcasted_iota(jnp.int32, (stabs, blocks), 1)
        widen = jnp.where(owner == column, 1.0, 0.0).astype(jnp.bfloat16)
        rows = dot(widen, listed.astype(jnp.bfloat16)).astype(jnp.bfloat16)
        bias_scr[...] = jnp.where(dot_nt(rows, widen) > 0.5, 0.0, MASKED_SCORE)

    n = n_scr[...]
    q_ref[...] = dot(n, wq_ref[...]).astype(jnp.bfloat16)
    k_ref[...] = dot(n, wk_ref[...]).astype(jnp.bfloat16)
    v_ref[...] = dot(n, wv_ref[...]).astype(jnp.bfloat16)
    for head in range(2):
        cols = slice(head * HEAD_DIM, (head + 1) * HEAD_DIM)
        keys = k_ref[:, cols]
        values = v_ref[:, cols]
        for start in range(0, stabs, CHUNK):
            rows = slice(start, start + CHUNK)
            scores = dot_nt(q_ref[rows, cols] * FACTOR, keys) + bias_scr[rows, :]
            weights = softmax_rows(scores)
            p_ref[head, rows, :] = weights
            o_ref[rows, cols] = dot(weights, values).astype(jnp.bfloat16)
    acc_scr[...] += dot(o_ref[...], wo_ref[...])

    @pl.when(step == pl.num_programs(0) - 1)
    def _():
        h_ref[...] = acc_scr[...].astype(jnp.bfloat16)


def space_backward_kernel(
    x_ref, gain_ref, g_ref, q_ref, k_ref, v_ref, o_ref, p_ref,
    wq_ref, wk_ref, wv_ref, wo_ref,
    out_ref,
    gn_scr, go_scr, gs_scr, dq_scr, dk_scr, dv_scr,
):
    step = pl.program_id(0)
    stabs = x_ref.shape[0]
    go = dot_nt(g_ref[...], wo_ref[...]).astype(jnp.bfloat16)
    go_scr[...] = go
    product = go.astype(jnp.float32) * o_ref[...].astype(jnp.float32)
    q_turned = q_ref[...].T
    go_turned = go.T
    for head in range(2):
        cols = slice(head * HEAD_DIM, (head + 1) * HEAD_DIM)
        keys = k_ref[:, cols]
        values = v_ref[:, cols]
        delta = jnp.sum(product[:, cols], axis=-1, keepdims=True)
        for start in range(0, stabs, BACK_CHUNK):
            rows = slice(start, start + BACK_CHUNK)
            grad_weights = dot_nt(go_scr[rows, cols], values)
            weights = p_ref[head, rows, :].astype(jnp.float32)
            grad_scores = (
                weights * ((grad_weights - delta[start : start + BACK_CHUNK]) * FACTOR)
            ).astype(jnp.bfloat16)
            gs_scr[rows, :] = grad_scores
            dq_scr[rows, cols] = dot(grad_scores, keys).astype(jnp.bfloat16)
        dk_scr[cols, :] = dot(q_turned[cols, :], gs_scr[...]).astype(jnp.bfloat16)
        dv_scr[cols, :] = dot(go_turned[cols, :], p_ref[head]).astype(jnp.bfloat16)
    part = (
        dot_nt(dq_scr[...], wq_ref[...])
        + dot_nt(dk_scr[...].T, wk_ref[...])
        + dot_nt(dv_scr[...].T, wv_ref[...])
    )

    @pl.when(step == 0)
    def _():
        gn_scr[...] = part

    @pl.when(step > 0)
    def _():
        gn_scr[...] += part

    @pl.when(step == pl.num_programs(0) - 1)
    def _():
        x = x_ref[...].astype(jnp.float32)
        back = norm_back(x, inverse_rms(x), gain_ref[...], gn_scr[...])
        out_ref[...] = (g_ref[...].astype(jnp.float32) + back).astype(jnp.bfloat16)


def time_kernel(
    width, h_ref, side_ref, gain_ref, readout_ref, win_ref, wout_ref,
    g_ref,
    qkv_scr, p_scr, o_scr, go_scr, d_scr,
):
    total, features = h_ref.shape
    tokens = p_scr.shape[-1]
    groups = total // tokens
    hidden = h_ref[...].astype(jnp.float32)
    inverse = inverse_rms(hidden)
    gain = gain_ref[...]
    normed = (hidden * inverse * gain).astype(jnp.bfloat16)
    qkv_scr[...] = dot(normed, win_ref[...]).astype(jnp.bfloat16)
    left = lax.broadcasted_iota(jnp.int32, (tokens, tokens), 0)
    right = lax.broadcasted_iota(jnp.int32, (tokens, tokens), 1)
    kept = ((left % width) == (right % width)) & (right <= left)
    bias = jnp.where(kept, 0.0, MASKED_SCORE)
    bias = jnp.concatenate([bias, bias], axis=0)

    pairs = features // PAIR
    lanes = lax.broadcasted_iota(jnp.int32, (tokens, PAIR), 1)
    near = lanes < HEAD_DIM

    def part(index, pair):
        start = index * features + pair * PAIR
        return slice(start, start + PAIR)

    def rows_of(group):
        return pl.ds(pl.multiple_of(group * tokens, tokens), tokens)

    def stacked(block):
        empty = jnp.zeros_like(block)
        return jnp.concatenate(
            [jnp.where(near, block, empty), jnp.where(near, empty, block)], axis=0
        )

    def merged(block):
        return jnp.where(near, block[:tokens], block[tokens:]).astype(jnp.bfloat16)

    def ahead(group, carry):
        rows = rows_of(group)
        scores = [
            dot_nt(stacked(qkv_scr[rows, part(0, pair)] * FACTOR), qkv_scr[rows, part(1, pair)])
            for pair in range(pairs)
        ]
        weights = [softmax_rows(score + bias) for score in scores]
        for pair in range(pairs):
            p_scr[group * pairs + pair] = weights[pair]
        outs = [dot(weights[pair], qkv_scr[rows, part(2, pair)]) for pair in range(pairs)]
        for pair in range(pairs):
            o_scr[rows, part(0, pair)] = merged(outs[pair])
        return carry

    lax.fori_loop(0, groups, ahead, 0)
    readout = readout_ref[...]
    after = hidden + dot(o_scr[...], wout_ref[...])
    logits = jnp.sum(after * readout, axis=-1, keepdims=True)
    side = side_ref[...]
    grad_logits = (jax.nn.sigmoid(logits) - side[:, 0:1]) * side[:, 1:2]
    grad_after = grad_logits * readout
    go_scr[...] = dot_nt(grad_after.astype(jnp.bfloat16), wout_ref[...]).astype(jnp.bfloat16)

    def behind(group, carry):
        rows = rows_of(group)
        span = range(pairs)
        upstream = [stacked(go_scr[rows, part(0, pair)]) for pair in span]
        products = [dot_nt(upstream[pair], qkv_scr[rows, part(2, pair)]) for pair in span]
        weights = [p_scr[group * pairs + pair] for pair in span]
        grad_scores = []
        for pair in span:
            attended = o_scr[rows, part(0, pair)].astype(jnp.float32)
            attended = jnp.concatenate([attended, attended], axis=0)
            delta = jnp.sum(
                upstream[pair].astype(jnp.float32) * attended, axis=-1, keepdims=True
            )
            grad_scores.append(
                (weights[pair].astype(jnp.float32) * ((products[pair] - delta) * FACTOR)).astype(
                    jnp.bfloat16
                )
            )
        queries = [dot(grad_scores[pair], qkv_scr[rows, part(1, pair)]) for pair in span]
        keys = [dot_tn(grad_scores[pair], stacked(qkv_scr[rows, part(0, pair)])) for pair in span]
        values = [dot_tn(weights[pair], upstream[pair]) for pair in span]
        for pair in span:
            d_scr[rows, part(0, pair)] = merged(queries[pair])
            d_scr[rows, part(1, pair)] = keys[pair].astype(jnp.bfloat16)
            d_scr[rows, part(2, pair)] = values[pair].astype(jnp.bfloat16)
        return carry

    lax.fori_loop(0, groups, behind, 0)
    grad_normed = dot_nt(d_scr[...], win_ref[...])
    hidden = h_ref[...].astype(jnp.float32)
    back = norm_back(hidden, inverse, gain, grad_normed)
    g_ref[...] = (grad_logits * readout + back).astype(jnp.bfloat16)


def whole(*shape):
    return pl.BlockSpec(shape, lambda step: (0,) * len(shape))


def weight_specs(features):
    pairs = features // PAIR
    return [
        pl.BlockSpec((features, PAIR), lambda step: (0, step)),
        pl.BlockSpec((features, PAIR), lambda step: (0, pairs + step)),
        pl.BlockSpec((features, PAIR), lambda step: (0, 2 * pairs + step)),
        pl.BlockSpec((PAIR, features), lambda step: (step, 0)),
    ]


def space_forward(x, neighbours, gain, w_in, w_out):
    stabs, features = x.shape
    pairs = features // PAIR
    column = pl.BlockSpec((stabs, PAIR), lambda step: (0, step))
    rows = jax.ShapeDtypeStruct((stabs, features), jnp.bfloat16)
    square = pl.BlockSpec((2, stabs, stabs), lambda step: (step, 0, 0))
    return pl.pallas_call(
        space_forward_kernel,
        grid=(pairs,),
        in_specs=[whole(stabs, features), whole(*neighbours.shape), whole(1, features)]
        + weight_specs(features),
        out_specs=[whole(stabs, features), column, column, column, column, square],
        out_shape=[
            rows, rows, rows, rows, rows,
            jax.ShapeDtypeStruct((2 * pairs, stabs, stabs), jnp.bfloat16),
        ],
        scratch_shapes=[
            pltpu.VMEM((stabs, features), jnp.bfloat16),
            pltpu.VMEM((stabs, stabs), jnp.float32),
            pltpu.VMEM((stabs, features), jnp.float32),
        ],
        compiler_params=pltpu.CompilerParams(vmem_limit_bytes=VMEM_LIMIT),
        name="space_forward",
    )(x, neighbours, gain, w_in, w_in, w_in, w_out)


def space_backward(x, gain, grad, saved, w_in, w_out):
    stabs, features = x.shape
    pairs = features // PAIR
    column = pl.BlockSpec((stabs, PAIR), lambda step: (0, step))
    square = pl.BlockSpec((2, stabs, stabs), lambda step: (step, 0, 0))
    return pl.pallas_call(
        space_backward_kernel,
        grid=(pairs,),
        in_specs=[whole(stabs, features), whole(1, features), whole(stabs, features)]
        + [column] * 4
        + [square]
        + weight_specs(features),
        out_specs=whole(stabs, features),
        out_shape=jax.ShapeDtypeStruct((stabs, features), jnp.bfloat16),
        scratch_shapes=[
            pltpu.VMEM((stabs, features), jnp.float32),
            pltpu.VMEM((stabs, PAIR), jnp.bfloat16),
            pltpu.VMEM((stabs, stabs), jnp.bfloat16),
            pltpu.VMEM((stabs, PAIR), jnp.bfloat16),
            pltpu.VMEM((PAIR, stabs), jnp.bfloat16),
            pltpu.VMEM((PAIR, stabs), jnp.bfloat16),
        ],
        compiler_params=pltpu.CompilerParams(vmem_limit_bytes=VMEM_LIMIT),
        name="space_backward",
    )(x, gain, grad, *saved, w_in, w_in, w_in, w_out)


def time_both(hidden, side, gain, readout, w_in, w_out, width, tokens):
    total, features = hidden.shape
    return pl.pallas_call(
        functools.partial(time_kernel, width),
        out_shape=jax.ShapeDtypeStruct((total, features), jnp.bfloat16),
        scratch_shapes=[
            pltpu.VMEM((total, 3 * features), jnp.bfloat16),
            pltpu.VMEM((total // tokens * (features // PAIR), 2 * tokens, tokens), jnp.bfloat16),
            pltpu.VMEM((total, features), jnp.bfloat16),
            pltpu.VMEM((total, features), jnp.bfloat16),
            pltpu.VMEM((total, 3 * features), jnp.bfloat16),
        ],
        compiler_params=pltpu.CompilerParams(vmem_limit_bytes=VMEM_LIMIT),
        name="time_both",
    )(hidden, side, gain, readout, w_in, w_out)


PIECE = 16
SPLIT = (2, 3, 2)
PARTS = (2, 2, 3)
MEGA_VMEM = 60 * 1024 * 1024


def spans(counts=SPLIT):
    first = 0
    found = []
    for count in counts:
        found.append((first, count))
        first += count
    return found


def half_turn(tiles):
    return pltpu.roll(tiles, 4, 1)


def pack_messages(rows):
    tiles = rows.shape[0] // 8
    cut = rows.reshape(tiles, 8, rows.shape[1])
    upper = lax.broadcasted_iota(jnp.int32, (tiles, 8, 128), 1) < 4
    parts = [cut[:, :, at : at + 128] for at in range(0, rows.shape[1], 128)]
    turned = [half_turn(part) for part in parts]
    low = [jnp.where(upper, parts[at], turned[at + 1]) for at in (0, 2)]
    high = [jnp.where(upper, turned[at], parts[at + 1]) for at in (0, 2)]
    low = jnp.concatenate(low, axis=1)[:, None]
    high = jnp.concatenate(high, axis=1)[:, None]
    return jnp.concatenate([low, high], axis=1).reshape(2 * tiles, 16, 128)


def unpack_messages(messages):
    tiles = messages.shape[0] // 2
    cut = messages.astype(jnp.float32).reshape(tiles, 2, 2, 8, 128)
    upper = lax.broadcasted_iota(jnp.int32, (tiles, 8, 128), 1) < 4
    found = []
    for part in range(2):
        low, high = cut[:, 0, part], cut[:, 1, part]
        found.append(jnp.where(upper, low, half_turn(high)))
        found.append(jnp.where(upper, half_turn(low), high))
    return jnp.concatenate(found, axis=2).reshape(8 * tiles, 512)


def layer_kernel(
    sizes,
    x_in, labels_in, near_ref, space_gain_ref, time_gain_ref, readout_ref,
    space_in_hbm, space_out_hbm, time_in_hbm, time_out_hbm,
    out_ref,
    x_scr, lab_scr, wsi, wso, wti, wto,
    bias_scr, qkv_scr, p_scr, o_scr, inv_scr,
    send_h, recv_h, send_g, recv_g, g_scr, go_scr, dq_scr, acc_scr, d_scr, out_scr,
    tqkv, tp, to, tgo, td,
    weight_sem, x_send, x_recv, lab_send, lab_recv,
    h_send, h_recv, g_send, g_recv, out_send, out_recv,
):
    depth, inner = sizes
    total = depth * inner
    here_z, here_s = lax.axis_index("round"), lax.axis_index("stab")
    here = here_z * inner + here_s
    here_chip = here_s // 2
    here_core = lax.rem(here_s, 2)
    mesh_ids = pl.DeviceIdType.MESH
    pieces_here, _, _, features = x_scr.shape
    rounds_here, stabs_here = labels_in.shape
    stabs = rounds_here * stabs_here
    rounds = depth * rounds_here
    pairs = features // PAIR

    def device(index):
        return (index // inner, lax.rem(index, inner))

    barrier = pltpu.get_barrier_semaphore()

    def greet(step, carry):
        pl.semaphore_signal(
            barrier, inc=1, device_id=device(lax.rem(here + step, total)), device_id_type=mesh_ids
        )
        return carry

    lax.fori_loop(1, total, greet, 0)
    weights = [
        pltpu.make_async_copy(source, target, weight_sem.at[index])
        for index, (source, target) in enumerate(
            [(space_in_hbm, wsi), (space_out_hbm, wso), (time_in_hbm, wti), (time_out_hbm, wto)]
        )
    ]
    for copy in weights:
        copy.start()
    pl.semaphore_wait(barrier, total - 1)

    chips = inner // 2

    def send_x(peer):
        pltpu.make_async_remote_copy(
            src_ref=x_in.at[peer], dst_ref=x_scr.at[:, here_s],
            send_sem=x_send, recv_sem=x_recv.at[here_s],
            device_id=(here_z, peer), device_id_type=mesh_ids,
        ).start()

    def send_x_chip(step, carry):
        chip = lax.rem(here_chip + step, chips)
        send_x(2 * chip)
        send_x(2 * chip + 1)
        return carry

    lax.fori_loop(1, chips, send_x_chip, 0)
    send_x(2 * here_chip + 1 - here_core)
    pltpu.make_async_copy(x_in.at[here_s], x_scr.at[:, here_s], x_recv.at[here_s]).start()

    def send_labels(step, carry):
        peer = lax.rem(here_z + step, depth)
        pltpu.make_async_remote_copy(
            src_ref=labels_in, dst_ref=lab_scr.at[here_z],
            send_sem=lab_send, recv_sem=lab_recv,
            device_id=(peer, here_s), device_id_type=mesh_ids,
        ).start()
        return carry

    lax.fori_loop(1, depth, send_labels, 0)
    pltpu.make_async_copy(labels_in, lab_scr.at[here_z], lab_recv).start()

    blocks = stabs // BLOCK
    piece_blocks = PIECE // BLOCK
    round_blocks = stabs_here // BLOCK
    key = lax.broadcasted_iota(jnp.int32, (stabs, blocks), 0)
    owner = (
        (key // PIECE) % inner * round_blocks
        + key // (PIECE * inner) * piece_blocks
        + key % PIECE // BLOCK
    )
    column = lax.broadcasted_iota(jnp.int32, (stabs, blocks), 1)
    widen = jnp.where(owner == column, 1.0, 0.0).astype(jnp.bfloat16)
    near = near_ref[...]
    key_block = lax.broadcasted_iota(jnp.int32, (blocks, blocks), 0)
    listed = jnp.zeros((blocks, blocks), jnp.float32)
    for link in range(near.shape[0]):
        listed = jnp.where(key_block == near[link : link + 1, :], 1.0, listed)
    listed = listed.astype(jnp.bfloat16)
    slot = lax.broadcasted_iota(jnp.int32, (128, blocks), 0)
    slot_column = lax.broadcasted_iota(jnp.int32, (128, blocks), 1)
    for index, (first, count) in enumerate(spans()):
        source = (
            (slot // piece_blocks) % inner * round_blocks
            + (first + slot // (piece_blocks * inner)) * piece_blocks
            + slot % piece_blocks
        )
        held = (source == slot_column) & (slot < count * piece_blocks * inner)
        mine = dot_nt(jnp.where(held, 1.0, 0.0).astype(jnp.bfloat16), listed).astype(jnp.bfloat16)
        spread = dot_nt(widen, mine)
        bias_scr[index] = jnp.where(spread > 0.5, 0.0, MASKED_SCORE).astype(jnp.bfloat16)

    near_lanes = lax.broadcasted_iota(jnp.int32, (1, PAIR), 1) < HEAD_DIM
    head_masks = [
        near_lanes.astype(jnp.float32).astype(jnp.bfloat16),
        1 - near_lanes.astype(jnp.float32).astype(jnp.bfloat16),
    ]

    weights[0].wait()

    def project(step, carry):
        chip = lax.rem(here_chip + chips - step, chips)
        for core in range(2):
            place = x_scr.at[:, 2 * chip + core]
            pltpu.make_async_copy(place, place, x_recv.at[2 * chip + core]).wait()
        both = pl.ds(2 * chip, 2)
        rows = pieces_here * 2 * PIECE
        x = x_scr[:, both].reshape(rows, features).astype(jnp.float32)
        normed = (x * inverse_rms(x) * space_gain_ref[...]).astype(jnp.bfloat16)
        made = dot(normed, wsi[...]).astype(jnp.bfloat16)
        qkv_scr[:, both] = made.reshape(pieces_here, 2, PIECE, 3 * features)
        return carry

    lax.fori_loop(0, chips, project, 0)
    weights[1].wait()

    def pair_cols(pair, third):
        return pl.ds(third * features + pair * PAIR, PAIR)

    def all_rows(pair, third):
        return qkv_scr[:, :, :, pair_cols(pair, third)].reshape(stabs, PAIR)

    def send_span(first, count, source, target, send_sem, recv_sem):
        rows = pl.ds(first * PIECE, count * PIECE)

        def send(step, carry):
            peer = lax.rem(here + step, total)
            pltpu.make_async_remote_copy(
                src_ref=source.at[peer, rows], dst_ref=target.at[here, rows],
                send_sem=send_sem, recv_sem=recv_sem,
                device_id=device(peer), device_id_type=mesh_ids,
            ).start()
            return carry

        lax.fori_loop(1, total, send, 0)
        pltpu.make_async_copy(source.at[here, rows], target.at[here, rows], recv_sem).start()

    def wait_span(first, count, target, recv_sem):
        whole_span = target.at[:, pl.ds(first * PIECE, count * PIECE)]
        pltpu.make_async_copy(whole_span, whole_span, recv_sem).wait()

    for index, (first, count) in enumerate(spans()):
        height = count * 128
        rows = slice(first, first + count)
        flat = slice(first * 128, (first + count) * 128)
        row_block = lax.broadcasted_iota(jnp.int32, (height, 128), 0) // BLOCK
        lane = lax.broadcasted_iota(jnp.int32, (height, 128), 1)
        onehot = jnp.where(row_block == lane, 1.0, 0.0).astype(jnp.bfloat16)

        def ahead(pair, carry, rows=rows, flat=flat, height=height, onehot=onehot, index=index):
            queries = qkv_scr[rows, :, :, pair_cols(pair, 0)].reshape(height, PAIR) * FACTOR
            keys = jnp.concatenate([all_rows(pair, 1), bias_scr[index]], axis=1)
            values = all_rows(pair, 2)
            out = None
            for half in range(2):
                mask = head_masks[half]
                scores = dot_nt(jnp.concatenate([queries * mask, onehot], axis=1), keys)
                highest = jnp.max(scores, axis=-1, keepdims=True)
                expd = jnp.exp(scores - highest).astype(jnp.bfloat16)
                p_scr[pair * 2 + half, flat, :] = expd
                ones = jnp.broadcast_to(mask, (stabs, PAIR))
                part = dot(expd, jnp.concatenate([values * mask, ones], axis=1))
                out = part if out is None else out + part
            inverse = 1.0 / out[:, PAIR:]
            inv_scr[flat, pair_cols(pair, 0)] = inverse
            o_scr[flat, pair_cols(pair, 0)] = (out[:, :PAIR] * inverse).astype(jnp.bfloat16)
            return carry

        for pair in range(pairs):
            ahead(pair, 0)
        hidden = x_scr[rows].reshape(height, features).astype(jnp.float32)
        hidden = hidden + dot(o_scr[flat, :], wso[...])
        for piece in range(count):
            packed = pack_messages(hidden[piece * 128 : (piece + 1) * 128]).astype(jnp.bfloat16)
            packed = packed.reshape(inner, depth, 16, 128)
            at = slice((first + piece) * PIECE, (first + piece + 1) * PIECE)
            for z in range(depth):
                send_h[z * inner : (z + 1) * inner, at, :] = packed[:, z]
        send_span(first, count, send_h, recv_h, h_send, h_recv.at[index])

    tokens = BLOCK * rounds
    left = lax.broadcasted_iota(jnp.int32, (tokens, tokens), 0)
    right = lax.broadcasted_iota(jnp.int32, (tokens, tokens), 1)
    kept = ((left % BLOCK) == (right % BLOCK)) & (right <= left)
    causal = jnp.where(kept, 0.0, MASKED_SCORE)
    causal = jnp.concatenate([causal, causal], axis=0)
    lanes = lax.broadcasted_iota(jnp.int32, (tokens, PAIR), 1)
    is_near = lanes < HEAD_DIM

    def stacked(block):
        empty = jnp.zeros_like(block)
        return jnp.concatenate(
            [jnp.where(is_near, block, empty), jnp.where(is_near, empty, block)], axis=0
        )

    def merged(block):
        return jnp.where(is_near, block[:tokens], block[tokens:]).astype(jnp.bfloat16)

    pltpu.make_async_copy(lab_scr, lab_scr, lab_recv).wait()
    token_round = lax.broadcasted_iota(jnp.int32, (tokens, rounds), 0) // BLOCK
    which_round = lax.broadcasted_iota(jnp.int32, (tokens, rounds), 1)
    pick = jnp.where(token_round == which_round, 1.0, 0.0).astype(jnp.bfloat16)
    labels = lab_scr[...].reshape(rounds, stabs_here).astype(jnp.float32).astype(jnp.bfloat16)
    token_labels = dot(pick, labels)
    stab_lane = lax.broadcasted_iota(jnp.int32, (tokens, stabs_here), 1)
    token_slot = lax.broadcasted_iota(jnp.int32, (tokens, stabs_here), 0) % BLOCK
    slot_column = lax.broadcasted_iota(jnp.int32, (tokens, 1), 0) % BLOCK
    weights[2].wait()
    weights[3].wait()

    for index, (first, count) in enumerate(spans()):
        wait_span(first, count, recv_h, h_recv.at[index])
        height = count * tokens
        pieces = range(count)
        found = [
            unpack_messages(recv_h[:, (first + piece) * PIECE : (first + piece + 1) * PIECE, :])
            for piece in pieces
        ]
        hidden = jnp.concatenate(found, axis=0) if count > 1 else found[0]
        inverse = inverse_rms(hidden)
        gain = time_gain_ref[...]
        normed = (hidden * inverse * gain).astype(jnp.bfloat16)
        tqkv[:height, :] = dot(normed, wti[...]).astype(jnp.bfloat16)
        jobs = [(piece, pair) for piece in pieces for pair in range(pairs)]

        def part(third, pair):
            return slice(third * features + pair * PAIR, third * features + (pair + 1) * PAIR)

        def span_of(piece):
            return slice(piece * tokens, (piece + 1) * tokens)

        scores = [
            dot_nt(stacked(tqkv[span_of(i), part(0, p)] * FACTOR), tqkv[span_of(i), part(1, p)])
            for i, p in jobs
        ]
        probs = [softmax_rows(score + causal) for score in scores]
        for job, (i, p) in enumerate(jobs):
            tp[job] = probs[job]
        outs = [dot(probs[job], tqkv[span_of(i), part(2, p)]) for job, (i, p) in enumerate(jobs)]
        for job, (i, p) in enumerate(jobs):
            to[span_of(i), part(0, p)] = merged(outs[job])
        readout = readout_ref[...]
        after = hidden + dot(to[:height, :], wto[...])
        logits = jnp.sum(after * readout, axis=-1, keepdims=True)
        targets, real = [], []
        for piece in pieces:
            at = (first + piece) * PIECE + here_z * BLOCK
            chosen = jnp.where(stab_lane == at + token_slot, token_labels, 0.0)
            targets.append(jnp.sum(chosen, axis=-1, keepdims=True))
            where = here_s * stabs_here + at + slot_column
            real.append(jnp.where(where < STABS_REAL, 1.0, 0.0))
        targets = jnp.concatenate(targets, axis=0) if count > 1 else targets[0]
        real = jnp.concatenate(real, axis=0) if count > 1 else real[0]
        grad_logits = (jax.nn.sigmoid(logits) - targets) * real
        grad_after = grad_logits * readout
        tgo[:height, :] = dot_nt(grad_after.astype(jnp.bfloat16), wto[...]).astype(jnp.bfloat16)

        upstream = [stacked(tgo[span_of(i), part(0, p)]) for i, p in jobs]
        products = [
            dot_nt(upstream[job], tqkv[span_of(i), part(2, p)]) for job, (i, p) in enumerate(jobs)
        ]
        grads = []
        for job, (i, p) in enumerate(jobs):
            attended = to[span_of(i), part(0, p)].astype(jnp.float32)
            attended = jnp.concatenate([attended, attended], axis=0)
            delta = jnp.sum(
                upstream[job].astype(jnp.float32) * attended, axis=-1, keepdims=True
            )
            grads.append(
                (tp[job].astype(jnp.float32) * ((products[job] - delta) * FACTOR)).astype(
                    jnp.bfloat16
                )
            )
        for job, (i, p) in enumerate(jobs):
            td[span_of(i), part(0, p)] = merged(dot(grads[job], tqkv[span_of(i), part(1, p)]))
            keys = dot_tn(grads[job], stacked(tqkv[span_of(i), part(0, p)]))
            td[span_of(i), part(1, p)] = keys.astype(jnp.bfloat16)
            td[span_of(i), part(2, p)] = dot_tn(tp[job], upstream[job]).astype(jnp.bfloat16)
        grad_normed = dot_nt(td[:height, :], wti[...])
        grad_hidden = grad_after + norm_back(hidden, inverse, gain, grad_normed)
        for piece in pieces:
            packed = pack_messages(grad_hidden[span_of(piece)]).astype(jnp.bfloat16)
            send_g[:, (first + piece) * PIECE : (first + piece + 1) * PIECE, :] = packed
        send_span(first, count, send_g, recv_g, g_send, g_recv.at[index])

    def finish(first, count, recv_sem):
        rows = slice(first, first + count)
        flat = slice(first * 128, (first + count) * 128)
        for step in range(2 * pairs):
            block = acc_scr[step * PAIR : (step + 1) * PAIR, flat].astype(jnp.bfloat16)
            start = features + step * PAIR
            d_scr[rows, :, :, start : start + PAIR] = block.T.reshape(count, inner, PIECE, PAIR)
        grad_normed = dot_nt(d_scr[rows].reshape(count * 128, 3 * features), wsi[...])
        x = x_scr[rows].reshape(count * 128, features).astype(jnp.float32)
        back = norm_back(x, inverse_rms(x), space_gain_ref[...], grad_normed)
        grad = g_scr[rows].reshape(count * 128, features).astype(jnp.float32) + back
        out_scr[rows] = grad.astype(jnp.bfloat16).reshape(count, inner, PIECE, features)
        part = pl.ds(first, count)

        def send_out(step, carry):
            peer = lax.rem(here_s + step, inner)
            pltpu.make_async_remote_copy(
                src_ref=out_scr.at[part, peer], dst_ref=out_ref.at[here_s, part],
                send_sem=out_send, recv_sem=recv_sem,
                device_id=(here_z, peer), device_id_type=mesh_ids,
            ).start()
            return carry

        lax.fori_loop(1, inner, send_out, 0)
        pltpu.make_async_copy(out_scr.at[part, here_s], out_ref.at[here_s, part], recv_sem).start()

    for index, (first, count) in enumerate(spans()):
        wait_span(first, count, recv_g, g_recv.at[index])
        height = count * 128
        rows = slice(first, first + count)
        flat = slice(first * 128, (first + count) * 128)
        for piece in range(count):
            at = slice((first + piece) * PIECE, (first + piece + 1) * PIECE)
            cut = jnp.concatenate(
                [recv_g[z * inner : (z + 1) * inner, at, :][:, None] for z in range(depth)], axis=1
            )
            grad = unpack_messages(cut.reshape(total, 16, 128)).astype(jnp.bfloat16)
            g_scr[first + piece] = grad.reshape(inner, PIECE, features)
        grad = g_scr[rows].reshape(height, features)
        go_scr[:height, :] = dot_nt(grad, wso[...]).astype(jnp.bfloat16)
        lane = lax.broadcasted_iota(jnp.int32, (height, PAIR), 1)

        def behind(pair, key_first, key_count):
            cols = pair_cols(pair, 0)
            key_rows = slice(key_first * 128, (key_first + key_count) * 128)
            queries = qkv_scr[rows, :, :, cols].reshape(height, PAIR) * FACTOR
            keys, values = all_rows(pair, 1)[key_rows], all_rows(pair, 2)[key_rows]
            scaled = (go_scr[:height, cols].astype(jnp.float32) * inv_scr[flat, cols]).astype(
                jnp.bfloat16
            )
            product = scaled.astype(jnp.float32) * o_scr[flat, cols].astype(jnp.float32)
            queries_turned, scaled_turned = queries.T, scaled.T
            ones = jnp.ones((key_count * 128, PAIR), jnp.bfloat16)
            values = jnp.concatenate([values, ones], axis=1)
            grad_queries = None
            for half in range(2):
                mask = head_masks[half]
                own = (lane < HEAD_DIM) if half == 0 else (lane >= HEAD_DIM)
                delta = jnp.sum(jnp.where(own, product, 0.0), axis=-1, keepdims=True)
                coarse = delta.astype(jnp.bfloat16).astype(jnp.float32)
                extra = jnp.where(lane == 0, -coarse, jnp.where(lane == 1, coarse - delta, 0.0))
                joined = jnp.concatenate([scaled * mask, extra.astype(jnp.bfloat16)], axis=1)
                grad_weights = dot_nt(joined, values)
                expd = p_scr[pair * 2 + half, flat, key_rows]
                grad_scores = (expd.astype(jnp.float32) * grad_weights).astype(jnp.bfloat16)
                part = dot(grad_scores, keys * mask)
                grad_queries = part if grad_queries is None else grad_queries + part
                turned = slice(half * HEAD_DIM, (half + 1) * HEAD_DIM)
                for kind, turned_rows, square in (
                    (0, queries_turned, grad_scores), (1, scaled_turned, expd),
                ):
                    start = kind * features + pair * PAIR + half * HEAD_DIM
                    into = slice(start, start + HEAD_DIM)
                    made = dot(turned_rows[turned, :], square)
                    if index == 0:
                        acc_scr[into, key_rows] = made
                    else:
                        acc_scr[into, key_rows] += made
            if key_first > 0:
                grad_queries = grad_queries + dq_scr[:height, cols]
            if key_first + key_count < pieces_here:
                dq_scr[:height, cols] = grad_queries
            else:
                made = (grad_queries * FACTOR).astype(jnp.bfloat16)
                d_scr[rows, :, :, cols] = made.reshape(count, inner, PIECE, PAIR)

        last = index == len(SPLIT) - 1
        parts = spans(PARTS) if last else [(0, pieces_here)]
        for part_index, (key_first, key_count) in enumerate(parts):
            for pair in range(pairs):
                behind(pair, key_first, key_count)
            if last:
                finish(key_first, key_count, out_recv.at[part_index])

    for index, (key_first, key_count) in enumerate(spans(PARTS)):
        landed = out_ref.at[:, pl.ds(key_first, key_count)]
        pltpu.make_async_copy(landed, landed, out_recv.at[index]).wait()

    def drain(buffer, sem):
        some = buffer.at[pl.ds(0, buffer.shape[0] - 1)]
        pltpu.make_async_copy(some, some, sem).wait()

    drain(lab_scr, lab_send)
    drain(send_h, h_send)
    drain(send_g, g_send)
    some = out_ref.at[pl.ds(0, inner - 1)]
    pltpu.make_async_copy(some, some, x_send).wait()
    pltpu.make_async_copy(some, some, out_send).wait()


def whole_layer(
    sizes, x, labels, near, space_gain, time_gain, readout, space_in, space_out, time_in, time_out
):
    depth, inner = sizes
    total = depth * inner
    rounds_here, stabs_here, features = x.shape
    sent = (rounds_here, stabs_here // PIECE, PIECE, features)
    tiles = (stabs_here // PIECE, inner, PIECE)
    stabs = rounds_here * stabs_here
    bf16, f32 = jnp.bfloat16, jnp.float32
    most = max(SPLIT)
    tokens = BLOCK * depth * rounds_here
    pieces = stabs_here // PIECE
    vmem = pl.BlockSpec(memory_space=pltpu.VMEM)
    anywhere = pl.BlockSpec(memory_space=pl.ANY)
    messages = pltpu.VMEM((total, pieces * PIECE, 128), bf16)
    dma = pltpu.SemaphoreType.DMA
    grad = pl.pallas_call(
        functools.partial(layer_kernel, sizes),
        out_shape=jax.ShapeDtypeStruct(sent, bf16),
        in_specs=[anywhere, anywhere, vmem, vmem, vmem, vmem] + [anywhere] * 4,
        out_specs=anywhere,
        scratch_shapes=[
            pltpu.VMEM(tiles + (features,), bf16),
            pltpu.VMEM((depth,) + labels.shape, jnp.int32),
            pltpu.VMEM(space_in.shape, bf16),
            pltpu.VMEM(space_out.shape, bf16),
            pltpu.VMEM(time_in.shape, bf16),
            pltpu.VMEM(time_out.shape, bf16),
            pltpu.VMEM((len(SPLIT), stabs, 128), bf16),
            pltpu.VMEM(tiles + (3 * features,), bf16),
            pltpu.VMEM((HEADS, stabs, stabs), bf16),
            pltpu.VMEM((stabs, features), bf16),
            pltpu.VMEM((stabs, features), f32),
            messages, messages, messages, messages,
            pltpu.VMEM(tiles + (features,), bf16),
            pltpu.VMEM((most * 128, features), bf16),
            pltpu.VMEM((SPLIT[-1] * 128, features), f32),
            pltpu.VMEM((2 * features, stabs), f32),
            pltpu.VMEM(tiles + (3 * features,), bf16),
            pltpu.VMEM(tiles + (features,), bf16),
            pltpu.VMEM((most * tokens, 3 * features), bf16),
            pltpu.VMEM((most * (features // PAIR), 2 * tokens, tokens), bf16),
            pltpu.VMEM((most * tokens, features), bf16),
            pltpu.VMEM((most * tokens, features), bf16),
            pltpu.VMEM((most * tokens, 3 * features), bf16),
            dma((4,)), dma, dma((inner,)), dma, dma,
            dma, dma((len(SPLIT),)), dma, dma((len(SPLIT),)), dma, dma((len(PARTS),)),
        ],
        compiler_params=pltpu.CompilerParams(
            collective_id=1, has_side_effects=True, vmem_limit_bytes=MEGA_VMEM
        ),
        name="whole_layer",
    )(x.reshape(sent), labels, near, space_gain, time_gain, readout, space_in, space_out, time_in, time_out)
    return grad.reshape(x.shape)


def body(
    round_size,
    stab_size,
    inputs,
    labels,
    neighbours,
    space_in_weights,
    space_out_weights,
    space_gain,
    time_in_weights,
    time_out_weights,
    time_gain,
    readout,
):
    rounds_here, stabs_here, features = inputs.shape
    rounds = rounds_here * round_size
    stabs = stabs_here * stab_size
    copies = stab_size // rounds_here
    assert copies * rounds_here == stab_size
    padded = -(-stabs_here // round_size) * round_size
    part = padded // round_size
    direct = copies == 1 and padded == stabs_here
    both = ("round", "stab")
    space_gain, time_gain, readout = space_gain[None], time_gain[None], readout[None]
    sizes = (round_size, stab_size)
    if (
        copies == 1
        and round_size * BLOCK == PIECE
        and stabs_here == sum(SPLIT) * PIECE
        and rounds * BLOCK == GROUP
        and stab_size * PIECE == GROUP
    ):
        grad = whole_layer(
            sizes, inputs, labels, neighbours.T, space_gain, time_gain, readout,
            space_in_weights, space_out_weights, time_in_weights, time_out_weights,
        )
        return grad.astype(jnp.float32)

    def to_rounds(tokens):
        if copies > 1:
            tokens = jnp.repeat(tokens, copies, axis=0)
        return lax.all_to_all(tokens, "stab", split_axis=0, concat_axis=1, tiled=True)[0]

    def to_tokens(rows):
        split = rows.reshape(stab_size, stabs_here, features)
        moved = lax.all_to_all(split, "stab", split_axis=0, concat_axis=0, tiled=True)
        return moved[::copies] if copies > 1 else moved

    def pad_stabs(tokens):
        return jnp.pad(tokens, ((0, 0), (0, padded - stabs_here), (0, 0)))

    def to_times(rows):
        if direct:
            return lax.all_to_all(
                rows.reshape(rounds, part, features), both, split_axis=0, concat_axis=0, tiled=True
            )
        tokens = pad_stabs(to_tokens(rows))
        return lax.all_to_all(tokens, "round", split_axis=1, concat_axis=0, tiled=True)

    def from_times(times):
        if direct:
            moved = lax.all_to_all(times, both, split_axis=0, concat_axis=0, tiled=True)
            return moved.reshape(stabs, features)
        tokens = lax.all_to_all(times, "round", split_axis=0, concat_axis=1, tiled=True)
        return to_rounds(tokens[:, :stabs_here])

    here_round, here_stab = lax.axis_index("round"), lax.axis_index("stab")
    if direct:
        first = (here_round * stab_size + here_stab) * part
        chunks = jnp.transpose(labels.reshape(rounds_here, round_size, part), (1, 0, 2))
        sent = jnp.tile(chunks.reshape(round_size, rounds_here * part), (stab_size, 1))
        came = lax.all_to_all(sent, both, split_axis=0, concat_axis=0, tiled=True)
        came = came.reshape(round_size, stab_size, rounds_here, part)
        owner = (here_round * stab_size + here_stab) // round_size
        targets = lax.dynamic_index_in_dim(came, owner, 1, keepdims=False)
        targets = targets.reshape(rounds, part).astype(jnp.float32)
    else:
        first = here_stab * stabs_here + here_round * part
        labels_all = lax.all_gather(labels, both, axis=0, tiled=False)
        labels_all = labels_all.reshape(round_size, stab_size, rounds_here, stabs_here)
        labels_all = jnp.transpose(labels_all, (0, 2, 1, 3)).reshape(rounds, stabs)
        labels_all = jnp.pad(labels_all, ((0, 0), (0, padded)))
        targets = lax.dynamic_slice(labels_all, (0, first), (rounds, part)).astype(jnp.float32)
    slot = jnp.arange(part) + (here_round * part if not direct else 0)
    real = first + jnp.arange(part) < STABS_REAL
    if not direct:
        real = real & (slot < stabs_here)
    side = jnp.stack([targets, jnp.broadcast_to(real.astype(jnp.float32), targets.shape)], axis=-1)

    width = max(1, GROUP // rounds)
    while part % width:
        width -= 1
    groups = part // width
    tokens = width * rounds

    def to_groups(times):
        depth = times.shape[-1]
        split = times.reshape(rounds, groups, width, depth)
        return jnp.transpose(split, (1, 0, 2, 3)).reshape(groups * tokens, depth)

    def from_groups(rows):
        split = rows.reshape(groups, rounds, width, features)
        return jnp.transpose(split, (1, 0, 2, 3)).reshape(rounds, part, features)

    x = to_rounds(inputs)
    after_space, *saved = space_forward(
        x, neighbours, space_gain, space_in_weights, space_out_weights
    )
    times = to_groups(to_times(after_space))
    grad_times = time_both(
        times, to_groups(side), time_gain, readout, time_in_weights, time_out_weights, width, tokens
    )
    grad_space = from_times(from_groups(grad_times))
    grad = space_backward(x, space_gain, grad_space, saved, space_in_weights, space_out_weights)
    return to_tokens(grad).astype(jnp.float32)


def solution(mesh):
    in_specs = (
        P("round", "stab", None),
        P("round", "stab"),
        P(),
        P(),
        P(),
        P(),
        P(),
        P(),
        P(),
        P(),
    )
    out_specs = P("round", "stab", None)
    sized = functools.partial(body, mesh.shape["round"], mesh.shape["stab"])
    return jax.shard_map(sized, mesh=mesh, in_specs=in_specs, out_specs=out_specs, check_vma=False)
```

```python
import functools

import jax
import jax.numpy as jnp
from jax import lax
from jax.experimental import pallas as pl
from jax.experimental.pallas import tpu as pltpu
from jax.sharding import PartitionSpec as P

HEADS = 8
HEAD_DIM = 64
STABS_REAL = 840
BLOCK = 4
PAIR = 2 * HEAD_DIM
CHUNK = 448
BACK_CHUNK = 448
GROUP = 128

EPSILON = 1e-06
MASKED_SCORE = -1e30
FACTOR = HEAD_DIM ** (-0.5)
VMEM_LIMIT = 50 * 1024 * 1024


def dot(first, second):
    return jnp.dot(first, second, preferred_element_type=jnp.float32)


def dot_nt(first, second):
    return lax.dot_general(
        first, second, (((1,), (1,)), ((), ())), preferred_element_type=jnp.float32
    )


def dot_tn(first, second):
    return lax.dot_general(
        first, second, (((0,), (0,)), ((), ())), preferred_element_type=jnp.float32
    )


def inverse_rms(hidden):
    return lax.rsqrt(jnp.mean(hidden * hidden, axis=-1, keepdims=True) + EPSILON)


def norm_back(hidden, inverse, gain, upstream):
    scaled = upstream * gain
    inner = jnp.mean(hidden * scaled, axis=-1, keepdims=True)
    return inverse * scaled - hidden * (inverse * inverse * inverse * inner)


def softmax_rows(scores):
    highest = jnp.max(scores, axis=-1, keepdims=True)
    weights = jnp.exp(scores - highest)
    total = jnp.sum(weights, axis=-1, keepdims=True)
    return (weights * (1.0 / total)).astype(jnp.bfloat16)


def space_forward_kernel(
    x_ref, near_ref, gain_ref, wq_ref, wk_ref, wv_ref, wo_ref,
    h_ref, q_ref, k_ref, v_ref, o_ref, p_ref,
    n_scr, bias_scr, acc_scr,
):
    step = pl.program_id(0)
    stabs = x_ref.shape[0]
    blocks, links = near_ref.shape

    @pl.when(step == 0)
    def _():
        x = x_ref[...].astype(jnp.float32)
        n_scr[...] = (x * inverse_rms(x) * gain_ref[...]).astype(jnp.bfloat16)
        acc_scr[...] = x
        lanes = lax.broadcasted_iota(jnp.int32, (blocks, blocks), 1)
        near = near_ref[...]
        listed = jnp.zeros((blocks, blocks), jnp.float32)
        for link in range(links):
            listed = jnp.where(lanes == near[:, link : link + 1], 1.0, listed)
        owner = lax.broadcasted_iota(jnp.int32, (stabs, blocks), 0) // BLOCK
        column = lax.broadcasted_iota(jnp.int32, (stabs, blocks), 1)
        widen = jnp.where(owner == column, 1.0, 0.0).astype(jnp.bfloat16)
        rows = dot(widen, listed.astype(jnp.bfloat16)).astype(jnp.bfloat16)
        bias_scr[...] = jnp.where(dot_nt(rows, widen) > 0.5, 0.0, MASKED_SCORE)

    n = n_scr[...]
    q_ref[...] = dot(n, wq_ref[...]).astype(jnp.bfloat16)
    k_ref[...] = dot(n, wk_ref[...]).astype(jnp.bfloat16)
    v_ref[...] = dot(n, wv_ref[...]).astype(jnp.bfloat16)
    for head in range(2):
        cols = slice(head * HEAD_DIM, (head + 1) * HEAD_DIM)
        keys = k_ref[:, cols]
        values = v_ref[:, cols]
        for start in range(0, stabs, CHUNK):
            rows = slice(start, start + CHUNK)
            scores = dot_nt(q_ref[rows, cols] * FACTOR, keys) + bias_scr[rows, :]
            weights = softmax_rows(scores)
            p_ref[head, rows, :] = weights
            o_ref[rows, cols] = dot(weights, values).astype(jnp.bfloat16)
    acc_scr[...] += dot(o_ref[...], wo_ref[...])

    @pl.when(step == pl.num_programs(0) - 1)
    def _():
        h_ref[...] = acc_scr[...].astype(jnp.bfloat16)


def space_backward_kernel(
    x_ref, gain_ref, g_ref, q_ref, k_ref, v_ref, o_ref, p_ref,
    wq_ref, wk_ref, wv_ref, wo_ref,
    out_ref,
    gn_scr, go_scr, gs_scr, dq_scr, dk_scr, dv_scr,
):
    step = pl.program_id(0)
    stabs = x_ref.shape[0]
    go = dot_nt(g_ref[...], wo_ref[...]).astype(jnp.bfloat16)
    go_scr[...] = go
    product = go.astype(jnp.float32) * o_ref[...].astype(jnp.float32)
    q_turned = q_ref[...].T
    go_turned = go.T
    for head in range(2):
        cols = slice(head * HEAD_DIM, (head + 1) * HEAD_DIM)
        keys = k_ref[:, cols]
        values = v_ref[:, cols]
        delta = jnp.sum(product[:, cols], axis=-1, keepdims=True)
        for start in range(0, stabs, BACK_CHUNK):
            rows = slice(start, start + BACK_CHUNK)
            grad_weights = dot_nt(go_scr[rows, cols], values)
            weights = p_ref[head, rows, :].astype(jnp.float32)
            grad_scores = (
                weights * ((grad_weights - delta[start : start + BACK_CHUNK]) * FACTOR)
            ).astype(jnp.bfloat16)
            gs_scr[rows, :] = grad_scores
            dq_scr[rows, cols] = dot(grad_scores, keys).astype(jnp.bfloat16)
        dk_scr[cols, :] = dot(q_turned[cols, :], gs_scr[...]).astype(jnp.bfloat16)
        dv_scr[cols, :] = dot(go_turned[cols, :], p_ref[head]).astype(jnp.bfloat16)
    part = (
        dot_nt(dq_scr[...], wq_ref[...])
        + dot_nt(dk_scr[...].T, wk_ref[...])
        + dot_nt(dv_scr[...].T, wv_ref[...])
    )

    @pl.when(step == 0)
    def _():
        gn_scr[...] = part

    @pl.when(step > 0)
    def _():
        gn_scr[...] += part

    @pl.when(step == pl.num_programs(0) - 1)
    def _():
        x = x_ref[...].astype(jnp.float32)
        back = norm_back(x, inverse_rms(x), gain_ref[...], gn_scr[...])
        out_ref[...] = (g_ref[...].astype(jnp.float32) + back).astype(jnp.bfloat16)


def time_kernel(
    width, h_ref, side_ref, gain_ref, readout_ref, win_ref, wout_ref,
    g_ref,
    qkv_scr, p_scr, o_scr, go_scr, d_scr,
):
    total, features = h_ref.shape
    tokens = p_scr.shape[-1]
    groups = total // tokens
    hidden = h_ref[...].astype(jnp.float32)
    inverse = inverse_rms(hidden)
    gain = gain_ref[...]
    normed = (hidden * inverse * gain).astype(jnp.bfloat16)
    qkv_scr[...] = dot(normed, win_ref[...]).astype(jnp.bfloat16)
    left = lax.broadcasted_iota(jnp.int32, (tokens, tokens), 0)
    right = lax.broadcasted_iota(jnp.int32, (tokens, tokens), 1)
    kept = ((left % width) == (right % width)) & (right <= left)
    bias = jnp.where(kept, 0.0, MASKED_SCORE)
    bias = jnp.concatenate([bias, bias], axis=0)

    pairs = features // PAIR
    lanes = lax.broadcasted_iota(jnp.int32, (tokens, PAIR), 1)
    near = lanes < HEAD_DIM

    def part(index, pair):
        start = index * features + pair * PAIR
        return slice(start, start + PAIR)

    def rows_of(group):
        return pl.ds(pl.multiple_of(group * tokens, tokens), tokens)

    def stacked(block):
        empty = jnp.zeros_like(block)
        return jnp.concatenate(
            [jnp.where(near, block, empty), jnp.where(near, empty, block)], axis=0
        )

    def merged(block):
        return jnp.where(near, block[:tokens], block[tokens:]).astype(jnp.bfloat16)

    def ahead(group, carry):
        rows = rows_of(group)
        scores = [
            dot_nt(stacked(qkv_scr[rows, part(0, pair)] * FACTOR), qkv_scr[rows, part(1, pair)])
            for pair in range(pairs)
        ]
        weights = [softmax_rows(score + bias) for score in scores]
        for pair in range(pairs):
            p_scr[group * pairs + pair] = weights[pair]
        outs = [dot(weights[pair], qkv_scr[rows, part(2, pair)]) for pair in range(pairs)]
        for pair in range(pairs):
            o_scr[rows, part(0, pair)] = merged(outs[pair])
        return carry

    lax.fori_loop(0, groups, ahead, 0)
    readout = readout_ref[...]
    after = hidden + dot(o_scr[...], wout_ref[...])
    logits = jnp.sum(after * readout, axis=-1, keepdims=True)
    side = side_ref[...]
    grad_logits = (jax.nn.sigmoid(logits) - side[:, 0:1]) * side[:, 1:2]
    grad_after = grad_logits * readout
    go_scr[...] = dot_nt(grad_after.astype(jnp.bfloat16), wout_ref[...]).astype(jnp.bfloat16)

    def behind(group, carry):
        rows = rows_of(group)
        span = range(pairs)
        upstream = [stacked(go_scr[rows, part(0, pair)]) for pair in span]
        products = [dot_nt(upstream[pair], qkv_scr[rows, part(2, pair)]) for pair in span]
        weights = [p_scr[group * pairs + pair] for pair in span]
        grad_scores = []
        for pair in span:
            attended = o_scr[rows, part(0, pair)].astype(jnp.float32)
            attended = jnp.concatenate([attended, attended], axis=0)
            delta = jnp.sum(
                upstream[pair].astype(jnp.float32) * attended, axis=-1, keepdims=True
            )
            grad_scores.append(
                (weights[pair].astype(jnp.float32) * ((products[pair] - delta) * FACTOR)).astype(
                    jnp.bfloat16
                )
            )
        queries = [dot(grad_scores[pair], qkv_scr[rows, part(1, pair)]) for pair in span]
        keys = [dot_tn(grad_scores[pair], stacked(qkv_scr[rows, part(0, pair)])) for pair in span]
        values = [dot_tn(weights[pair], upstream[pair]) for pair in span]
        for pair in span:
            d_scr[rows, part(0, pair)] = merged(queries[pair])
            d_scr[rows, part(1, pair)] = keys[pair].astype(jnp.bfloat16)
            d_scr[rows, part(2, pair)] = values[pair].astype(jnp.bfloat16)
        return carry

    lax.fori_loop(0, groups, behind, 0)
    grad_normed = dot_nt(d_scr[...], win_ref[...])
    hidden = h_ref[...].astype(jnp.float32)
    back = norm_back(hidden, inverse, gain, grad_normed)
    g_ref[...] = (grad_logits * readout + back).astype(jnp.bfloat16)


def whole(*shape):
    return pl.BlockSpec(shape, lambda step: (0,) * len(shape))


def weight_specs(features):
    pairs = features // PAIR
    return [
        pl.BlockSpec((features, PAIR), lambda step: (0, step)),
        pl.BlockSpec((features, PAIR), lambda step: (0, pairs + step)),
        pl.BlockSpec((features, PAIR), lambda step: (0, 2 * pairs + step)),
        pl.BlockSpec((PAIR, features), lambda step: (step, 0)),
    ]


def space_forward(x, neighbours, gain, w_in, w_out):
    stabs, features = x.shape
    pairs = features // PAIR
    column = pl.BlockSpec((stabs, PAIR), lambda step: (0, step))
    rows = jax.ShapeDtypeStruct((stabs, features), jnp.bfloat16)
    square = pl.BlockSpec((2, stabs, stabs), lambda step: (step, 0, 0))
    return pl.pallas_call(
        space_forward_kernel,
        grid=(pairs,),
        in_specs=[whole(stabs, features), whole(*neighbours.shape), whole(1, features)]
        + weight_specs(features),
        out_specs=[whole(stabs, features), column, column, column, column, square],
        out_shape=[
            rows, rows, rows, rows, rows,
            jax.ShapeDtypeStruct((2 * pairs, stabs, stabs), jnp.bfloat16),
        ],
        scratch_shapes=[
            pltpu.VMEM((stabs, features), jnp.bfloat16),
            pltpu.VMEM((stabs, stabs), jnp.float32),
            pltpu.VMEM((stabs, features), jnp.float32),
        ],
        compiler_params=pltpu.CompilerParams(vmem_limit_bytes=VMEM_LIMIT),
        name="space_forward",
    )(x, neighbours, gain, w_in, w_in, w_in, w_out)


def space_backward(x, gain, grad, saved, w_in, w_out):
    stabs, features = x.shape
    pairs = features // PAIR
    column = pl.BlockSpec((stabs, PAIR), lambda step: (0, step))
    square = pl.BlockSpec((2, stabs, stabs), lambda step: (step, 0, 0))
    return pl.pallas_call(
        space_backward_kernel,
        grid=(pairs,),
        in_specs=[whole(stabs, features), whole(1, features), whole(stabs, features)]
        + [column] * 4
        + [square]
        + weight_specs(features),
        out_specs=whole(stabs, features),
        out_shape=jax.ShapeDtypeStruct((stabs, features), jnp.bfloat16),
        scratch_shapes=[
            pltpu.VMEM((stabs, features), jnp.float32),
            pltpu.VMEM((stabs, PAIR), jnp.bfloat16),
            pltpu.VMEM((stabs, stabs), jnp.bfloat16),
            pltpu.VMEM((stabs, PAIR), jnp.bfloat16),
            pltpu.VMEM((PAIR, stabs), jnp.bfloat16),
            pltpu.VMEM((PAIR, stabs), jnp.bfloat16),
        ],
        compiler_params=pltpu.CompilerParams(vmem_limit_bytes=VMEM_LIMIT),
        name="space_backward",
    )(x, gain, grad, *saved, w_in, w_in, w_in, w_out)


def time_both(hidden, side, gain, readout, w_in, w_out, width, tokens):
    total, features = hidden.shape
    return pl.pallas_call(
        functools.partial(time_kernel, width),
        out_shape=jax.ShapeDtypeStruct((total, features), jnp.bfloat16),
        scratch_shapes=[
            pltpu.VMEM((total, 3 * features), jnp.bfloat16),
            pltpu.VMEM((total // tokens * (features // PAIR), 2 * tokens, tokens), jnp.bfloat16),
            pltpu.VMEM((total, features), jnp.bfloat16),
            pltpu.VMEM((total, features), jnp.bfloat16),
            pltpu.VMEM((total, 3 * features), jnp.bfloat16),
        ],
        compiler_params=pltpu.CompilerParams(vmem_limit_bytes=VMEM_LIMIT),
        name="time_both",
    )(hidden, side, gain, readout, w_in, w_out)


PIECE = 16
SPLIT = (2, 3, 2)
PARTS = (2, 2, 3)
MEGA_VMEM = 60 * 1024 * 1024


def spans(counts=SPLIT):
    first = 0
    found = []
    for count in counts:
        found.append((first, count))
        first += count
    return found


def half_turn(tiles):
    return pltpu.roll(tiles, 4, 1)


def pack_messages(rows):
    tiles = rows.shape[0] // 8
    cut = rows.reshape(tiles, 8, rows.shape[1])
    upper = lax.broadcasted_iota(jnp.int32, (tiles, 8, 128), 1) < 4
    parts = [cut[:, :, at : at + 128] for at in range(0, rows.shape[1], 128)]
    turned = [half_turn(part) for part in parts]
    low = [jnp.where(upper, parts[at], turned[at + 1]) for at in (0, 2)]
    high = [jnp.where(upper, turned[at], parts[at + 1]) for at in (0, 2)]
    low = jnp.concatenate(low, axis=1)[:, None]
    high = jnp.concatenate(high, axis=1)[:, None]
    return jnp.concatenate([low, high], axis=1).reshape(2 * tiles, 16, 128)


def unpack_messages(messages):
    tiles = messages.shape[0] // 2
    cut = messages.astype(jnp.float32).reshape(tiles, 2, 2, 8, 128)
    upper = lax.broadcasted_iota(jnp.int32, (tiles, 8, 128), 1) < 4
    found = []
    for part in range(2):
        low, high = cut[:, 0, part], cut[:, 1, part]
        found.append(jnp.where(upper, low, half_turn(high)))
        found.append(jnp.where(upper, half_turn(low), high))
    return jnp.concatenate(found, axis=2).reshape(8 * tiles, 512)


def layer_kernel(
    sizes,
    x_in, labels_in, near_ref, space_gain_ref, time_gain_ref, readout_ref,
    space_in_hbm, space_out_hbm, time_in_hbm, time_out_hbm,
    out_ref,
    x_scr, lab_scr, wsi, wso, wti, wto,
    bias_scr, qkv_scr, p_scr, o_scr, inv_scr,
    send_h, recv_h, send_g, recv_g, g_scr, go_scr, dq_scr, acc_scr, d_scr, out_scr,
    tqkv, tp, to, tgo, td,
    weight_sem, x_send, x_recv, lab_send, lab_recv,
    h_send, h_recv, g_send, g_recv, out_send, out_recv,
):
    depth, inner = sizes
    total = depth * inner
    here_z, here_s = lax.axis_index("round"), lax.axis_index("stab")
    here = here_z * inner + here_s
    here_chip = here_s // 2
    here_core = lax.rem(here_s, 2)
    mesh_ids = pl.DeviceIdType.MESH
    pieces_here, _, _, features = x_scr.shape
    rounds_here, stabs_here = labels_in.shape
    stabs = rounds_here * stabs_here
    rounds = depth * rounds_here
    pairs = features // PAIR

    def device(index):
        return (index // inner, lax.rem(index, inner))

    barrier = pltpu.get_barrier_semaphore()

    def greet(step, carry):
        pl.semaphore_signal(
            barrier, inc=1, device_id=device(lax.rem(here + step, total)), device_id_type=mesh_ids
        )
        return carry

    lax.fori_loop(1, total, greet, 0)
    weights = [
        pltpu.make_async_copy(source, target, weight_sem.at[index])
        for index, (source, target) in enumerate(
            [(space_in_hbm, wsi), (space_out_hbm, wso), (time_in_hbm, wti), (time_out_hbm, wto)]
        )
    ]
    for copy in weights:
        copy.start()
    pl.semaphore_wait(barrier, total - 1)

    chips = inner // 2

    def send_x(peer):
        pltpu.make_async_remote_copy(
            src_ref=x_in.at[peer], dst_ref=x_scr.at[:, here_s],
            send_sem=x_send, recv_sem=x_recv.at[here_s],
            device_id=(here_z, peer), device_id_type=mesh_ids,
        ).start()

    def send_x_chip(step, carry):
        chip = lax.rem(here_chip + step, chips)
        send_x(2 * chip)
        send_x(2 * chip + 1)
        return carry

    lax.fori_loop(1, chips, send_x_chip, 0)
    send_x(2 * here_chip + 1 - here_core)
    pltpu.make_async_copy(x_in.at[here_s], x_scr.at[:, here_s], x_recv.at[here_s]).start()

    def send_labels(step, carry):
        peer = lax.rem(here_z + step, depth)
        pltpu.make_async_remote_copy(
            src_ref=labels_in, dst_ref=lab_scr.at[here_z],
            send_sem=lab_send, recv_sem=lab_recv,
            device_id=(peer, here_s), device_id_type=mesh_ids,
        ).start()
        return carry

    lax.fori_loop(1, depth, send_labels, 0)
    pltpu.make_async_copy(labels_in, lab_scr.at[here_z], lab_recv).start()

    blocks = stabs // BLOCK
    piece_blocks = PIECE // BLOCK
    round_blocks = stabs_here // BLOCK
    key = lax.broadcasted_iota(jnp.int32, (stabs, blocks), 0)
    owner = (
        (key // PIECE) % inner * round_blocks
        + key // (PIECE * inner) * piece_blocks
        + key % PIECE // BLOCK
    )
    column = lax.broadcasted_iota(jnp.int32, (stabs, blocks), 1)
    widen = jnp.where(owner == column, 1.0, 0.0).astype(jnp.bfloat16)
    near = near_ref[...]
    key_block = lax.broadcasted_iota(jnp.int32, (blocks, blocks), 0)
    listed = jnp.zeros((blocks, blocks), jnp.float32)
    for link in range(near.shape[0]):
        listed = jnp.where(key_block == near[link : link + 1, :], 1.0, listed)
    listed = listed.astype(jnp.bfloat16)
    slot = lax.broadcasted_iota(jnp.int32, (128, blocks), 0)
    slot_column = lax.broadcasted_iota(jnp.int32, (128, blocks), 1)
    for index, (first, count) in enumerate(spans()):
        source = (
            (slot // piece_blocks) % inner * round_blocks
            + (first + slot // (piece_blocks * inner)) * piece_blocks
            + slot % piece_blocks
        )
        held = (source == slot_column) & (slot < count * piece_blocks * inner)
        mine = dot_nt(jnp.where(held, 1.0, 0.0).astype(jnp.bfloat16), listed).astype(jnp.bfloat16)
        spread = dot_nt(widen, mine)
        bias_scr[index] = jnp.where(spread > 0.5, 0.0, MASKED_SCORE).astype(jnp.bfloat16)

    near_lanes = lax.broadcasted_iota(jnp.int32, (1, PAIR), 1) < HEAD_DIM
    head_masks = [
        near_lanes.astype(jnp.float32).astype(jnp.bfloat16),
        1 - near_lanes.astype(jnp.float32).astype(jnp.bfloat16),
    ]

    weights[0].wait()

    def project(step, carry):
        chip = lax.rem(here_chip + chips - step, chips)
        for core in range(2):
            place = x_scr.at[:, 2 * chip + core]
            pltpu.make_async_copy(place, place, x_recv.at[2 * chip + core]).wait()
        both = pl.ds(2 * chip, 2)
        rows = pieces_here * 2 * PIECE
        x = x_scr[:, both].reshape(rows, features).astype(jnp.float32)
        normed = (x * inverse_rms(x) * space_gain_ref[...]).astype(jnp.bfloat16)
        made = dot(normed, wsi[...]).astype(jnp.bfloat16)
        qkv_scr[:, both] = made.reshape(pieces_here, 2, PIECE, 3 * features)
        return carry

    lax.fori_loop(0, chips, project, 0)
    weights[1].wait()

    def pair_cols(pair, third):
        return pl.ds(third * features + pair * PAIR, PAIR)

    def all_rows(pair, third):
        return qkv_scr[:, :, :, pair_cols(pair, third)].reshape(stabs, PAIR)

    def send_span(first, count, source, target, send_sem, recv_sem):
        rows = pl.ds(first * PIECE, count * PIECE)

        def send(step, carry):
            peer = lax.rem(here + step, total)
            pltpu.make_async_remote_copy(
                src_ref=source.at[peer, rows], dst_ref=target.at[here, rows],
                send_sem=send_sem, recv_sem=recv_sem,
                device_id=device(peer), device_id_type=mesh_ids,
            ).start()
            return carry

        lax.fori_loop(1, total, send, 0)
        pltpu.make_async_copy(source.at[here, rows], target.at[here, rows], recv_sem).start()

    def wait_span(first, count, target, recv_sem):
        whole_span = target.at[:, pl.ds(first * PIECE, count * PIECE)]
        pltpu.make_async_copy(whole_span, whole_span, recv_sem).wait()

    for index, (first, count) in enumerate(spans()):
        height = count * 128
        rows = slice(first, first + count)
        flat = slice(first * 128, (first + count) * 128)
        row_block = lax.broadcasted_iota(jnp.int32, (height, 128), 0) // BLOCK
        lane = lax.broadcasted_iota(jnp.int32, (height, 128), 1)
        onehot = jnp.where(row_block == lane, 1.0, 0.0).astype(jnp.bfloat16)

        def ahead(pair, carry, rows=rows, flat=flat, height=height, onehot=onehot, index=index):
            queries = qkv_scr[rows, :, :, pair_cols(pair, 0)].reshape(height, PAIR) * FACTOR
            keys = jnp.concatenate([all_rows(pair, 1), bias_scr[index]], axis=1)
            values = all_rows(pair, 2)
            out = None
            for half in range(2):
                mask = head_masks[half]
                scores = dot_nt(jnp.concatenate([queries * mask, onehot], axis=1), keys)
                highest = jnp.max(scores, axis=-1, keepdims=True)
                expd = jnp.exp(scores - highest).astype(jnp.bfloat16)
                p_scr[pair * 2 + half, flat, :] = expd
                ones = jnp.broadcast_to(mask, (stabs, PAIR))
                part = dot(expd, jnp.concatenate([values * mask, ones], axis=1))
                out = part if out is None else out + part
            inverse = 1.0 / out[:, PAIR:]
            inv_scr[flat, pair_cols(pair, 0)] = inverse
            o_scr[flat, pair_cols(pair, 0)] = (out[:, :PAIR] * inverse).astype(jnp.bfloat16)
            return carry

        for pair in range(pairs):
            ahead(pair, 0)
        hidden = x_scr[rows].reshape(height, features).astype(jnp.float32)
        hidden = hidden + dot(o_scr[flat, :], wso[...])
        for piece in range(count):
            packed = pack_messages(hidden[piece * 128 : (piece + 1) * 128]).astype(jnp.bfloat16)
            packed = packed.reshape(inner, depth, 16, 128)
            at = slice((first + piece) * PIECE, (first + piece + 1) * PIECE)
            for z in range(depth):
                send_h[z * inner : (z + 1) * inner, at, :] = packed[:, z]
        send_span(first, count, send_h, recv_h, h_send, h_recv.at[index])

    tokens = BLOCK * rounds
    left = lax.broadcasted_iota(jnp.int32, (tokens, tokens), 0)
    right = lax.broadcasted_iota(jnp.int32, (tokens, tokens), 1)
    kept = ((left % BLOCK) == (right % BLOCK)) & (right <= left)
    causal = jnp.where(kept, 0.0, MASKED_SCORE)
    causal = jnp.concatenate([causal, causal], axis=0)
    lanes = lax.broadcasted_iota(jnp.int32, (tokens, PAIR), 1)
    is_near = lanes < HEAD_DIM

    def stacked(block):
        empty = jnp.zeros_like(block)
        return jnp.concatenate(
            [jnp.where(is_near, block, empty), jnp.where(is_near, empty, block)], axis=0
        )

    def merged(block):
        return jnp.where(is_near, block[:tokens], block[tokens:]).astype(jnp.bfloat16)

    pltpu.make_async_copy(lab_scr, lab_scr, lab_recv).wait()
    token_round = lax.broadcasted_iota(jnp.int32, (tokens, rounds), 0) // BLOCK
    which_round = lax.broadcasted_iota(jnp.int32, (tokens, rounds), 1)
    pick = jnp.where(token_round == which_round, 1.0, 0.0).astype(jnp.bfloat16)
    labels = lab_scr[...].reshape(rounds, stabs_here).astype(jnp.float32).astype(jnp.bfloat16)
    token_labels = dot(pick, labels)
    stab_lane = lax.broadcasted_iota(jnp.int32, (tokens, stabs_here), 1)
    token_slot = lax.broadcasted_iota(jnp.int32, (tokens, stabs_here), 0) % BLOCK
    slot_column = lax.broadcasted_iota(jnp.int32, (tokens, 1), 0) % BLOCK
    weights[2].wait()
    weights[3].wait()

    for index, (first, count) in enumerate(spans()):
        wait_span(first, count, recv_h, h_recv.at[index])
        height = count * tokens
        pieces = range(count)
        found = [
            unpack_messages(recv_h[:, (first + piece) * PIECE : (first + piece + 1) * PIECE, :])
            for piece in pieces
        ]
        hidden = jnp.concatenate(found, axis=0) if count > 1 else found[0]
        inverse = inverse_rms(hidden)
        gain = time_gain_ref[...]
        normed = (hidden * inverse * gain).astype(jnp.bfloat16)
        tqkv[:height, :] = dot(normed, wti[...]).astype(jnp.bfloat16)
        jobs = [(piece, pair) for piece in pieces for pair in range(pairs)]

        def part(third, pair):
            return slice(third * features + pair * PAIR, third * features + (pair + 1) * PAIR)

        def span_of(piece):
            return slice(piece * tokens, (piece + 1) * tokens)

        scores = [
            dot_nt(stacked(tqkv[span_of(i), part(0, p)] * FACTOR), tqkv[span_of(i), part(1, p)])
            for i, p in jobs
        ]
        probs = [softmax_rows(score + causal) for score in scores]
        for job, (i, p) in enumerate(jobs):
            tp[job] = probs[job]
        outs = [dot(probs[job], tqkv[span_of(i), part(2, p)]) for job, (i, p) in enumerate(jobs)]
        for job, (i, p) in enumerate(jobs):
            to[span_of(i), part(0, p)] = merged(outs[job])
        readout = readout_ref[...]
        after = hidden + dot(to[:height, :], wto[...])
        logits = jnp.sum(after * readout, axis=-1, keepdims=True)
        targets, real = [], []
        for piece in pieces:
            at = (first + piece) * PIECE + here_z * BLOCK
            chosen = jnp.where(stab_lane == at + token_slot, token_labels, 0.0)
            targets.append(jnp.sum(chosen, axis=-1, keepdims=True))
            where = here_s * stabs_here + at + slot_column
            real.append(jnp.where(where < STABS_REAL, 1.0, 0.0))
        targets = jnp.concatenate(targets, axis=0) if count > 1 else targets[0]
        real = jnp.concatenate(real, axis=0) if count > 1 else real[0]
        grad_logits = (jax.nn.sigmoid(logits) - targets) * real
        grad_after = grad_logits * readout
        tgo[:height, :] = dot_nt(grad_after.astype(jnp.bfloat16), wto[...]).astype(jnp.bfloat16)

        upstream = [stacked(tgo[span_of(i), part(0, p)]) for i, p in jobs]
        products = [
            dot_nt(upstream[job], tqkv[span_of(i), part(2, p)]) for job, (i, p) in enumerate(jobs)
        ]
        grads = []
        for job, (i, p) in enumerate(jobs):
            attended = to[span_of(i), part(0, p)].astype(jnp.float32)
            attended = jnp.concatenate([attended, attended], axis=0)
            delta = jnp.sum(
                upstream[job].astype(jnp.float32) * attended, axis=-1, keepdims=True
            )
            grads.append(
                (tp[job].astype(jnp.float32) * ((products[job] - delta) * FACTOR)).astype(
                    jnp.bfloat16
                )
            )
        for job, (i, p) in enumerate(jobs):
            td[span_of(i), part(0, p)] = merged(dot(grads[job], tqkv[span_of(i), part(1, p)]))
            keys = dot_tn(grads[job], stacked(tqkv[span_of(i), part(0, p)]))
            td[span_of(i), part(1, p)] = keys.astype(jnp.bfloat16)
            td[span_of(i), part(2, p)] = dot_tn(tp[job], upstream[job]).astype(jnp.bfloat16)
        grad_normed = dot_nt(td[:height, :], wti[...])
        grad_hidden = grad_after + norm_back(hidden, inverse, gain, grad_normed)
        for piece in pieces:
            packed = pack_messages(grad_hidden[span_of(piece)]).astype(jnp.bfloat16)
            send_g[:, (first + piece) * PIECE : (first + piece + 1) * PIECE, :] = packed
        send_span(first, count, send_g, recv_g, g_send, g_recv.at[index])

    def finish(first, count, recv_sem):
        rows = slice(first, first + count)
        flat = slice(first * 128, (first + count) * 128)
        for step in range(2 * pairs):
            block = acc_scr[step * PAIR : (step + 1) * PAIR, flat].astype(jnp.bfloat16)
            start = features + step * PAIR
            d_scr[rows, :, :, start : start + PAIR] = block.T.reshape(count, inner, PIECE, PAIR)
        grad_normed = dot_nt(d_scr[rows].reshape(count * 128, 3 * features), wsi[...])
        x = x_scr[rows].reshape(count * 128, features).astype(jnp.float32)
        back = norm_back(x, inverse_rms(x), space_gain_ref[...], grad_normed)
        grad = g_scr[rows].reshape(count * 128, features).astype(jnp.float32) + back
        out_scr[rows] = grad.astype(jnp.bfloat16).reshape(count, inner, PIECE, features)
        part = pl.ds(first, count)

        def send_out(step, carry):
            peer = lax.rem(here_s + step, inner)
            pltpu.make_async_remote_copy(
                src_ref=out_scr.at[part, peer], dst_ref=out_ref.at[here_s, part],
                send_sem=out_send, recv_sem=recv_sem,
                device_id=(here_z, peer), device_id_type=mesh_ids,
            ).start()
            return carry

        lax.fori_loop(1, inner, send_out, 0)
        pltpu.make_async_copy(out_scr.at[part, here_s], out_ref.at[here_s, part], recv_sem).start()

    for index, (first, count) in enumerate(spans()):
        wait_span(first, count, recv_g, g_recv.at[index])
        height = count * 128
        rows = slice(first, first + count)
        flat = slice(first * 128, (first + count) * 128)
        for piece in range(count):
            at = slice((first + piece) * PIECE, (first + piece + 1) * PIECE)
            cut = jnp.concatenate(
                [recv_g[z * inner : (z + 1) * inner, at, :][:, None] for z in range(depth)], axis=1
            )
            grad = unpack_messages(cut.reshape(total, 16, 128)).astype(jnp.bfloat16)
            g_scr[first + piece] = grad.reshape(inner, PIECE, features)
        grad = g_scr[rows].reshape(height, features)
        go_scr[:height, :] = dot_nt(grad, wso[...]).astype(jnp.bfloat16)
        lane = lax.broadcasted_iota(jnp.int32, (height, PAIR), 1)

        def prepare(pair):
            cols = pair_cols(pair, 0)
            queries = qkv_scr[rows, :, :, cols].reshape(height, PAIR) * FACTOR
            scaled = (go_scr[:height, cols].astype(jnp.float32) * inv_scr[flat, cols]).astype(
                jnp.bfloat16
            )
            product = scaled.astype(jnp.float32) * o_scr[flat, cols].astype(jnp.float32)
            joined = []
            for half in range(2):
                own = (lane < HEAD_DIM) if half == 0 else (lane >= HEAD_DIM)
                delta = jnp.sum(jnp.where(own, product, 0.0), axis=-1, keepdims=True)
                coarse = delta.astype(jnp.bfloat16).astype(jnp.float32)
                extra = jnp.where(lane == 0, -coarse, jnp.where(lane == 1, coarse - delta, 0.0))
                joined.append(
                    jnp.concatenate([scaled * head_masks[half], extra.astype(jnp.bfloat16)], axis=1)
                )
            return queries.T, scaled.T, joined

        prepared = [prepare(pair) for pair in range(pairs)]

        def behind(pair, key_first, key_count):
            cols = pair_cols(pair, 0)
            key_rows = slice(key_first * 128, (key_first + key_count) * 128)
            keys, values = all_rows(pair, 1)[key_rows], all_rows(pair, 2)[key_rows]
            queries_turned, scaled_turned, joined = prepared[pair]
            ones = jnp.ones((key_count * 128, PAIR), jnp.bfloat16)
            values = jnp.concatenate([values, ones], axis=1)
            grad_queries = None
            for half in range(2):
                grad_weights = dot_nt(joined[half], values)
                expd = p_scr[pair * 2 + half, flat, key_rows]
                grad_scores = (expd.astype(jnp.float32) * grad_weights).astype(jnp.bfloat16)
                part = dot(grad_scores, keys * head_masks[half])
                grad_queries = part if grad_queries is None else grad_queries + part
                turned = slice(half * HEAD_DIM, (half + 1) * HEAD_DIM)
                for kind, turned_rows, square in (
                    (0, queries_turned, grad_scores), (1, scaled_turned, expd),
                ):
                    start = kind * features + pair * PAIR + half * HEAD_DIM
                    into = slice(start, start + HEAD_DIM)
                    made = dot(turned_rows[turned, :], square)
                    if index == 0:
                        acc_scr[into, key_rows] = made
                    else:
                        acc_scr[into, key_rows] += made
            if key_first > 0:
                grad_queries = grad_queries + dq_scr[:height, cols]
            if key_first + key_count < pieces_here:
                dq_scr[:height, cols] = grad_queries
            else:
                made = (grad_queries * FACTOR).astype(jnp.bfloat16)
                d_scr[rows, :, :, cols] = made.reshape(count, inner, PIECE, PAIR)

        last = index == len(SPLIT) - 1
        parts = spans(PARTS) if last else [(0, pieces_here)]
        for part_index, (key_first, key_count) in enumerate(parts):
            for pair in range(pairs):
                behind(pair, key_first, key_count)
            if last:
                finish(key_first, key_count, out_recv.at[part_index])

    for index, (key_first, key_count) in enumerate(spans(PARTS)):
        landed = out_ref.at[:, pl.ds(key_first, key_count)]
        pltpu.make_async_copy(landed, landed, out_recv.at[index]).wait()

    def drain(buffer, sem):
        some = buffer.at[pl.ds(0, buffer.shape[0] - 1)]
        pltpu.make_async_copy(some, some, sem).wait()

    drain(lab_scr, lab_send)
    drain(send_h, h_send)
    drain(send_g, g_send)
    some = out_ref.at[pl.ds(0, inner - 1)]
    pltpu.make_async_copy(some, some, x_send).wait()
    pltpu.make_async_copy(some, some, out_send).wait()


def whole_layer(
    sizes, x, labels, near, space_gain, time_gain, readout, space_in, space_out, time_in, time_out
):
    depth, inner = sizes
    total = depth * inner
    rounds_here, stabs_here, features = x.shape
    sent = (rounds_here, stabs_here // PIECE, PIECE, features)
    tiles = (stabs_here // PIECE, inner, PIECE)
    stabs = rounds_here * stabs_here
    bf16, f32 = jnp.bfloat16, jnp.float32
    most = max(SPLIT)
    tokens = BLOCK * depth * rounds_here
    pieces = stabs_here // PIECE
    vmem = pl.BlockSpec(memory_space=pltpu.VMEM)
    anywhere = pl.BlockSpec(memory_space=pl.ANY)
    messages = pltpu.VMEM((total, pieces * PIECE, 128), bf16)
    dma = pltpu.SemaphoreType.DMA
    grad = pl.pallas_call(
        functools.partial(layer_kernel, sizes),
        out_shape=pltpu.VMEM(sent, bf16),
        in_specs=[anywhere, anywhere, vmem, vmem, vmem, vmem] + [anywhere] * 4,
        out_specs=vmem,
        scratch_shapes=[
            pltpu.VMEM(tiles + (features,), bf16),
            pltpu.VMEM((depth,) + labels.shape, jnp.int32),
            pltpu.VMEM(space_in.shape, bf16),
            pltpu.VMEM(space_out.shape, bf16),
            pltpu.VMEM(time_in.shape, bf16),
            pltpu.VMEM(time_out.shape, bf16),
            pltpu.VMEM((len(SPLIT), stabs, 128), bf16),
            pltpu.VMEM(tiles + (3 * features,), bf16),
            pltpu.VMEM((HEADS, stabs, stabs), bf16),
            pltpu.VMEM((stabs, features), bf16),
            pltpu.VMEM((stabs, features), f32),
            messages, messages, messages, messages,
            pltpu.VMEM(tiles + (features,), bf16),
            pltpu.VMEM((most * 128, features), bf16),
            pltpu.VMEM((SPLIT[-1] * 128, features), f32),
            pltpu.VMEM((2 * features, stabs), f32),
            pltpu.VMEM(tiles + (3 * features,), bf16),
            pltpu.VMEM(tiles + (features,), bf16),
            pltpu.VMEM((most * tokens, 3 * features), bf16),
            pltpu.VMEM((most * (features // PAIR), 2 * tokens, tokens), bf16),
            pltpu.VMEM((most * tokens, features), bf16),
            pltpu.VMEM((most * tokens, features), bf16),
            pltpu.VMEM((most * tokens, 3 * features), bf16),
            dma((4,)), dma, dma((inner,)), dma, dma,
            dma, dma((len(SPLIT),)), dma, dma((len(SPLIT),)), dma, dma((len(PARTS),)),
        ],
        compiler_params=pltpu.CompilerParams(
            collective_id=1, has_side_effects=True, vmem_limit_bytes=MEGA_VMEM
        ),
        name="whole_layer",
    )(x.reshape(sent), labels, near, space_gain, time_gain, readout, space_in, space_out, time_in, time_out)
    return grad.reshape(x.shape)


def body(
    round_size,
    stab_size,
    inputs,
    labels,
    neighbours,
    space_in_weights,
    space_out_weights,
    space_gain,
    time_in_weights,
    time_out_weights,
    time_gain,
    readout,
):
    rounds_here, stabs_here, features = inputs.shape
    rounds = rounds_here * round_size
    stabs = stabs_here * stab_size
    copies = stab_size // rounds_here
    assert copies * rounds_here == stab_size
    padded = -(-stabs_here // round_size) * round_size
    part = padded // round_size
    direct = copies == 1 and padded == stabs_here
    both = ("round", "stab")
    space_gain, time_gain, readout = space_gain[None], time_gain[None], readout[None]
    sizes = (round_size, stab_size)
    if (
        copies == 1
        and round_size * BLOCK == PIECE
        and stabs_here == sum(SPLIT) * PIECE
        and rounds * BLOCK == GROUP
        and stab_size * PIECE == GROUP
    ):
        grad = whole_layer(
            sizes, inputs, labels, neighbours.T, space_gain, time_gain, readout,
            space_in_weights, space_out_weights, time_in_weights, time_out_weights,
        )
        return grad.astype(jnp.float32)

    def to_rounds(tokens):
        if copies > 1:
            tokens = jnp.repeat(tokens, copies, axis=0)
        return lax.all_to_all(tokens, "stab", split_axis=0, concat_axis=1, tiled=True)[0]

    def to_tokens(rows):
        split = rows.reshape(stab_size, stabs_here, features)
        moved = lax.all_to_all(split, "stab", split_axis=0, concat_axis=0, tiled=True)
        return moved[::copies] if copies > 1 else moved

    def pad_stabs(tokens):
        return jnp.pad(tokens, ((0, 0), (0, padded - stabs_here), (0, 0)))

    def to_times(rows):
        if direct:
            return lax.all_to_all(
                rows.reshape(rounds, part, features), both, split_axis=0, concat_axis=0, tiled=True
            )
        tokens = pad_stabs(to_tokens(rows))
        return lax.all_to_all(tokens, "round", split_axis=1, concat_axis=0, tiled=True)

    def from_times(times):
        if direct:
            moved = lax.all_to_all(times, both, split_axis=0, concat_axis=0, tiled=True)
            return moved.reshape(stabs, features)
        tokens = lax.all_to_all(times, "round", split_axis=0, concat_axis=1, tiled=True)
        return to_rounds(tokens[:, :stabs_here])

    here_round, here_stab = lax.axis_index("round"), lax.axis_index("stab")
    if direct:
        first = (here_round * stab_size + here_stab) * part
        chunks = jnp.transpose(labels.reshape(rounds_here, round_size, part), (1, 0, 2))
        sent = jnp.tile(chunks.reshape(round_size, rounds_here * part), (stab_size, 1))
        came = lax.all_to_all(sent, both, split_axis=0, concat_axis=0, tiled=True)
        came = came.reshape(round_size, stab_size, rounds_here, part)
        owner = (here_round * stab_size + here_stab) // round_size
        targets = lax.dynamic_index_in_dim(came, owner, 1, keepdims=False)
        targets = targets.reshape(rounds, part).astype(jnp.float32)
    else:
        first = here_stab * stabs_here + here_round * part
        labels_all = lax.all_gather(labels, both, axis=0, tiled=False)
        labels_all = labels_all.reshape(round_size, stab_size, rounds_here, stabs_here)
        labels_all = jnp.transpose(labels_all, (0, 2, 1, 3)).reshape(rounds, stabs)
        labels_all = jnp.pad(labels_all, ((0, 0), (0, padded)))
        targets = lax.dynamic_slice(labels_all, (0, first), (rounds, part)).astype(jnp.float32)
    slot = jnp.arange(part) + (here_round * part if not direct else 0)
    real = first + jnp.arange(part) < STABS_REAL
    if not direct:
        real = real & (slot < stabs_here)
    side = jnp.stack([targets, jnp.broadcast_to(real.astype(jnp.float32), targets.shape)], axis=-1)

    width = max(1, GROUP // rounds)
    while part % width:
        width -= 1
    groups = part // width
    tokens = width * rounds

    def to_groups(times):
        depth = times.shape[-1]
        split = times.reshape(rounds, groups, width, depth)
        return jnp.transpose(split, (1, 0, 2, 3)).reshape(groups * tokens, depth)

    def from_groups(rows):
        split = rows.reshape(groups, rounds, width, features)
        return jnp.transpose(split, (1, 0, 2, 3)).reshape(rounds, part, features)

    x = to_rounds(inputs)
    after_space, *saved = space_forward(
        x, neighbours, space_gain, space_in_weights, space_out_weights
    )
    times = to_groups(to_times(after_space))
    grad_times = time_both(
        times, to_groups(side), time_gain, readout, time_in_weights, time_out_weights, width, tokens
    )
    grad_space = from_times(from_groups(grad_times))
    grad = space_backward(x, space_gain, grad_space, saved, space_in_weights, space_out_weights)
    return to_tokens(grad).astype(jnp.float32)


def solution(mesh):
    in_specs = (
        P("round", "stab", None),
        P("round", "stab"),
        P(),
        P(),
        P(),
        P(),
        P(),
        P(),
        P(),
        P(),
    )
    out_specs = P("round", "stab", None)
    sized = functools.partial(body, mesh.shape["round"], mesh.shape["stab"])
    return jax.shard_map(sized, mesh=mesh, in_specs=in_specs, out_specs=out_specs, check_vma=False)
```

```python
import functools

import jax
import jax.numpy as jnp
from jax import lax
from jax.experimental import pallas as pl
from jax.experimental.pallas import tpu as pltpu
from jax.sharding import PartitionSpec as P

HEADS = 8
HEAD_DIM = 64
STABS_REAL = 840
BLOCK = 4
PAIR = 2 * HEAD_DIM
CHUNK = 448
BACK_CHUNK = 448
GROUP = 128

EPSILON = 1e-06
MASKED_SCORE = -1e30
FACTOR = HEAD_DIM ** (-0.5)
VMEM_LIMIT = 50 * 1024 * 1024


def dot(first, second):
    return jnp.dot(first, second, preferred_element_type=jnp.float32)


def dot_nt(first, second):
    return lax.dot_general(
        first, second, (((1,), (1,)), ((), ())), preferred_element_type=jnp.float32
    )


def dot_tn(first, second):
    return lax.dot_general(
        first, second, (((0,), (0,)), ((), ())), preferred_element_type=jnp.float32
    )


def inverse_rms(hidden):
    return lax.rsqrt(jnp.mean(hidden * hidden, axis=-1, keepdims=True) + EPSILON)


def norm_back(hidden, inverse, gain, upstream):
    scaled = upstream * gain
    inner = jnp.mean(hidden * scaled, axis=-1, keepdims=True)
    return inverse * scaled - hidden * (inverse * inverse * inverse * inner)


def softmax_rows(scores):
    highest = jnp.max(scores, axis=-1, keepdims=True)
    weights = jnp.exp(scores - highest)
    total = jnp.sum(weights, axis=-1, keepdims=True)
    return (weights * (1.0 / total)).astype(jnp.bfloat16)


def space_forward_kernel(
    x_ref, near_ref, gain_ref, wq_ref, wk_ref, wv_ref, wo_ref,
    h_ref, q_ref, k_ref, v_ref, o_ref, p_ref,
    n_scr, bias_scr, acc_scr,
):
    step = pl.program_id(0)
    stabs = x_ref.shape[0]
    blocks, links = near_ref.shape

    @pl.when(step == 0)
    def _():
        x = x_ref[...].astype(jnp.float32)
        n_scr[...] = (x * inverse_rms(x) * gain_ref[...]).astype(jnp.bfloat16)
        acc_scr[...] = x
        lanes = lax.broadcasted_iota(jnp.int32, (blocks, blocks), 1)
        near = near_ref[...]
        listed = jnp.zeros((blocks, blocks), jnp.float32)
        for link in range(links):
            listed = jnp.where(lanes == near[:, link : link + 1], 1.0, listed)
        owner = lax.broadcasted_iota(jnp.int32, (stabs, blocks), 0) // BLOCK
        column = lax.broadcasted_iota(jnp.int32, (stabs, blocks), 1)
        widen = jnp.where(owner == column, 1.0, 0.0).astype(jnp.bfloat16)
        rows = dot(widen, listed.astype(jnp.bfloat16)).astype(jnp.bfloat16)
        bias_scr[...] = jnp.where(dot_nt(rows, widen) > 0.5, 0.0, MASKED_SCORE)

    n = n_scr[...]
    q_ref[...] = dot(n, wq_ref[...]).astype(jnp.bfloat16)
    k_ref[...] = dot(n, wk_ref[...]).astype(jnp.bfloat16)
    v_ref[...] = dot(n, wv_ref[...]).astype(jnp.bfloat16)
    for head in range(2):
        cols = slice(head * HEAD_DIM, (head + 1) * HEAD_DIM)
        keys = k_ref[:, cols]
        values = v_ref[:, cols]
        for start in range(0, stabs, CHUNK):
            rows = slice(start, start + CHUNK)
            scores = dot_nt(q_ref[rows, cols] * FACTOR, keys) + bias_scr[rows, :]
            weights = softmax_rows(scores)
            p_ref[head, rows, :] = weights
            o_ref[rows, cols] = dot(weights, values).astype(jnp.bfloat16)
    acc_scr[...] += dot(o_ref[...], wo_ref[...])

    @pl.when(step == pl.num_programs(0) - 1)
    def _():
        h_ref[...] = acc_scr[...].astype(jnp.bfloat16)


def space_backward_kernel(
    x_ref, gain_ref, g_ref, q_ref, k_ref, v_ref, o_ref, p_ref,
    wq_ref, wk_ref, wv_ref, wo_ref,
    out_ref,
    gn_scr, go_scr, gs_scr, dq_scr, dk_scr, dv_scr,
):
    step = pl.program_id(0)
    stabs = x_ref.shape[0]
    go = dot_nt(g_ref[...], wo_ref[...]).astype(jnp.bfloat16)
    go_scr[...] = go
    product = go.astype(jnp.float32) * o_ref[...].astype(jnp.float32)
    q_turned = q_ref[...].T
    go_turned = go.T
    for head in range(2):
        cols = slice(head * HEAD_DIM, (head + 1) * HEAD_DIM)
        keys = k_ref[:, cols]
        values = v_ref[:, cols]
        delta = jnp.sum(product[:, cols], axis=-1, keepdims=True)
        for start in range(0, stabs, BACK_CHUNK):
            rows = slice(start, start + BACK_CHUNK)
            grad_weights = dot_nt(go_scr[rows, cols], values)
            weights = p_ref[head, rows, :].astype(jnp.float32)
            grad_scores = (
                weights * ((grad_weights - delta[start : start + BACK_CHUNK]) * FACTOR)
            ).astype(jnp.bfloat16)
            gs_scr[rows, :] = grad_scores
            dq_scr[rows, cols] = dot(grad_scores, keys).astype(jnp.bfloat16)
        dk_scr[cols, :] = dot(q_turned[cols, :], gs_scr[...]).astype(jnp.bfloat16)
        dv_scr[cols, :] = dot(go_turned[cols, :], p_ref[head]).astype(jnp.bfloat16)
    part = (
        dot_nt(dq_scr[...], wq_ref[...])
        + dot_nt(dk_scr[...].T, wk_ref[...])
        + dot_nt(dv_scr[...].T, wv_ref[...])
    )

    @pl.when(step == 0)
    def _():
        gn_scr[...] = part

    @pl.when(step > 0)
    def _():
        gn_scr[...] += part

    @pl.when(step == pl.num_programs(0) - 1)
    def _():
        x = x_ref[...].astype(jnp.float32)
        back = norm_back(x, inverse_rms(x), gain_ref[...], gn_scr[...])
        out_ref[...] = (g_ref[...].astype(jnp.float32) + back).astype(jnp.bfloat16)


def time_kernel(
    width, h_ref, side_ref, gain_ref, readout_ref, win_ref, wout_ref,
    g_ref,
    qkv_scr, p_scr, o_scr, go_scr, d_scr,
):
    total, features = h_ref.shape
    tokens = p_scr.shape[-1]
    groups = total // tokens
    hidden = h_ref[...].astype(jnp.float32)
    inverse = inverse_rms(hidden)
    gain = gain_ref[...]
    normed = (hidden * inverse * gain).astype(jnp.bfloat16)
    qkv_scr[...] = dot(normed, win_ref[...]).astype(jnp.bfloat16)
    left = lax.broadcasted_iota(jnp.int32, (tokens, tokens), 0)
    right = lax.broadcasted_iota(jnp.int32, (tokens, tokens), 1)
    kept = ((left % width) == (right % width)) & (right <= left)
    bias = jnp.where(kept, 0.0, MASKED_SCORE)
    bias = jnp.concatenate([bias, bias], axis=0)

    pairs = features // PAIR
    lanes = lax.broadcasted_iota(jnp.int32, (tokens, PAIR), 1)
    near = lanes < HEAD_DIM

    def part(index, pair):
        start = index * features + pair * PAIR
        return slice(start, start + PAIR)

    def rows_of(group):
        return pl.ds(pl.multiple_of(group * tokens, tokens), tokens)

    def stacked(block):
        empty = jnp.zeros_like(block)
        return jnp.concatenate(
            [jnp.where(near, block, empty), jnp.where(near, empty, block)], axis=0
        )

    def merged(block):
        return jnp.where(near, block[:tokens], block[tokens:]).astype(jnp.bfloat16)

    def ahead(group, carry):
        rows = rows_of(group)
        scores = [
            dot_nt(stacked(qkv_scr[rows, part(0, pair)] * FACTOR), qkv_scr[rows, part(1, pair)])
            for pair in range(pairs)
        ]
        weights = [softmax_rows(score + bias) for score in scores]
        for pair in range(pairs):
            p_scr[group * pairs + pair] = weights[pair]
        outs = [dot(weights[pair], qkv_scr[rows, part(2, pair)]) for pair in range(pairs)]
        for pair in range(pairs):
            o_scr[rows, part(0, pair)] = merged(outs[pair])
        return carry

    lax.fori_loop(0, groups, ahead, 0)
    readout = readout_ref[...]
    after = hidden + dot(o_scr[...], wout_ref[...])
    logits = jnp.sum(after * readout, axis=-1, keepdims=True)
    side = side_ref[...]
    grad_logits = (jax.nn.sigmoid(logits) - side[:, 0:1]) * side[:, 1:2]
    grad_after = grad_logits * readout
    go_scr[...] = dot_nt(grad_after.astype(jnp.bfloat16), wout_ref[...]).astype(jnp.bfloat16)

    def behind(group, carry):
        rows = rows_of(group)
        span = range(pairs)
        upstream = [stacked(go_scr[rows, part(0, pair)]) for pair in span]
        products = [dot_nt(upstream[pair], qkv_scr[rows, part(2, pair)]) for pair in span]
        weights = [p_scr[group * pairs + pair] for pair in span]
        grad_scores = []
        for pair in span:
            attended = o_scr[rows, part(0, pair)].astype(jnp.float32)
            attended = jnp.concatenate([attended, attended], axis=0)
            delta = jnp.sum(
                upstream[pair].astype(jnp.float32) * attended, axis=-1, keepdims=True
            )
            grad_scores.append(
                (weights[pair].astype(jnp.float32) * ((products[pair] - delta) * FACTOR)).astype(
                    jnp.bfloat16
                )
            )
        queries = [dot(grad_scores[pair], qkv_scr[rows, part(1, pair)]) for pair in span]
        keys = [dot_tn(grad_scores[pair], stacked(qkv_scr[rows, part(0, pair)])) for pair in span]
        values = [dot_tn(weights[pair], upstream[pair]) for pair in span]
        for pair in span:
            d_scr[rows, part(0, pair)] = merged(queries[pair])
            d_scr[rows, part(1, pair)] = keys[pair].astype(jnp.bfloat16)
            d_scr[rows, part(2, pair)] = values[pair].astype(jnp.bfloat16)
        return carry

    lax.fori_loop(0, groups, behind, 0)
    grad_normed = dot_nt(d_scr[...], win_ref[...])
    hidden = h_ref[...].astype(jnp.float32)
    back = norm_back(hidden, inverse, gain, grad_normed)
    g_ref[...] = (grad_logits * readout + back).astype(jnp.bfloat16)


def whole(*shape):
    return pl.BlockSpec(shape, lambda step: (0,) * len(shape))


def weight_specs(features):
    pairs = features // PAIR
    return [
        pl.BlockSpec((features, PAIR), lambda step: (0, step)),
        pl.BlockSpec((features, PAIR), lambda step: (0, pairs + step)),
        pl.BlockSpec((features, PAIR), lambda step: (0, 2 * pairs + step)),
        pl.BlockSpec((PAIR, features), lambda step: (step, 0)),
    ]


def space_forward(x, neighbours, gain, w_in, w_out):
    stabs, features = x.shape
    pairs = features // PAIR
    column = pl.BlockSpec((stabs, PAIR), lambda step: (0, step))
    rows = jax.ShapeDtypeStruct((stabs, features), jnp.bfloat16)
    square = pl.BlockSpec((2, stabs, stabs), lambda step: (step, 0, 0))
    return pl.pallas_call(
        space_forward_kernel,
        grid=(pairs,),
        in_specs=[whole(stabs, features), whole(*neighbours.shape), whole(1, features)]
        + weight_specs(features),
        out_specs=[whole(stabs, features), column, column, column, column, square],
        out_shape=[
            rows, rows, rows, rows, rows,
            jax.ShapeDtypeStruct((2 * pairs, stabs, stabs), jnp.bfloat16),
        ],
        scratch_shapes=[
            pltpu.VMEM((stabs, features), jnp.bfloat16),
            pltpu.VMEM((stabs, stabs), jnp.float32),
            pltpu.VMEM((stabs, features), jnp.float32),
        ],
        compiler_params=pltpu.CompilerParams(vmem_limit_bytes=VMEM_LIMIT),
        name="space_forward",
    )(x, neighbours, gain, w_in, w_in, w_in, w_out)


def space_backward(x, gain, grad, saved, w_in, w_out):
    stabs, features = x.shape
    pairs = features // PAIR
    column = pl.BlockSpec((stabs, PAIR), lambda step: (0, step))
    square = pl.BlockSpec((2, stabs, stabs), lambda step: (step, 0, 0))
    return pl.pallas_call(
        space_backward_kernel,
        grid=(pairs,),
        in_specs=[whole(stabs, features), whole(1, features), whole(stabs, features)]
        + [column] * 4
        + [square]
        + weight_specs(features),
        out_specs=whole(stabs, features),
        out_shape=jax.ShapeDtypeStruct((stabs, features), jnp.bfloat16),
        scratch_shapes=[
            pltpu.VMEM((stabs, features), jnp.float32),
            pltpu.VMEM((stabs, PAIR), jnp.bfloat16),
            pltpu.VMEM((stabs, stabs), jnp.bfloat16),
            pltpu.VMEM((stabs, PAIR), jnp.bfloat16),
            pltpu.VMEM((PAIR, stabs), jnp.bfloat16),
            pltpu.VMEM((PAIR, stabs), jnp.bfloat16),
        ],
        compiler_params=pltpu.CompilerParams(vmem_limit_bytes=VMEM_LIMIT),
        name="space_backward",
    )(x, gain, grad, *saved, w_in, w_in, w_in, w_out)


def time_both(hidden, side, gain, readout, w_in, w_out, width, tokens):
    total, features = hidden.shape
    return pl.pallas_call(
        functools.partial(time_kernel, width),
        out_shape=jax.ShapeDtypeStruct((total, features), jnp.bfloat16),
        scratch_shapes=[
            pltpu.VMEM((total, 3 * features), jnp.bfloat16),
            pltpu.VMEM((total // tokens * (features // PAIR), 2 * tokens, tokens), jnp.bfloat16),
            pltpu.VMEM((total, features), jnp.bfloat16),
            pltpu.VMEM((total, features), jnp.bfloat16),
            pltpu.VMEM((total, 3 * features), jnp.bfloat16),
        ],
        compiler_params=pltpu.CompilerParams(vmem_limit_bytes=VMEM_LIMIT),
        name="time_both",
    )(hidden, side, gain, readout, w_in, w_out)


PIECE = 16
SPLIT = (2, 3, 2)
PARTS = (2, 2, 3)
MEGA_VMEM = 60 * 1024 * 1024


def spans(counts=SPLIT):
    first = 0
    found = []
    for count in counts:
        found.append((first, count))
        first += count
    return found


def half_turn(tiles):
    return pltpu.roll(tiles, 4, 1)


def pack_messages(rows):
    tiles = rows.shape[0] // 8
    cut = rows.reshape(tiles, 8, rows.shape[1])
    upper = lax.broadcasted_iota(jnp.int32, (tiles, 8, 128), 1) < 4
    parts = [cut[:, :, at : at + 128] for at in range(0, rows.shape[1], 128)]
    turned = [half_turn(part) for part in parts]
    low = [jnp.where(upper, parts[at], turned[at + 1]) for at in (0, 2)]
    high = [jnp.where(upper, turned[at], parts[at + 1]) for at in (0, 2)]
    low = jnp.concatenate(low, axis=1)[:, None]
    high = jnp.concatenate(high, axis=1)[:, None]
    return jnp.concatenate([low, high], axis=1).reshape(2 * tiles, 16, 128)


def unpack_messages(messages):
    tiles = messages.shape[0] // 2
    cut = messages.astype(jnp.float32).reshape(tiles, 2, 2, 8, 128)
    upper = lax.broadcasted_iota(jnp.int32, (tiles, 8, 128), 1) < 4
    found = []
    for part in range(2):
        low, high = cut[:, 0, part], cut[:, 1, part]
        found.append(jnp.where(upper, low, half_turn(high)))
        found.append(jnp.where(upper, half_turn(low), high))
    return jnp.concatenate(found, axis=2).reshape(8 * tiles, 512)


def layer_kernel(
    sizes,
    x_in, labels_in, near_ref, space_gain_ref, time_gain_ref, readout_ref,
    space_in_hbm, space_out_hbm, time_in_hbm, time_out_hbm,
    out_ref,
    x_scr, lab_scr, wsi, wso, wti, wto,
    bias_scr, qkv_scr, p_scr, o_scr, inv_scr,
    send_h, recv_h, send_g, recv_g, g_scr, go_scr, dq_scr, acc_scr, d_scr, out_scr,
    tqkv, tp, to, tgo, td,
    weight_sem, x_send, x_recv, lab_send, lab_recv,
    h_send, h_recv, g_send, g_recv, out_send, out_recv,
):
    depth, inner = sizes
    total = depth * inner
    here_z, here_s = lax.axis_index("round"), lax.axis_index("stab")
    here = here_z * inner + here_s
    here_chip = here_s // 2
    here_core = lax.rem(here_s, 2)
    mesh_ids = pl.DeviceIdType.MESH
    pieces_here, _, _, features = x_scr.shape
    rounds_here, stabs_here = labels_in.shape
    stabs = rounds_here * stabs_here
    rounds = depth * rounds_here
    pairs = features // PAIR

    def device(index):
        return (index // inner, lax.rem(index, inner))

    barrier = pltpu.get_barrier_semaphore()

    def greet(step, carry):
        pl.semaphore_signal(
            barrier, inc=1, device_id=device(lax.rem(here + step, total)), device_id_type=mesh_ids
        )
        return carry

    lax.fori_loop(1, total, greet, 0)
    weights = [
        pltpu.make_async_copy(source, target, weight_sem.at[index])
        for index, (source, target) in enumerate(
            [(space_in_hbm, wsi), (space_out_hbm, wso), (time_in_hbm, wti), (time_out_hbm, wto)]
        )
    ]
    for copy in weights:
        copy.start()
    pl.semaphore_wait(barrier, total - 1)

    chips = inner // 2

    def send_x(peer):
        pltpu.make_async_remote_copy(
            src_ref=x_in.at[peer], dst_ref=x_scr.at[:, here_s],
            send_sem=x_send, recv_sem=x_recv.at[here_s],
            device_id=(here_z, peer), device_id_type=mesh_ids,
        ).start()

    def send_x_chip(step, carry):
        chip = lax.rem(here_chip + step, chips)
        send_x(2 * chip)
        send_x(2 * chip + 1)
        return carry

    lax.fori_loop(1, chips, send_x_chip, 0)
    send_x(2 * here_chip + 1 - here_core)
    pltpu.make_async_copy(x_in.at[here_s], x_scr.at[:, here_s], x_recv.at[here_s]).start()

    def send_labels(step, carry):
        peer = lax.rem(here_z + step, depth)
        pltpu.make_async_remote_copy(
            src_ref=labels_in, dst_ref=lab_scr.at[here_z],
            send_sem=lab_send, recv_sem=lab_recv,
            device_id=(peer, here_s), device_id_type=mesh_ids,
        ).start()
        return carry

    lax.fori_loop(1, depth, send_labels, 0)
    pltpu.make_async_copy(labels_in, lab_scr.at[here_z], lab_recv).start()

    blocks = stabs // BLOCK
    piece_blocks = PIECE // BLOCK
    round_blocks = stabs_here // BLOCK
    key = lax.broadcasted_iota(jnp.int32, (stabs, blocks), 0)
    owner = (
        (key // PIECE) % inner * round_blocks
        + key // (PIECE * inner) * piece_blocks
        + key % PIECE // BLOCK
    )
    column = lax.broadcasted_iota(jnp.int32, (stabs, blocks), 1)
    widen = jnp.where(owner == column, 1.0, 0.0).astype(jnp.bfloat16)
    near = near_ref[...]
    key_block = lax.broadcasted_iota(jnp.int32, (blocks, blocks), 0)
    listed = jnp.zeros((blocks, blocks), jnp.float32)
    for link in range(near.shape[0]):
        listed = jnp.where(key_block == near[link : link + 1, :], 1.0, listed)
    listed = listed.astype(jnp.bfloat16)
    slot = lax.broadcasted_iota(jnp.int32, (128, blocks), 0)
    slot_column = lax.broadcasted_iota(jnp.int32, (128, blocks), 1)
    for index, (first, count) in enumerate(spans()):
        source = (
            (slot // piece_blocks) % inner * round_blocks
            + (first + slot // (piece_blocks * inner)) * piece_blocks
            + slot % piece_blocks
        )
        held = (source == slot_column) & (slot < count * piece_blocks * inner)
        mine = dot_nt(jnp.where(held, 1.0, 0.0).astype(jnp.bfloat16), listed).astype(jnp.bfloat16)
        spread = dot_nt(widen, mine)
        bias_scr[index] = jnp.where(spread > 0.5, 0.0, MASKED_SCORE).astype(jnp.bfloat16)

    near_lanes = lax.broadcasted_iota(jnp.int32, (1, PAIR), 1) < HEAD_DIM
    head_masks = [
        near_lanes.astype(jnp.float32).astype(jnp.bfloat16),
        1 - near_lanes.astype(jnp.float32).astype(jnp.bfloat16),
    ]

    weights[0].wait()

    def project(step, carry):
        chip = lax.rem(here_chip + chips - step, chips)
        for core in range(2):
            place = x_scr.at[:, 2 * chip + core]
            pltpu.make_async_copy(place, place, x_recv.at[2 * chip + core]).wait()
        both = pl.ds(2 * chip, 2)
        rows = pieces_here * 2 * PIECE
        x = x_scr[:, both].reshape(rows, features).astype(jnp.float32)
        normed = (x * inverse_rms(x) * space_gain_ref[...]).astype(jnp.bfloat16)
        made = dot(normed, wsi[...]).astype(jnp.bfloat16)
        qkv_scr[:, both] = made.reshape(pieces_here, 2, PIECE, 3 * features)
        return carry

    lax.fori_loop(0, chips, project, 0)
    weights[1].wait()

    def pair_cols(pair, third):
        start = third * features + pair * PAIR
        return pl.ds(start if isinstance(pair, int) else pl.multiple_of(start, PAIR), PAIR)

    def all_rows(pair, third):
        return qkv_scr[:, :, :, pair_cols(pair, third)].reshape(stabs, PAIR)

    def send_span(first, count, source, target, send_sem, recv_sem):
        rows = pl.ds(first * PIECE, count * PIECE)

        def send(step, carry):
            peer = lax.rem(here + step, total)
            pltpu.make_async_remote_copy(
                src_ref=source.at[peer, rows], dst_ref=target.at[here, rows],
                send_sem=send_sem, recv_sem=recv_sem,
                device_id=device(peer), device_id_type=mesh_ids,
            ).start()
            return carry

        lax.fori_loop(1, total, send, 0)
        pltpu.make_async_copy(source.at[here, rows], target.at[here, rows], recv_sem).start()

    def wait_span(first, count, target, recv_sem):
        whole_span = target.at[:, pl.ds(first * PIECE, count * PIECE)]
        pltpu.make_async_copy(whole_span, whole_span, recv_sem).wait()

    for index, (first, count) in enumerate(spans()):
        height = count * 128
        rows = slice(first, first + count)
        flat = slice(first * 128, (first + count) * 128)
        row_block = lax.broadcasted_iota(jnp.int32, (height, 128), 0) // BLOCK
        lane = lax.broadcasted_iota(jnp.int32, (height, 128), 1)
        onehot = jnp.where(row_block == lane, 1.0, 0.0).astype(jnp.bfloat16)

        def ahead(pair, carry, rows=rows, flat=flat, height=height, onehot=onehot, index=index):
            queries = qkv_scr[rows, :, :, pair_cols(pair, 0)].reshape(height, PAIR) * FACTOR
            keys = jnp.concatenate([all_rows(pair, 1), bias_scr[index]], axis=1)
            values = all_rows(pair, 2)
            out = None
            for half in range(2):
                mask = head_masks[half]
                scores = dot_nt(jnp.concatenate([queries * mask, onehot], axis=1), keys)
                highest = jnp.max(scores, axis=-1, keepdims=True)
                expd = jnp.exp(scores - highest).astype(jnp.bfloat16)
                p_scr[pair * 2 + half, flat, :] = expd
                ones = jnp.broadcast_to(mask, (stabs, PAIR))
                part = dot(expd, jnp.concatenate([values * mask, ones], axis=1))
                out = part if out is None else out + part
            inverse = 1.0 / out[:, PAIR:]
            inv_scr[flat, pair_cols(pair, 0)] = inverse
            o_scr[flat, pair_cols(pair, 0)] = (out[:, :PAIR] * inverse).astype(jnp.bfloat16)
            return carry

        if index == 0:
            for pair in range(pairs):
                ahead(pair, 0)
        else:
            def two_ahead(step, carry, ahead=ahead):
                ahead(2 * step, 0)
                ahead(2 * step + 1, 0)
                return carry

            lax.fori_loop(0, pairs // 2, two_ahead, 0)
        hidden = x_scr[rows].reshape(height, features).astype(jnp.float32)
        hidden = hidden + dot(o_scr[flat, :], wso[...])
        for piece in range(count):
            packed = pack_messages(hidden[piece * 128 : (piece + 1) * 128]).astype(jnp.bfloat16)
            packed = packed.reshape(inner, depth, 16, 128)
            at = slice((first + piece) * PIECE, (first + piece + 1) * PIECE)
            for z in range(depth):
                send_h[z * inner : (z + 1) * inner, at, :] = packed[:, z]
        send_span(first, count, send_h, recv_h, h_send, h_recv.at[index])

    tokens = BLOCK * rounds
    left = lax.broadcasted_iota(jnp.int32, (tokens, tokens), 0)
    right = lax.broadcasted_iota(jnp.int32, (tokens, tokens), 1)
    kept = ((left % BLOCK) == (right % BLOCK)) & (right <= left)
    causal = jnp.where(kept, 0.0, MASKED_SCORE)
    causal = jnp.concatenate([causal, causal], axis=0)
    lanes = lax.broadcasted_iota(jnp.int32, (tokens, PAIR), 1)
    is_near = lanes < HEAD_DIM

    def stacked(block):
        empty = jnp.zeros_like(block)
        return jnp.concatenate(
            [jnp.where(is_near, block, empty), jnp.where(is_near, empty, block)], axis=0
        )

    def merged(block):
        return jnp.where(is_near, block[:tokens], block[tokens:]).astype(jnp.bfloat16)

    pltpu.make_async_copy(lab_scr, lab_scr, lab_recv).wait()
    token_round = lax.broadcasted_iota(jnp.int32, (tokens, rounds), 0) // BLOCK
    which_round = lax.broadcasted_iota(jnp.int32, (tokens, rounds), 1)
    pick = jnp.where(token_round == which_round, 1.0, 0.0).astype(jnp.bfloat16)
    labels = lab_scr[...].reshape(rounds, stabs_here).astype(jnp.float32).astype(jnp.bfloat16)
    token_labels = dot(pick, labels)
    stab_lane = lax.broadcasted_iota(jnp.int32, (tokens, stabs_here), 1)
    token_slot = lax.broadcasted_iota(jnp.int32, (tokens, stabs_here), 0) % BLOCK
    slot_column = lax.broadcasted_iota(jnp.int32, (tokens, 1), 0) % BLOCK
    weights[2].wait()
    weights[3].wait()

    for index, (first, count) in enumerate(spans()):
        wait_span(first, count, recv_h, h_recv.at[index])
        height = count * tokens
        pieces = range(count)
        found = [
            unpack_messages(recv_h[:, (first + piece) * PIECE : (first + piece + 1) * PIECE, :])
            for piece in pieces
        ]
        hidden = jnp.concatenate(found, axis=0) if count > 1 else found[0]
        inverse = inverse_rms(hidden)
        gain = time_gain_ref[...]
        normed = (hidden * inverse * gain).astype(jnp.bfloat16)
        tqkv[:height, :] = dot(normed, wti[...]).astype(jnp.bfloat16)
        jobs = [(piece, pair) for piece in pieces for pair in range(pairs)]

        def part(third, pair):
            return slice(third * features + pair * PAIR, third * features + (pair + 1) * PAIR)

        def span_of(piece):
            return slice(piece * tokens, (piece + 1) * tokens)

        scores = [
            dot_nt(stacked(tqkv[span_of(i), part(0, p)] * FACTOR), tqkv[span_of(i), part(1, p)])
            for i, p in jobs
        ]
        probs = [softmax_rows(score + causal) for score in scores]
        for job, (i, p) in enumerate(jobs):
            tp[job] = probs[job]
        outs = [dot(probs[job], tqkv[span_of(i), part(2, p)]) for job, (i, p) in enumerate(jobs)]
        for job, (i, p) in enumerate(jobs):
            to[span_of(i), part(0, p)] = merged(outs[job])
        readout = readout_ref[...]
        after = hidden + dot(to[:height, :], wto[...])
        logits = jnp.sum(after * readout, axis=-1, keepdims=True)
        targets, real = [], []
        for piece in pieces:
            at = (first + piece) * PIECE + here_z * BLOCK
            chosen = jnp.where(stab_lane == at + token_slot, token_labels, 0.0)
            targets.append(jnp.sum(chosen, axis=-1, keepdims=True))
            where = here_s * stabs_here + at + slot_column
            real.append(jnp.where(where < STABS_REAL, 1.0, 0.0))
        targets = jnp.concatenate(targets, axis=0) if count > 1 else targets[0]
        real = jnp.concatenate(real, axis=0) if count > 1 else real[0]
        grad_logits = (jax.nn.sigmoid(logits) - targets) * real
        grad_after = grad_logits * readout
        tgo[:height, :] = dot_nt(grad_after.astype(jnp.bfloat16), wto[...]).astype(jnp.bfloat16)

        upstream = [stacked(tgo[span_of(i), part(0, p)]) for i, p in jobs]
        products = [
            dot_nt(upstream[job], tqkv[span_of(i), part(2, p)]) for job, (i, p) in enumerate(jobs)
        ]
        grads = []
        for job, (i, p) in enumerate(jobs):
            attended = to[span_of(i), part(0, p)].astype(jnp.float32)
            attended = jnp.concatenate([attended, attended], axis=0)
            delta = jnp.sum(
                upstream[job].astype(jnp.float32) * attended, axis=-1, keepdims=True
            )
            grads.append(
                (tp[job].astype(jnp.float32) * ((products[job] - delta) * FACTOR)).astype(
                    jnp.bfloat16
                )
            )
        for job, (i, p) in enumerate(jobs):
            td[span_of(i), part(0, p)] = merged(dot(grads[job], tqkv[span_of(i), part(1, p)]))
            keys = dot_tn(grads[job], stacked(tqkv[span_of(i), part(0, p)]))
            td[span_of(i), part(1, p)] = keys.astype(jnp.bfloat16)
            td[span_of(i), part(2, p)] = dot_tn(tp[job], upstream[job]).astype(jnp.bfloat16)
        grad_normed = dot_nt(td[:height, :], wti[...])
        grad_hidden = grad_after + norm_back(hidden, inverse, gain, grad_normed)
        for piece in pieces:
            packed = pack_messages(grad_hidden[span_of(piece)]).astype(jnp.bfloat16)
            send_g[:, (first + piece) * PIECE : (first + piece + 1) * PIECE, :] = packed
        send_span(first, count, send_g, recv_g, g_send, g_recv.at[index])

    def finish(first, count, recv_sem):
        rows = slice(first, first + count)
        flat = slice(first * 128, (first + count) * 128)
        for step in range(2 * pairs):
            block = acc_scr[step * PAIR : (step + 1) * PAIR, flat].astype(jnp.bfloat16)
            start = features + step * PAIR
            d_scr[rows, :, :, start : start + PAIR] = block.T.reshape(count, inner, PIECE, PAIR)
        grad_normed = dot_nt(d_scr[rows].reshape(count * 128, 3 * features), wsi[...])
        x = x_scr[rows].reshape(count * 128, features).astype(jnp.float32)
        back = norm_back(x, inverse_rms(x), space_gain_ref[...], grad_normed)
        grad = g_scr[rows].reshape(count * 128, features).astype(jnp.float32) + back
        out_scr[rows] = grad.astype(jnp.bfloat16).reshape(count, inner, PIECE, features)
        part = pl.ds(first, count)

        def send_out(step, carry):
            peer = lax.rem(here_s + step, inner)
            pltpu.make_async_remote_copy(
                src_ref=out_scr.at[part, peer], dst_ref=out_ref.at[here_s, part],
                send_sem=out_send, recv_sem=recv_sem,
                device_id=(here_z, peer), device_id_type=mesh_ids,
            ).start()
            return carry

        lax.fori_loop(1, inner, send_out, 0)
        pltpu.make_async_copy(out_scr.at[part, here_s], out_ref.at[here_s, part], recv_sem).start()

    for index, (first, count) in enumerate(spans()):
        wait_span(first, count, recv_g, g_recv.at[index])
        height = count * 128
        rows = slice(first, first + count)
        flat = slice(first * 128, (first + count) * 128)
        for piece in range(count):
            at = slice((first + piece) * PIECE, (first + piece + 1) * PIECE)
            cut = jnp.concatenate(
                [recv_g[z * inner : (z + 1) * inner, at, :][:, None] for z in range(depth)], axis=1
            )
            grad = unpack_messages(cut.reshape(total, 16, 128)).astype(jnp.bfloat16)
            g_scr[first + piece] = grad.reshape(inner, PIECE, features)
        grad = g_scr[rows].reshape(height, features)
        go_scr[:height, :] = dot_nt(grad, wso[...]).astype(jnp.bfloat16)
        lane = lax.broadcasted_iota(jnp.int32, (height, PAIR), 1)

        def prepare(pair):
            cols = pair_cols(pair, 0)
            queries = qkv_scr[rows, :, :, cols].reshape(height, PAIR) * FACTOR
            scaled = (go_scr[:height, cols].astype(jnp.float32) * inv_scr[flat, cols]).astype(
                jnp.bfloat16
            )
            product = scaled.astype(jnp.float32) * o_scr[flat, cols].astype(jnp.float32)
            joined = []
            for half in range(2):
                own = (lane < HEAD_DIM) if half == 0 else (lane >= HEAD_DIM)
                delta = jnp.sum(jnp.where(own, product, 0.0), axis=-1, keepdims=True)
                coarse = delta.astype(jnp.bfloat16).astype(jnp.float32)
                extra = jnp.where(lane == 0, -coarse, jnp.where(lane == 1, coarse - delta, 0.0))
                joined.append(
                    jnp.concatenate([scaled * head_masks[half], extra.astype(jnp.bfloat16)], axis=1)
                )
            return queries.T, scaled.T, joined

        def behind(pair, prepared, key_first, key_count):
            cols = pair_cols(pair, 0)
            key_rows = slice(key_first * 128, (key_first + key_count) * 128)
            keys, values = all_rows(pair, 1)[key_rows], all_rows(pair, 2)[key_rows]
            queries_turned, scaled_turned, joined = prepared
            ones = jnp.ones((key_count * 128, PAIR), jnp.bfloat16)
            values = jnp.concatenate([values, ones], axis=1)
            grad_queries = None
            for half in range(2):
                grad_weights = dot_nt(joined[half], values)
                expd = p_scr[pair * 2 + half, flat, key_rows]
                grad_scores = (expd.astype(jnp.float32) * grad_weights).astype(jnp.bfloat16)
                part = dot(grad_scores, keys * head_masks[half])
                grad_queries = part if grad_queries is None else grad_queries + part
                turned = slice(half * HEAD_DIM, (half + 1) * HEAD_DIM)
                for kind, turned_rows, square in (
                    (0, queries_turned, grad_scores), (1, scaled_turned, expd),
                ):
                    start = kind * features + pair * PAIR + half * HEAD_DIM
                    if not isinstance(pair, int):
                        start = pl.multiple_of(start, HEAD_DIM)
                    into = pl.ds(start, HEAD_DIM)
                    made = dot(turned_rows[turned, :], square)
                    if index == 0:
                        acc_scr[into, key_rows] = made
                    else:
                        acc_scr[into, key_rows] += made
            if key_first > 0:
                grad_queries = grad_queries + dq_scr[:height, cols]
            if key_first + key_count < pieces_here:
                dq_scr[:height, cols] = grad_queries
            else:
                made = (grad_queries * FACTOR).astype(jnp.bfloat16)
                d_scr[rows, :, :, cols] = made.reshape(count, inner, PIECE, PAIR)

        if index < len(SPLIT) - 1:
            def two_behind(step, carry, prepare=prepare, behind=behind):
                behind(2 * step, prepare(2 * step), 0, pieces_here)
                behind(2 * step + 1, prepare(2 * step + 1), 0, pieces_here)
                return carry

            lax.fori_loop(0, pairs // 2, two_behind, 0)
        else:
            prepared = [prepare(pair) for pair in range(pairs)]
            for part_index, (key_first, key_count) in enumerate(spans(PARTS)):
                for pair in range(pairs):
                    behind(pair, prepared[pair], key_first, key_count)
                finish(key_first, key_count, out_recv.at[part_index])

    for index, (key_first, key_count) in enumerate(spans(PARTS)):
        landed = out_ref.at[:, pl.ds(key_first, key_count)]
        pltpu.make_async_copy(landed, landed, out_recv.at[index]).wait()

    def drain(buffer, sem):
        some = buffer.at[pl.ds(0, buffer.shape[0] - 1)]
        pltpu.make_async_copy(some, some, sem).wait()

    drain(lab_scr, lab_send)
    drain(send_h, h_send)
    drain(send_g, g_send)
    some = out_ref.at[pl.ds(0, inner - 1)]
    pltpu.make_async_copy(some, some, x_send).wait()
    pltpu.make_async_copy(some, some, out_send).wait()


def whole_layer(
    sizes, x, labels, near, space_gain, time_gain, readout, space_in, space_out, time_in, time_out
):
    depth, inner = sizes
    total = depth * inner
    rounds_here, stabs_here, features = x.shape
    sent = (rounds_here, stabs_here // PIECE, PIECE, features)
    tiles = (stabs_here // PIECE, inner, PIECE)
    stabs = rounds_here * stabs_here
    bf16, f32 = jnp.bfloat16, jnp.float32
    most = max(SPLIT)
    tokens = BLOCK * depth * rounds_here
    pieces = stabs_here // PIECE
    vmem = pl.BlockSpec(memory_space=pltpu.VMEM)
    anywhere = pl.BlockSpec(memory_space=pl.ANY)
    messages = pltpu.VMEM((total, pieces * PIECE, 128), bf16)
    dma = pltpu.SemaphoreType.DMA
    grad = pl.pallas_call(
        functools.partial(layer_kernel, sizes),
        out_shape=pltpu.VMEM(sent, bf16),
        in_specs=[anywhere, anywhere, vmem, vmem, vmem, vmem] + [anywhere] * 4,
        out_specs=vmem,
        scratch_shapes=[
            pltpu.VMEM(tiles + (features,), bf16),
            pltpu.VMEM((depth,) + labels.shape, jnp.int32),
            pltpu.VMEM(space_in.shape, bf16),
            pltpu.VMEM(space_out.shape, bf16),
            pltpu.VMEM(time_in.shape, bf16),
            pltpu.VMEM(time_out.shape, bf16),
            pltpu.VMEM((len(SPLIT), stabs, 128), bf16),
            pltpu.VMEM(tiles + (3 * features,), bf16),
            pltpu.VMEM((HEADS, stabs, stabs), bf16),
            pltpu.VMEM((stabs, features), bf16),
            pltpu.VMEM((stabs, features), f32),
            messages, messages, messages, messages,
            pltpu.VMEM(tiles + (features,), bf16),
            pltpu.VMEM((most * 128, features), bf16),
            pltpu.VMEM((SPLIT[-1] * 128, features), f32),
            pltpu.VMEM((2 * features, stabs), f32),
            pltpu.VMEM(tiles + (3 * features,), bf16),
            pltpu.VMEM(tiles + (features,), bf16),
            pltpu.VMEM((most * tokens, 3 * features), bf16),
            pltpu.VMEM((most * (features // PAIR), 2 * tokens, tokens), bf16),
            pltpu.VMEM((most * tokens, features), bf16),
            pltpu.VMEM((most * tokens, features), bf16),
            pltpu.VMEM((most * tokens, 3 * features), bf16),
            dma((4,)), dma, dma((inner,)), dma, dma,
            dma, dma((len(SPLIT),)), dma, dma((len(SPLIT),)), dma, dma((len(PARTS),)),
        ],
        compiler_params=pltpu.CompilerParams(
            collective_id=1, has_side_effects=True, vmem_limit_bytes=MEGA_VMEM
        ),
        name="whole_layer",
    )(x.reshape(sent), labels, near, space_gain, time_gain, readout, space_in, space_out, time_in, time_out)
    return grad.reshape(x.shape)


def body(
    round_size,
    stab_size,
    inputs,
    labels,
    neighbours,
    space_in_weights,
    space_out_weights,
    space_gain,
    time_in_weights,
    time_out_weights,
    time_gain,
    readout,
):
    rounds_here, stabs_here, features = inputs.shape
    rounds = rounds_here * round_size
    stabs = stabs_here * stab_size
    copies = stab_size // rounds_here
    assert copies * rounds_here == stab_size
    padded = -(-stabs_here // round_size) * round_size
    part = padded // round_size
    direct = copies == 1 and padded == stabs_here
    both = ("round", "stab")
    space_gain, time_gain, readout = space_gain[None], time_gain[None], readout[None]
    sizes = (round_size, stab_size)
    if (
        copies == 1
        and round_size * BLOCK == PIECE
        and stabs_here == sum(SPLIT) * PIECE
        and rounds * BLOCK == GROUP
        and stab_size * PIECE == GROUP
    ):
        grad = whole_layer(
            sizes, inputs, labels, neighbours.T, space_gain, time_gain, readout,
            space_in_weights, space_out_weights, time_in_weights, time_out_weights,
        )
        return grad.astype(jnp.float32)

    def to_rounds(tokens):
        if copies > 1:
            tokens = jnp.repeat(tokens, copies, axis=0)
        return lax.all_to_all(tokens, "stab", split_axis=0, concat_axis=1, tiled=True)[0]

    def to_tokens(rows):
        split = rows.reshape(stab_size, stabs_here, features)
        moved = lax.all_to_all(split, "stab", split_axis=0, concat_axis=0, tiled=True)
        return moved[::copies] if copies > 1 else moved

    def pad_stabs(tokens):
        return jnp.pad(tokens, ((0, 0), (0, padded - stabs_here), (0, 0)))

    def to_times(rows):
        if direct:
            return lax.all_to_all(
                rows.reshape(rounds, part, features), both, split_axis=0, concat_axis=0, tiled=True
            )
        tokens = pad_stabs(to_tokens(rows))
        return lax.all_to_all(tokens, "round", split_axis=1, concat_axis=0, tiled=True)

    def from_times(times):
        if direct:
            moved = lax.all_to_all(times, both, split_axis=0, concat_axis=0, tiled=True)
            return moved.reshape(stabs, features)
        tokens = lax.all_to_all(times, "round", split_axis=0, concat_axis=1, tiled=True)
        return to_rounds(tokens[:, :stabs_here])

    here_round, here_stab = lax.axis_index("round"), lax.axis_index("stab")
    if direct:
        first = (here_round * stab_size + here_stab) * part
        chunks = jnp.transpose(labels.reshape(rounds_here, round_size, part), (1, 0, 2))
        sent = jnp.tile(chunks.reshape(round_size, rounds_here * part), (stab_size, 1))
        came = lax.all_to_all(sent, both, split_axis=0, concat_axis=0, tiled=True)
        came = came.reshape(round_size, stab_size, rounds_here, part)
        owner = (here_round * stab_size + here_stab) // round_size
        targets = lax.dynamic_index_in_dim(came, owner, 1, keepdims=False)
        targets = targets.reshape(rounds, part).astype(jnp.float32)
    else:
        first = here_stab * stabs_here + here_round * part
        labels_all = lax.all_gather(labels, both, axis=0, tiled=False)
        labels_all = labels_all.reshape(round_size, stab_size, rounds_here, stabs_here)
        labels_all = jnp.transpose(labels_all, (0, 2, 1, 3)).reshape(rounds, stabs)
        labels_all = jnp.pad(labels_all, ((0, 0), (0, padded)))
        targets = lax.dynamic_slice(labels_all, (0, first), (rounds, part)).astype(jnp.float32)
    slot = jnp.arange(part) + (here_round * part if not direct else 0)
    real = first + jnp.arange(part) < STABS_REAL
    if not direct:
        real = real & (slot < stabs_here)
    side = jnp.stack([targets, jnp.broadcast_to(real.astype(jnp.float32), targets.shape)], axis=-1)

    width = max(1, GROUP // rounds)
    while part % width:
        width -= 1
    groups = part // width
    tokens = width * rounds

    def to_groups(times):
        depth = times.shape[-1]
        split = times.reshape(rounds, groups, width, depth)
        return jnp.transpose(split, (1, 0, 2, 3)).reshape(groups * tokens, depth)

    def from_groups(rows):
        split = rows.reshape(groups, rounds, width, features)
        return jnp.transpose(split, (1, 0, 2, 3)).reshape(rounds, part, features)

    x = to_rounds(inputs)
    after_space, *saved = space_forward(
        x, neighbours, space_gain, space_in_weights, space_out_weights
    )
    times = to_groups(to_times(after_space))
    grad_times = time_both(
        times, to_groups(side), time_gain, readout, time_in_weights, time_out_weights, width, tokens
    )
    grad_space = from_times(from_groups(grad_times))
    grad = space_backward(x, space_gain, grad_space, saved, space_in_weights, space_out_weights)
    return to_tokens(grad).astype(jnp.float32)


def solution(mesh):
    in_specs = (
        P("round", "stab", None),
        P("round", "stab"),
        P(),
        P(),
        P(),
        P(),
        P(),
        P(),
        P(),
        P(),
    )
    out_specs = P("round", "stab", None)
    sized = functools.partial(body, mesh.shape["round"], mesh.shape["stab"])
    return jax.shard_map(sized, mesh=mesh, in_specs=in_specs, out_specs=out_specs, check_vma=False)
```

```python
import functools

import jax
import jax.numpy as jnp
from jax import lax
from jax.experimental import pallas as pl
from jax.experimental.pallas import tpu as pltpu
from jax.sharding import PartitionSpec as P

HEADS = 8
HEAD_DIM = 64
STABS_REAL = 840
BLOCK = 4
PAIR = 2 * HEAD_DIM
CHUNK = 448
BACK_CHUNK = 448
GROUP = 128

EPSILON = 1e-06
MASKED_SCORE = -1e30
FACTOR = HEAD_DIM ** (-0.5)
VMEM_LIMIT = 50 * 1024 * 1024


def dot(first, second):
    return jnp.dot(first, second, preferred_element_type=jnp.float32)


def dot_nt(first, second):
    return lax.dot_general(
        first, second, (((1,), (1,)), ((), ())), preferred_element_type=jnp.float32
    )


def dot_tn(first, second):
    return lax.dot_general(
        first, second, (((0,), (0,)), ((), ())), preferred_element_type=jnp.float32
    )


def inverse_rms(hidden):
    return lax.rsqrt(jnp.mean(hidden * hidden, axis=-1, keepdims=True) + EPSILON)


def norm_back(hidden, inverse, gain, upstream):
    scaled = upstream * gain
    inner = jnp.mean(hidden * scaled, axis=-1, keepdims=True)
    return inverse * scaled - hidden * (inverse * inverse * inverse * inner)


def softmax_rows(scores):
    highest = jnp.max(scores, axis=-1, keepdims=True)
    weights = jnp.exp(scores - highest)
    total = jnp.sum(weights, axis=-1, keepdims=True)
    return (weights * (1.0 / total)).astype(jnp.bfloat16)


def space_forward_kernel(
    x_ref, near_ref, gain_ref, wq_ref, wk_ref, wv_ref, wo_ref,
    h_ref, q_ref, k_ref, v_ref, o_ref, p_ref,
    n_scr, bias_scr, acc_scr,
):
    step = pl.program_id(0)
    stabs = x_ref.shape[0]
    blocks, links = near_ref.shape

    @pl.when(step == 0)
    def _():
        x = x_ref[...].astype(jnp.float32)
        n_scr[...] = (x * inverse_rms(x) * gain_ref[...]).astype(jnp.bfloat16)
        acc_scr[...] = x
        lanes = lax.broadcasted_iota(jnp.int32, (blocks, blocks), 1)
        near = near_ref[...]
        listed = jnp.zeros((blocks, blocks), jnp.float32)
        for link in range(links):
            listed = jnp.where(lanes == near[:, link : link + 1], 1.0, listed)
        owner = lax.broadcasted_iota(jnp.int32, (stabs, blocks), 0) // BLOCK
        column = lax.broadcasted_iota(jnp.int32, (stabs, blocks), 1)
        widen = jnp.where(owner == column, 1.0, 0.0).astype(jnp.bfloat16)
        rows = dot(widen, listed.astype(jnp.bfloat16)).astype(jnp.bfloat16)
        bias_scr[...] = jnp.where(dot_nt(rows, widen) > 0.5, 0.0, MASKED_SCORE)

    n = n_scr[...]
    q_ref[...] = dot(n, wq_ref[...]).astype(jnp.bfloat16)
    k_ref[...] = dot(n, wk_ref[...]).astype(jnp.bfloat16)
    v_ref[...] = dot(n, wv_ref[...]).astype(jnp.bfloat16)
    for head in range(2):
        cols = slice(head * HEAD_DIM, (head + 1) * HEAD_DIM)
        keys = k_ref[:, cols]
        values = v_ref[:, cols]
        for start in range(0, stabs, CHUNK):
            rows = slice(start, start + CHUNK)
            scores = dot_nt(q_ref[rows, cols] * FACTOR, keys) + bias_scr[rows, :]
            weights = softmax_rows(scores)
            p_ref[head, rows, :] = weights
            o_ref[rows, cols] = dot(weights, values).astype(jnp.bfloat16)
    acc_scr[...] += dot(o_ref[...], wo_ref[...])

    @pl.when(step == pl.num_programs(0) - 1)
    def _():
        h_ref[...] = acc_scr[...].astype(jnp.bfloat16)


def space_backward_kernel(
    x_ref, gain_ref, g_ref, q_ref, k_ref, v_ref, o_ref, p_ref,
    wq_ref, wk_ref, wv_ref, wo_ref,
    out_ref,
    gn_scr, go_scr, gs_scr, dq_scr, dk_scr, dv_scr,
):
    step = pl.program_id(0)
    stabs = x_ref.shape[0]
    go = dot_nt(g_ref[...], wo_ref[...]).astype(jnp.bfloat16)
    go_scr[...] = go
    product = go.astype(jnp.float32) * o_ref[...].astype(jnp.float32)
    q_turned = q_ref[...].T
    go_turned = go.T
    for head in range(2):
        cols = slice(head * HEAD_DIM, (head + 1) * HEAD_DIM)
        keys = k_ref[:, cols]
        values = v_ref[:, cols]
        delta = jnp.sum(product[:, cols], axis=-1, keepdims=True)
        for start in range(0, stabs, BACK_CHUNK):
            rows = slice(start, start + BACK_CHUNK)
            grad_weights = dot_nt(go_scr[rows, cols], values)
            weights = p_ref[head, rows, :].astype(jnp.float32)
            grad_scores = (
                weights * ((grad_weights - delta[start : start + BACK_CHUNK]) * FACTOR)
            ).astype(jnp.bfloat16)
            gs_scr[rows, :] = grad_scores
            dq_scr[rows, cols] = dot(grad_scores, keys).astype(jnp.bfloat16)
        dk_scr[cols, :] = dot(q_turned[cols, :], gs_scr[...]).astype(jnp.bfloat16)
        dv_scr[cols, :] = dot(go_turned[cols, :], p_ref[head]).astype(jnp.bfloat16)
    part = (
        dot_nt(dq_scr[...], wq_ref[...])
        + dot_nt(dk_scr[...].T, wk_ref[...])
        + dot_nt(dv_scr[...].T, wv_ref[...])
    )

    @pl.when(step == 0)
    def _():
        gn_scr[...] = part

    @pl.when(step > 0)
    def _():
        gn_scr[...] += part

    @pl.when(step == pl.num_programs(0) - 1)
    def _():
        x = x_ref[...].astype(jnp.float32)
        back = norm_back(x, inverse_rms(x), gain_ref[...], gn_scr[...])
        out_ref[...] = (g_ref[...].astype(jnp.float32) + back).astype(jnp.bfloat16)


def time_kernel(
    width, h_ref, side_ref, gain_ref, readout_ref, win_ref, wout_ref,
    g_ref,
    qkv_scr, p_scr, o_scr, go_scr, d_scr,
):
    total, features = h_ref.shape
    tokens = p_scr.shape[-1]
    groups = total // tokens
    hidden = h_ref[...].astype(jnp.float32)
    inverse = inverse_rms(hidden)
    gain = gain_ref[...]
    normed = (hidden * inverse * gain).astype(jnp.bfloat16)
    qkv_scr[...] = dot(normed, win_ref[...]).astype(jnp.bfloat16)
    left = lax.broadcasted_iota(jnp.int32, (tokens, tokens), 0)
    right = lax.broadcasted_iota(jnp.int32, (tokens, tokens), 1)
    kept = ((left % width) == (right % width)) & (right <= left)
    bias = jnp.where(kept, 0.0, MASKED_SCORE)
    bias = jnp.concatenate([bias, bias], axis=0)

    pairs = features // PAIR
    lanes = lax.broadcasted_iota(jnp.int32, (tokens, PAIR), 1)
    near = lanes < HEAD_DIM

    def part(index, pair):
        start = index * features + pair * PAIR
        return slice(start, start + PAIR)

    def rows_of(group):
        return pl.ds(pl.multiple_of(group * tokens, tokens), tokens)

    def stacked(block):
        empty = jnp.zeros_like(block)
        return jnp.concatenate(
            [jnp.where(near, block, empty), jnp.where(near, empty, block)], axis=0
        )

    def merged(block):
        return jnp.where(near, block[:tokens], block[tokens:]).astype(jnp.bfloat16)

    def ahead(group, carry):
        rows = rows_of(group)
        scores = [
            dot_nt(stacked(qkv_scr[rows, part(0, pair)] * FACTOR), qkv_scr[rows, part(1, pair)])
            for pair in range(pairs)
        ]
        weights = [softmax_rows(score + bias) for score in scores]
        for pair in range(pairs):
            p_scr[group * pairs + pair] = weights[pair]
        outs = [dot(weights[pair], qkv_scr[rows, part(2, pair)]) for pair in range(pairs)]
        for pair in range(pairs):
            o_scr[rows, part(0, pair)] = merged(outs[pair])
        return carry

    lax.fori_loop(0, groups, ahead, 0)
    readout = readout_ref[...]
    after = hidden + dot(o_scr[...], wout_ref[...])
    logits = jnp.sum(after * readout, axis=-1, keepdims=True)
    side = side_ref[...]
    grad_logits = (jax.nn.sigmoid(logits) - side[:, 0:1]) * side[:, 1:2]
    grad_after = grad_logits * readout
    go_scr[...] = dot_nt(grad_after.astype(jnp.bfloat16), wout_ref[...]).astype(jnp.bfloat16)

    def behind(group, carry):
        rows = rows_of(group)
        span = range(pairs)
        upstream = [stacked(go_scr[rows, part(0, pair)]) for pair in span]
        products = [dot_nt(upstream[pair], qkv_scr[rows, part(2, pair)]) for pair in span]
        weights = [p_scr[group * pairs + pair] for pair in span]
        grad_scores = []
        for pair in span:
            attended = o_scr[rows, part(0, pair)].astype(jnp.float32)
            attended = jnp.concatenate([attended, attended], axis=0)
            delta = jnp.sum(
                upstream[pair].astype(jnp.float32) * attended, axis=-1, keepdims=True
            )
            grad_scores.append(
                (weights[pair].astype(jnp.float32) * ((products[pair] - delta) * FACTOR)).astype(
                    jnp.bfloat16
                )
            )
        queries = [dot(grad_scores[pair], qkv_scr[rows, part(1, pair)]) for pair in span]
        keys = [dot_tn(grad_scores[pair], stacked(qkv_scr[rows, part(0, pair)])) for pair in span]
        values = [dot_tn(weights[pair], upstream[pair]) for pair in span]
        for pair in span:
            d_scr[rows, part(0, pair)] = merged(queries[pair])
            d_scr[rows, part(1, pair)] = keys[pair].astype(jnp.bfloat16)
            d_scr[rows, part(2, pair)] = values[pair].astype(jnp.bfloat16)
        return carry

    lax.fori_loop(0, groups, behind, 0)
    grad_normed = dot_nt(d_scr[...], win_ref[...])
    hidden = h_ref[...].astype(jnp.float32)
    back = norm_back(hidden, inverse, gain, grad_normed)
    g_ref[...] = (grad_logits * readout + back).astype(jnp.bfloat16)


def whole(*shape):
    return pl.BlockSpec(shape, lambda step: (0,) * len(shape))


def weight_specs(features):
    pairs = features // PAIR
    return [
        pl.BlockSpec((features, PAIR), lambda step: (0, step)),
        pl.BlockSpec((features, PAIR), lambda step: (0, pairs + step)),
        pl.BlockSpec((features, PAIR), lambda step: (0, 2 * pairs + step)),
        pl.BlockSpec((PAIR, features), lambda step: (step, 0)),
    ]


def space_forward(x, neighbours, gain, w_in, w_out):
    stabs, features = x.shape
    pairs = features // PAIR
    column = pl.BlockSpec((stabs, PAIR), lambda step: (0, step))
    rows = jax.ShapeDtypeStruct((stabs, features), jnp.bfloat16)
    square = pl.BlockSpec((2, stabs, stabs), lambda step: (step, 0, 0))
    return pl.pallas_call(
        space_forward_kernel,
        grid=(pairs,),
        in_specs=[whole(stabs, features), whole(*neighbours.shape), whole(1, features)]
        + weight_specs(features),
        out_specs=[whole(stabs, features), column, column, column, column, square],
        out_shape=[
            rows, rows, rows, rows, rows,
            jax.ShapeDtypeStruct((2 * pairs, stabs, stabs), jnp.bfloat16),
        ],
        scratch_shapes=[
            pltpu.VMEM((stabs, features), jnp.bfloat16),
            pltpu.VMEM((stabs, stabs), jnp.float32),
            pltpu.VMEM((stabs, features), jnp.float32),
        ],
        compiler_params=pltpu.CompilerParams(vmem_limit_bytes=VMEM_LIMIT),
        name="space_forward",
    )(x, neighbours, gain, w_in, w_in, w_in, w_out)


def space_backward(x, gain, grad, saved, w_in, w_out):
    stabs, features = x.shape
    pairs = features // PAIR
    column = pl.BlockSpec((stabs, PAIR), lambda step: (0, step))
    square = pl.BlockSpec((2, stabs, stabs), lambda step: (step, 0, 0))
    return pl.pallas_call(
        space_backward_kernel,
        grid=(pairs,),
        in_specs=[whole(stabs, features), whole(1, features), whole(stabs, features)]
        + [column] * 4
        + [square]
        + weight_specs(features),
        out_specs=whole(stabs, features),
        out_shape=jax.ShapeDtypeStruct((stabs, features), jnp.bfloat16),
        scratch_shapes=[
            pltpu.VMEM((stabs, features), jnp.float32),
            pltpu.VMEM((stabs, PAIR), jnp.bfloat16),
            pltpu.VMEM((stabs, stabs), jnp.bfloat16),
            pltpu.VMEM((stabs, PAIR), jnp.bfloat16),
            pltpu.VMEM((PAIR, stabs), jnp.bfloat16),
            pltpu.VMEM((PAIR, stabs), jnp.bfloat16),
        ],
        compiler_params=pltpu.CompilerParams(vmem_limit_bytes=VMEM_LIMIT),
        name="space_backward",
    )(x, gain, grad, *saved, w_in, w_in, w_in, w_out)


def time_both(hidden, side, gain, readout, w_in, w_out, width, tokens):
    total, features = hidden.shape
    return pl.pallas_call(
        functools.partial(time_kernel, width),
        out_shape=jax.ShapeDtypeStruct((total, features), jnp.bfloat16),
        scratch_shapes=[
            pltpu.VMEM((total, 3 * features), jnp.bfloat16),
            pltpu.VMEM((total // tokens * (features // PAIR), 2 * tokens, tokens), jnp.bfloat16),
            pltpu.VMEM((total, features), jnp.bfloat16),
            pltpu.VMEM((total, features), jnp.bfloat16),
            pltpu.VMEM((total, 3 * features), jnp.bfloat16),
        ],
        compiler_params=pltpu.CompilerParams(vmem_limit_bytes=VMEM_LIMIT),
        name="time_both",
    )(hidden, side, gain, readout, w_in, w_out)


PIECE = 16
SPLIT = (2, 3, 2)
PARTS = (2, 2, 3)
MEGA_VMEM = 60 * 1024 * 1024


def spans(counts=SPLIT):
    first = 0
    found = []
    for count in counts:
        found.append((first, count))
        first += count
    return found


def half_turn(tiles):
    return pltpu.roll(tiles, 4, 1)


def pack_messages(rows):
    tiles = rows.shape[0] // 8
    cut = rows.reshape(tiles, 8, rows.shape[1])
    upper = lax.broadcasted_iota(jnp.int32, (tiles, 8, 128), 1) < 4
    parts = [cut[:, :, at : at + 128] for at in range(0, rows.shape[1], 128)]
    turned = [half_turn(part) for part in parts]
    low = [jnp.where(upper, parts[at], turned[at + 1]) for at in (0, 2)]
    high = [jnp.where(upper, turned[at], parts[at + 1]) for at in (0, 2)]
    low = jnp.concatenate(low, axis=1)[:, None]
    high = jnp.concatenate(high, axis=1)[:, None]
    return jnp.concatenate([low, high], axis=1).reshape(2 * tiles, 16, 128)


def unpack_messages(messages):
    tiles = messages.shape[0] // 2
    cut = messages.astype(jnp.float32).reshape(tiles, 2, 2, 8, 128)
    upper = lax.broadcasted_iota(jnp.int32, (tiles, 8, 128), 1) < 4
    found = []
    for part in range(2):
        low, high = cut[:, 0, part], cut[:, 1, part]
        found.append(jnp.where(upper, low, half_turn(high)))
        found.append(jnp.where(upper, half_turn(low), high))
    return jnp.concatenate(found, axis=2).reshape(8 * tiles, 512)


def layer_kernel(
    sizes,
    x_in, labels_in, near_ref, space_gain_ref, time_gain_ref, readout_ref,
    space_in_hbm, space_out_hbm, time_in_hbm, time_out_hbm,
    out_ref,
    x_scr, lab_scr, wsi, wso, wti, wto,
    bias_scr, qkv_scr, p_scr, o_scr, inv_scr,
    send_h, recv_h, send_g, recv_g, g_scr, go_scr, dq_scr, acc_scr, d_scr, out_scr,
    tqkv, tp, to, tgo, td,
    weight_sem, x_send, x_recv, lab_send, lab_recv,
    h_send, h_recv, g_send, g_recv, out_send, out_recv,
):
    depth, inner = sizes
    total = depth * inner
    here_z, here_s = lax.axis_index("round"), lax.axis_index("stab")
    here = here_z * inner + here_s
    here_chip = here_s // 2
    here_core = lax.rem(here_s, 2)
    mesh_ids = pl.DeviceIdType.MESH
    pieces_here, _, _, features = x_scr.shape
    rounds_here, stabs_here = labels_in.shape
    stabs = rounds_here * stabs_here
    rounds = depth * rounds_here
    pairs = features // PAIR

    def device(index):
        return (index // inner, lax.rem(index, inner))

    barrier = pltpu.get_barrier_semaphore()

    def greet(step, carry):
        pl.semaphore_signal(
            barrier, inc=1, device_id=device(lax.rem(here + step, total)), device_id_type=mesh_ids
        )
        return carry

    lax.fori_loop(1, total, greet, 0)
    weights = [
        pltpu.make_async_copy(source, target, weight_sem.at[index])
        for index, (source, target) in enumerate(
            [(space_in_hbm, wsi), (space_out_hbm, wso), (time_in_hbm, wti), (time_out_hbm, wto)]
        )
    ]
    for copy in weights:
        copy.start()
    pl.semaphore_wait(barrier, total - 1)

    chips = inner // 2

    def send_x(peer):
        pltpu.make_async_remote_copy(
            src_ref=x_in.at[peer], dst_ref=x_scr.at[:, here_s],
            send_sem=x_send, recv_sem=x_recv.at[here_s],
            device_id=(here_z, peer), device_id_type=mesh_ids,
        ).start()

    def send_x_chip(step, carry):
        chip = lax.rem(here_chip + step, chips)
        send_x(2 * chip)
        send_x(2 * chip + 1)
        return carry

    lax.fori_loop(1, chips, send_x_chip, 0)
    send_x(2 * here_chip + 1 - here_core)
    pltpu.make_async_copy(x_in.at[here_s], x_scr.at[:, here_s], x_recv.at[here_s]).start()

    def send_labels(step, carry):
        peer = lax.rem(here_z + step, depth)
        pltpu.make_async_remote_copy(
            src_ref=labels_in, dst_ref=lab_scr.at[here_z],
            send_sem=lab_send, recv_sem=lab_recv,
            device_id=(peer, here_s), device_id_type=mesh_ids,
        ).start()
        return carry

    lax.fori_loop(1, depth, send_labels, 0)
    pltpu.make_async_copy(labels_in, lab_scr.at[here_z], lab_recv).start()

    blocks = stabs // BLOCK
    piece_blocks = PIECE // BLOCK
    round_blocks = stabs_here // BLOCK
    key = lax.broadcasted_iota(jnp.int32, (stabs, blocks), 0)
    owner = (
        (key // PIECE) % inner * round_blocks
        + key // (PIECE * inner) * piece_blocks
        + key % PIECE // BLOCK
    )
    column = lax.broadcasted_iota(jnp.int32, (stabs, blocks), 1)
    widen = jnp.where(owner == column, 1.0, 0.0).astype(jnp.bfloat16)
    near = near_ref[...]
    key_block = lax.broadcasted_iota(jnp.int32, (blocks, blocks), 0)
    listed = jnp.zeros((blocks, blocks), jnp.float32)
    for link in range(near.shape[0]):
        listed = jnp.where(key_block == near[link : link + 1, :], 1.0, listed)
    listed = listed.astype(jnp.bfloat16)
    slot = lax.broadcasted_iota(jnp.int32, (128, blocks), 0)
    slot_column = lax.broadcasted_iota(jnp.int32, (128, blocks), 1)
    for index, (first, count) in enumerate(spans()):
        source = (
            (slot // piece_blocks) % inner * round_blocks
            + (first + slot // (piece_blocks * inner)) * piece_blocks
            + slot % piece_blocks
        )
        held = (source == slot_column) & (slot < count * piece_blocks * inner)
        mine = dot_nt(jnp.where(held, 1.0, 0.0).astype(jnp.bfloat16), listed).astype(jnp.bfloat16)
        spread = dot_nt(widen, mine)
        bias_scr[index] = jnp.where(spread > 0.5, 0.0, MASKED_SCORE).astype(jnp.bfloat16)

    near_lanes = lax.broadcasted_iota(jnp.int32, (1, PAIR), 1) < HEAD_DIM
    head_masks = [
        near_lanes.astype(jnp.float32).astype(jnp.bfloat16),
        1 - near_lanes.astype(jnp.float32).astype(jnp.bfloat16),
    ]

    weights[0].wait()

    def project(step, carry):
        chip = lax.rem(here_chip + chips - step, chips)
        for core in range(2):
            place = x_scr.at[:, 2 * chip + core]
            pltpu.make_async_copy(place, place, x_recv.at[2 * chip + core]).wait()
        both = pl.ds(2 * chip, 2)
        rows = pieces_here * 2 * PIECE
        x = x_scr[:, both].reshape(rows, features).astype(jnp.float32)
        normed = (x * inverse_rms(x) * space_gain_ref[...]).astype(jnp.bfloat16)
        made = dot(normed, wsi[...]).astype(jnp.bfloat16)
        qkv_scr[:, both] = made.reshape(pieces_here, 2, PIECE, 3 * features)
        return carry

    lax.fori_loop(0, chips, project, 0)
    weights[1].wait()

    def pair_cols(pair, third):
        start = third * features + pair * PAIR
        return pl.ds(start if isinstance(pair, int) else pl.multiple_of(start, PAIR), PAIR)

    def all_rows(pair, third):
        return qkv_scr[:, :, :, pair_cols(pair, third)].reshape(stabs, PAIR)

    def send_span(first, count, source, target, send_sem, recv_sem):
        rows = pl.ds(first * PIECE, count * PIECE)

        def send(step, carry):
            peer = lax.rem(here + step, total)
            pltpu.make_async_remote_copy(
                src_ref=source.at[peer, rows], dst_ref=target.at[here, rows],
                send_sem=send_sem, recv_sem=recv_sem,
                device_id=device(peer), device_id_type=mesh_ids,
            ).start()
            return carry

        lax.fori_loop(1, total, send, 0)
        pltpu.make_async_copy(source.at[here, rows], target.at[here, rows], recv_sem).start()

    def wait_span(first, count, target, recv_sem):
        whole_span = target.at[:, pl.ds(first * PIECE, count * PIECE)]
        pltpu.make_async_copy(whole_span, whole_span, recv_sem).wait()

    for index, (first, count) in enumerate(spans()):
        height = count * 128
        rows = slice(first, first + count)
        flat = slice(first * 128, (first + count) * 128)
        row_block = lax.broadcasted_iota(jnp.int32, (height, 128), 0) // BLOCK
        lane = lax.broadcasted_iota(jnp.int32, (height, 128), 1)
        onehot = jnp.where(row_block == lane, 1.0, 0.0).astype(jnp.bfloat16)

        def ahead(pair, carry, rows=rows, flat=flat, height=height, onehot=onehot, index=index):
            queries = qkv_scr[rows, :, :, pair_cols(pair, 0)].reshape(height, PAIR) * FACTOR
            keys = jnp.concatenate([all_rows(pair, 1), bias_scr[index]], axis=1)
            values = all_rows(pair, 2)
            out = None
            for half in range(2):
                mask = head_masks[half]
                scores = dot_nt(jnp.concatenate([queries * mask, onehot], axis=1), keys)
                highest = jnp.max(scores, axis=-1, keepdims=True)
                expd = jnp.exp(scores - highest).astype(jnp.bfloat16)
                p_scr[pair * 2 + half, flat, :] = expd
                ones = jnp.broadcast_to(mask, (stabs, PAIR))
                part = dot(expd, jnp.concatenate([values * mask, ones], axis=1))
                out = part if out is None else out + part
            inverse = 1.0 / out[:, PAIR:]
            inv_scr[flat, pair_cols(pair, 0)] = inverse
            o_scr[flat, pair_cols(pair, 0)] = (out[:, :PAIR] * inverse).astype(jnp.bfloat16)
            return carry

        if index == 0:
            for pair in range(pairs):
                ahead(pair, 0)
        else:
            def two_ahead(step, carry, ahead=ahead):
                ahead(2 * step, 0)
                ahead(2 * step + 1, 0)
                return carry

            lax.fori_loop(0, pairs // 2, two_ahead, 0)
        hidden = x_scr[rows].reshape(height, features).astype(jnp.float32)
        hidden = hidden + dot(o_scr[flat, :], wso[...])
        for piece in range(count):
            packed = pack_messages(hidden[piece * 128 : (piece + 1) * 128]).astype(jnp.bfloat16)
            packed = packed.reshape(inner, depth, 16, 128)
            at = slice((first + piece) * PIECE, (first + piece + 1) * PIECE)
            for z in range(depth):
                send_h[z * inner : (z + 1) * inner, at, :] = packed[:, z]
        send_span(first, count, send_h, recv_h, h_send, h_recv.at[index])

    tokens = BLOCK * rounds
    left = lax.broadcasted_iota(jnp.int32, (tokens, tokens), 0)
    right = lax.broadcasted_iota(jnp.int32, (tokens, tokens), 1)
    kept = ((left % BLOCK) == (right % BLOCK)) & (right <= left)
    causal = jnp.where(kept, 0.0, MASKED_SCORE)
    causal = jnp.concatenate([causal, causal], axis=0)
    lanes = lax.broadcasted_iota(jnp.int32, (tokens, PAIR), 1)
    is_near = lanes < HEAD_DIM

    def stacked(block):
        empty = jnp.zeros_like(block)
        return jnp.concatenate(
            [jnp.where(is_near, block, empty), jnp.where(is_near, empty, block)], axis=0
        )

    def merged(block):
        return jnp.where(is_near, block[:tokens], block[tokens:]).astype(jnp.bfloat16)

    pltpu.make_async_copy(lab_scr, lab_scr, lab_recv).wait()
    token_round = lax.broadcasted_iota(jnp.int32, (tokens, rounds), 0) // BLOCK
    which_round = lax.broadcasted_iota(jnp.int32, (tokens, rounds), 1)
    pick = jnp.where(token_round == which_round, 1.0, 0.0).astype(jnp.bfloat16)
    labels = lab_scr[...].reshape(rounds, stabs_here).astype(jnp.float32).astype(jnp.bfloat16)
    token_labels = dot(pick, labels)
    stab_lane = lax.broadcasted_iota(jnp.int32, (tokens, stabs_here), 1)
    token_slot = lax.broadcasted_iota(jnp.int32, (tokens, stabs_here), 0) % BLOCK
    slot_column = lax.broadcasted_iota(jnp.int32, (tokens, 1), 0) % BLOCK
    weights[2].wait()
    weights[3].wait()

    for index, (first, count) in enumerate(spans()):
        wait_span(first, count, recv_h, h_recv.at[index])
        height = count * tokens
        pieces = range(count)
        found = [
            unpack_messages(recv_h[:, (first + piece) * PIECE : (first + piece + 1) * PIECE, :])
            for piece in pieces
        ]
        hidden = jnp.concatenate(found, axis=0) if count > 1 else found[0]
        inverse = inverse_rms(hidden)
        gain = time_gain_ref[...]
        normed = (hidden * inverse * gain).astype(jnp.bfloat16)
        tqkv[:height, :] = dot(normed, wti[...]).astype(jnp.bfloat16)
        jobs = [(piece, pair) for piece in pieces for pair in range(pairs)]

        def part(third, pair):
            return slice(third * features + pair * PAIR, third * features + (pair + 1) * PAIR)

        def span_of(piece):
            return slice(piece * tokens, (piece + 1) * tokens)

        scores = [
            dot_nt(stacked(tqkv[span_of(i), part(0, p)] * FACTOR), tqkv[span_of(i), part(1, p)])
            for i, p in jobs
        ]
        probs = [softmax_rows(score + causal) for score in scores]
        for job, (i, p) in enumerate(jobs):
            tp[job] = probs[job]
        outs = [dot(probs[job], tqkv[span_of(i), part(2, p)]) for job, (i, p) in enumerate(jobs)]
        for job, (i, p) in enumerate(jobs):
            to[span_of(i), part(0, p)] = merged(outs[job])
        readout = readout_ref[...]
        after = hidden + dot(to[:height, :], wto[...])
        logits = jnp.sum(after * readout, axis=-1, keepdims=True)
        targets, real = [], []
        for piece in pieces:
            at = (first + piece) * PIECE + here_z * BLOCK
            chosen = jnp.where(stab_lane == at + token_slot, token_labels, 0.0)
            targets.append(jnp.sum(chosen, axis=-1, keepdims=True))
            where = here_s * stabs_here + at + slot_column
            real.append(jnp.where(where < STABS_REAL, 1.0, 0.0))
        targets = jnp.concatenate(targets, axis=0) if count > 1 else targets[0]
        real = jnp.concatenate(real, axis=0) if count > 1 else real[0]
        grad_logits = (jax.nn.sigmoid(logits) - targets) * real
        grad_after = grad_logits * readout
        tgo[:height, :] = dot_nt(grad_after.astype(jnp.bfloat16), wto[...]).astype(jnp.bfloat16)

        upstream = [stacked(tgo[span_of(i), part(0, p)]) for i, p in jobs]
        products = [
            dot_nt(upstream[job], tqkv[span_of(i), part(2, p)]) for job, (i, p) in enumerate(jobs)
        ]
        grads = []
        for job, (i, p) in enumerate(jobs):
            attended = to[span_of(i), part(0, p)].astype(jnp.float32)
            attended = jnp.concatenate([attended, attended], axis=0)
            delta = jnp.sum(
                upstream[job].astype(jnp.float32) * attended, axis=-1, keepdims=True
            )
            grads.append(
                (tp[job].astype(jnp.float32) * ((products[job] - delta) * FACTOR)).astype(
                    jnp.bfloat16
                )
            )
        for job, (i, p) in enumerate(jobs):
            td[span_of(i), part(0, p)] = merged(dot(grads[job], tqkv[span_of(i), part(1, p)]))
            keys = dot_tn(grads[job], stacked(tqkv[span_of(i), part(0, p)]))
            td[span_of(i), part(1, p)] = keys.astype(jnp.bfloat16)
            td[span_of(i), part(2, p)] = dot_tn(tp[job], upstream[job]).astype(jnp.bfloat16)
        grad_normed = dot_nt(td[:height, :], wti[...])
        grad_hidden = grad_after + norm_back(hidden, inverse, gain, grad_normed)
        for piece in pieces:
            packed = pack_messages(grad_hidden[span_of(piece)]).astype(jnp.bfloat16)
            send_g[:, (first + piece) * PIECE : (first + piece + 1) * PIECE, :] = packed
        send_span(first, count, send_g, recv_g, g_send, g_recv.at[index])

    def finish(first, count, recv_sem):
        rows = slice(first, first + count)
        flat = slice(first * 128, (first + count) * 128)
        for step in range(2 * pairs):
            block = acc_scr[step * PAIR : (step + 1) * PAIR, flat].astype(jnp.bfloat16)
            start = features + step * PAIR
            d_scr[rows, :, :, start : start + PAIR] = block.T.reshape(count, inner, PIECE, PAIR)
        grad_normed = dot_nt(d_scr[rows].reshape(count * 128, 3 * features), wsi[...])
        x = x_scr[rows].reshape(count * 128, features).astype(jnp.float32)
        back = norm_back(x, inverse_rms(x), space_gain_ref[...], grad_normed)
        grad = g_scr[rows].reshape(count * 128, features).astype(jnp.float32) + back
        out_scr[rows] = grad.astype(jnp.bfloat16).reshape(count, inner, PIECE, features)
        part = pl.ds(first, count)

        def send_out(step, carry):
            peer = lax.rem(here_s + step, inner)
            pltpu.make_async_remote_copy(
                src_ref=out_scr.at[part, peer], dst_ref=out_ref.at[here_s, part],
                send_sem=out_send, recv_sem=recv_sem,
                device_id=(here_z, peer), device_id_type=mesh_ids,
            ).start()
            return carry

        lax.fori_loop(1, inner, send_out, 0)
        pltpu.make_async_copy(out_scr.at[part, here_s], out_ref.at[here_s, part], recv_sem).start()

    for index, (first, count) in enumerate(spans()):
        wait_span(first, count, recv_g, g_recv.at[index])
        height = count * 128
        rows = slice(first, first + count)
        flat = slice(first * 128, (first + count) * 128)
        for piece in range(count):
            at = slice((first + piece) * PIECE, (first + piece + 1) * PIECE)
            cut = jnp.concatenate(
                [recv_g[z * inner : (z + 1) * inner, at, :][:, None] for z in range(depth)], axis=1
            )
            grad = unpack_messages(cut.reshape(total, 16, 128)).astype(jnp.bfloat16)
            g_scr[first + piece] = grad.reshape(inner, PIECE, features)
        grad = g_scr[rows].reshape(height, features)
        go_scr[:height, :] = dot_nt(grad, wso[...]).astype(jnp.bfloat16)
        lane = lax.broadcasted_iota(jnp.int32, (height, PAIR), 1)

        def prepare(pair):
            cols = pair_cols(pair, 0)
            queries = qkv_scr[rows, :, :, cols].reshape(height, PAIR) * FACTOR
            scaled = (go_scr[:height, cols].astype(jnp.float32) * inv_scr[flat, cols]).astype(
                jnp.bfloat16
            )
            product = scaled.astype(jnp.float32) * o_scr[flat, cols].astype(jnp.float32)
            joined = []
            for half in range(2):
                own = (lane < HEAD_DIM) if half == 0 else (lane >= HEAD_DIM)
                delta = jnp.sum(jnp.where(own, product, 0.0), axis=-1, keepdims=True)
                coarse = delta.astype(jnp.bfloat16).astype(jnp.float32)
                extra = jnp.where(lane == 0, -coarse, jnp.where(lane == 1, coarse - delta, 0.0))
                joined.append(
                    jnp.concatenate([scaled * head_masks[half], extra.astype(jnp.bfloat16)], axis=1)
                )
            return queries.T, scaled.T, joined

        def behind(pair, prepared, key_first, key_count):
            cols = pair_cols(pair, 0)
            key_rows = slice(key_first * 128, (key_first + key_count) * 128)
            keys, values = all_rows(pair, 1)[key_rows], all_rows(pair, 2)[key_rows]
            queries_turned, scaled_turned, joined = prepared
            ones = jnp.ones((key_count * 128, PAIR), jnp.bfloat16)
            values = jnp.concatenate([values, ones], axis=1)
            grad_queries = None
            for half in range(2):
                grad_weights = dot_nt(joined[half], values)
                expd = p_scr[pair * 2 + half, flat, key_rows]
                grad_scores = (expd.astype(jnp.float32) * grad_weights).astype(jnp.bfloat16)
                part = dot(grad_scores, keys * head_masks[half])
                grad_queries = part if grad_queries is None else grad_queries + part
                turned = slice(half * HEAD_DIM, (half + 1) * HEAD_DIM)
                for kind, turned_rows, square in (
                    (0, queries_turned, grad_scores), (1, scaled_turned, expd),
                ):
                    start = kind * features + pair * PAIR + half * HEAD_DIM
                    if not isinstance(pair, int):
                        start = pl.multiple_of(start, HEAD_DIM)
                    into = pl.ds(start, HEAD_DIM)
                    made = dot(turned_rows[turned, :], square)
                    if index == 0:
                        acc_scr[into, key_rows] = made
                    else:
                        acc_scr[into, key_rows] += made
            if key_first > 0:
                grad_queries = grad_queries + dq_scr[:height, cols]
            if key_first + key_count < pieces_here:
                dq_scr[:height, cols] = grad_queries
            else:
                made = (grad_queries * FACTOR).astype(jnp.bfloat16)
                d_scr[rows, :, :, cols] = made.reshape(count, inner, PIECE, PAIR)

        if index == 0:
            def two_behind(step, carry, prepare=prepare, behind=behind):
                behind(2 * step, prepare(2 * step), 0, pieces_here)
                behind(2 * step + 1, prepare(2 * step + 1), 0, pieces_here)
                return carry

            lax.fori_loop(0, pairs // 2, two_behind, 0)
        else:
            prepared = [prepare(pair) for pair in range(pairs)]
            last = index == len(SPLIT) - 1
            parts = spans(PARTS) if last else [(0, pieces_here)]
            for part_index, (key_first, key_count) in enumerate(parts):
                for pair in range(pairs):
                    behind(pair, prepared[pair], key_first, key_count)
                if last:
                    finish(key_first, key_count, out_recv.at[part_index])

    for index, (key_first, key_count) in enumerate(spans(PARTS)):
        landed = out_ref.at[:, pl.ds(key_first, key_count)]
        pltpu.make_async_copy(landed, landed, out_recv.at[index]).wait()

    def drain(buffer, sem):
        some = buffer.at[pl.ds(0, buffer.shape[0] - 1)]
        pltpu.make_async_copy(some, some, sem).wait()

    drain(lab_scr, lab_send)
    drain(send_h, h_send)
    drain(send_g, g_send)
    some = out_ref.at[pl.ds(0, inner - 1)]
    pltpu.make_async_copy(some, some, x_send).wait()
    pltpu.make_async_copy(some, some, out_send).wait()


def whole_layer(
    sizes, x, labels, near, space_gain, time_gain, readout, space_in, space_out, time_in, time_out
):
    depth, inner = sizes
    total = depth * inner
    rounds_here, stabs_here, features = x.shape
    sent = (rounds_here, stabs_here // PIECE, PIECE, features)
    tiles = (stabs_here // PIECE, inner, PIECE)
    stabs = rounds_here * stabs_here
    bf16, f32 = jnp.bfloat16, jnp.float32
    most = max(SPLIT)
    tokens = BLOCK * depth * rounds_here
    pieces = stabs_here // PIECE
    vmem = pl.BlockSpec(memory_space=pltpu.VMEM)
    anywhere = pl.BlockSpec(memory_space=pl.ANY)
    messages = pltpu.VMEM((total, pieces * PIECE, 128), bf16)
    dma = pltpu.SemaphoreType.DMA
    grad = pl.pallas_call(
        functools.partial(layer_kernel, sizes),
        out_shape=pltpu.VMEM(sent, bf16),
        in_specs=[anywhere, anywhere, vmem, vmem, vmem, vmem] + [anywhere] * 4,
        out_specs=vmem,
        scratch_shapes=[
            pltpu.VMEM(tiles + (features,), bf16),
            pltpu.VMEM((depth,) + labels.shape, jnp.int32),
            pltpu.VMEM(space_in.shape, bf16),
            pltpu.VMEM(space_out.shape, bf16),
            pltpu.VMEM(time_in.shape, bf16),
            pltpu.VMEM(time_out.shape, bf16),
            pltpu.VMEM((len(SPLIT), stabs, 128), bf16),
            pltpu.VMEM(tiles + (3 * features,), bf16),
            pltpu.VMEM((HEADS, stabs, stabs), bf16),
            pltpu.VMEM((stabs, features), bf16),
            pltpu.VMEM((stabs, features), f32),
            messages, messages, messages, messages,
            pltpu.VMEM(tiles + (features,), bf16),
            pltpu.VMEM((most * 128, features), bf16),
            pltpu.VMEM((SPLIT[-1] * 128, features), f32),
            pltpu.VMEM((2 * features, stabs), f32),
            pltpu.VMEM(tiles + (3 * features,), bf16),
            pltpu.VMEM(tiles + (features,), bf16),
            pltpu.VMEM((most * tokens, 3 * features), bf16),
            pltpu.VMEM((most * (features // PAIR), 2 * tokens, tokens), bf16),
            pltpu.VMEM((most * tokens, features), bf16),
            pltpu.VMEM((most * tokens, features), bf16),
            pltpu.VMEM((most * tokens, 3 * features), bf16),
            dma((4,)), dma, dma((inner,)), dma, dma,
            dma, dma((len(SPLIT),)), dma, dma((len(SPLIT),)), dma, dma((len(PARTS),)),
        ],
        compiler_params=pltpu.CompilerParams(
            collective_id=1, has_side_effects=True, vmem_limit_bytes=MEGA_VMEM
        ),
        name="whole_layer",
    )(x.reshape(sent), labels, near, space_gain, time_gain, readout, space_in, space_out, time_in, time_out)
    return grad.reshape(x.shape)


def body(
    round_size,
    stab_size,
    inputs,
    labels,
    neighbours,
    space_in_weights,
    space_out_weights,
    space_gain,
    time_in_weights,
    time_out_weights,
    time_gain,
    readout,
):
    rounds_here, stabs_here, features = inputs.shape
    rounds = rounds_here * round_size
    stabs = stabs_here * stab_size
    copies = stab_size // rounds_here
    assert copies * rounds_here == stab_size
    padded = -(-stabs_here // round_size) * round_size
    part = padded // round_size
    direct = copies == 1 and padded == stabs_here
    both = ("round", "stab")
    space_gain, time_gain, readout = space_gain[None], time_gain[None], readout[None]
    sizes = (round_size, stab_size)
    if (
        copies == 1
        and round_size * BLOCK == PIECE
        and stabs_here == sum(SPLIT) * PIECE
        and rounds * BLOCK == GROUP
        and stab_size * PIECE == GROUP
    ):
        grad = whole_layer(
            sizes, inputs, labels, neighbours.T, space_gain, time_gain, readout,
            space_in_weights, space_out_weights, time_in_weights, time_out_weights,
        )
        return grad.astype(jnp.float32)

    def to_rounds(tokens):
        if copies > 1:
            tokens = jnp.repeat(tokens, copies, axis=0)
        return lax.all_to_all(tokens, "stab", split_axis=0, concat_axis=1, tiled=True)[0]

    def to_tokens(rows):
        split = rows.reshape(stab_size, stabs_here, features)
        moved = lax.all_to_all(split, "stab", split_axis=0, concat_axis=0, tiled=True)
        return moved[::copies] if copies > 1 else moved

    def pad_stabs(tokens):
        return jnp.pad(tokens, ((0, 0), (0, padded - stabs_here), (0, 0)))

    def to_times(rows):
        if direct:
            return lax.all_to_all(
                rows.reshape(rounds, part, features), both, split_axis=0, concat_axis=0, tiled=True
            )
        tokens = pad_stabs(to_tokens(rows))
        return lax.all_to_all(tokens, "round", split_axis=1, concat_axis=0, tiled=True)

    def from_times(times):
        if direct:
            moved = lax.all_to_all(times, both, split_axis=0, concat_axis=0, tiled=True)
            return moved.reshape(stabs, features)
        tokens = lax.all_to_all(times, "round", split_axis=0, concat_axis=1, tiled=True)
        return to_rounds(tokens[:, :stabs_here])

    here_round, here_stab = lax.axis_index("round"), lax.axis_index("stab")
    if direct:
        first = (here_round * stab_size + here_stab) * part
        chunks = jnp.transpose(labels.reshape(rounds_here, round_size, part), (1, 0, 2))
        sent = jnp.tile(chunks.reshape(round_size, rounds_here * part), (stab_size, 1))
        came = lax.all_to_all(sent, both, split_axis=0, concat_axis=0, tiled=True)
        came = came.reshape(round_size, stab_size, rounds_here, part)
        owner = (here_round * stab_size + here_stab) // round_size
        targets = lax.dynamic_index_in_dim(came, owner, 1, keepdims=False)
        targets = targets.reshape(rounds, part).astype(jnp.float32)
    else:
        first = here_stab * stabs_here + here_round * part
        labels_all = lax.all_gather(labels, both, axis=0, tiled=False)
        labels_all = labels_all.reshape(round_size, stab_size, rounds_here, stabs_here)
        labels_all = jnp.transpose(labels_all, (0, 2, 1, 3)).reshape(rounds, stabs)
        labels_all = jnp.pad(labels_all, ((0, 0), (0, padded)))
        targets = lax.dynamic_slice(labels_all, (0, first), (rounds, part)).astype(jnp.float32)
    slot = jnp.arange(part) + (here_round * part if not direct else 0)
    real = first + jnp.arange(part) < STABS_REAL
    if not direct:
        real = real & (slot < stabs_here)
    side = jnp.stack([targets, jnp.broadcast_to(real.astype(jnp.float32), targets.shape)], axis=-1)

    width = max(1, GROUP // rounds)
    while part % width:
        width -= 1
    groups = part // width
    tokens = width * rounds

    def to_groups(times):
        depth = times.shape[-1]
        split = times.reshape(rounds, groups, width, depth)
        return jnp.transpose(split, (1, 0, 2, 3)).reshape(groups * tokens, depth)

    def from_groups(rows):
        split = rows.reshape(groups, rounds, width, features)
        return jnp.transpose(split, (1, 0, 2, 3)).reshape(rounds, part, features)

    x = to_rounds(inputs)
    after_space, *saved = space_forward(
        x, neighbours, space_gain, space_in_weights, space_out_weights
    )
    times = to_groups(to_times(after_space))
    grad_times = time_both(
        times, to_groups(side), time_gain, readout, time_in_weights, time_out_weights, width, tokens
    )
    grad_space = from_times(from_groups(grad_times))
    grad = space_backward(x, space_gain, grad_space, saved, space_in_weights, space_out_weights)
    return to_tokens(grad).astype(jnp.float32)


def solution(mesh):
    in_specs = (
        P("round", "stab", None),
        P("round", "stab"),
        P(),
        P(),
        P(),
        P(),
        P(),
        P(),
        P(),
        P(),
    )
    out_specs = P("round", "stab", None)
    sized = functools.partial(body, mesh.shape["round"], mesh.shape["stab"])
    return jax.shard_map(sized, mesh=mesh, in_specs=in_specs, out_specs=out_specs, check_vma=False)
```
